32 devices in a mesh: fsdp: 8 (over z, x), mp: 4 (over y, core).
Axes of the slice: x: 2, y: 2, z: 4, core: 2. Of those that a mesh axis runs over, the one named last changes fastest.
Arguments:
- hidden_in: bfloat16 [16, 832, 768], P('fsdp'), may hold values from -6 to 6
- segment_ids: int32 [16, 832], P('fsdp'), may hold values from 0 to 16, never falling along the last dimension, each value on 1 to 128 neighbouring positions
- pad_flags: int32 [16, 832], P('fsdp'), may hold values 0 or 1
- gain1: bfloat16 [768], P('fsdp'), may hold values from 0.5 to 1.5
- shift1: bfloat16 [768], P('fsdp'), may hold values from -3 to 3
- w_query: bfloat16 [768, 768], P('fsdp', 'mp'), may hold values from -0.21875 to 0.21875
- b_query: bfloat16 [768], P('mp'), may hold values from -3 to 3
- w_key: bfloat16 [768, 768], P('fsdp', 'mp'), may hold values from -0.21875 to 0.21875
- w_value: bfloat16 [768, 768], P('fsdp', 'mp'), may hold values from -0.21875 to 0.21875
- b_value: bfloat16 [768], P('mp'), may hold values from -3 to 3
- w_out: bfloat16 [768, 768], P('mp', 'fsdp'), may hold values from -1.25 to 1.25
- b_out: bfloat16 [768], P('fsdp'), may hold values from -3 to 3
- gain2: bfloat16 [768], P('fsdp'), may hold values from 0.5 to 1.5
- shift2: bfloat16 [768], P('fsdp'), may hold values from -3 to 3
- w_up: bfloat16 [768, 768], P('fsdp', 'mp'), may hold values from -0.21875 to 0.21875
- b_up: bfloat16 [768], P('mp'), may hold values from -3 to 3
- w_down: bfloat16 [768, 768], P('mp', 'fsdp'), may hold values from -0.3125 to 0.3125
- b_down: bfloat16 [768], P('fsdp'), may hold values from -3 to 3
- cotangent: bfloat16 [16, 832, 768], P('fsdp'), may hold values from -6 to 6
Outputs:
- out_hidden: bfloat16 [16, 832, 768], P('fsdp')
- grad_hidden: bfloat16 [16, 832, 768], P('fsdp')
- grad_gain1: float32 [768], P('fsdp')
- grad_shift1: float32 [768], P('fsdp')
- grad_w_query: float32 [768, 768], P('fsdp', 'mp')
- grad_b_query: float32 [768], P('mp')
- grad_w_key: float32 [768, 768], P('fsdp', 'mp')
- grad_w_value: float32 [768, 768], P('fsdp', 'mp')
- grad_b_value: float32 [768], P('mp')
- grad_w_out: float32 [768, 768], P('mp', 'fsdp')
- grad_b_out: float32 [768], P('fsdp')
- grad_gain2: float32 [768], P('fsdp')
- grad_shift2: float32 [768], P('fsdp')
- grad_w_up: float32 [768, 768], P('fsdp', 'mp')
- grad_b_up: float32 [768], P('mp')
- grad_w_down: float32 [768, 768], P('mp', 'fsdp')
- grad_b_down: float32 [768], P('fsdp')
The draws below stay inside these ranges and needn't reach their ends.
Inputs may be any that keep to these rules, and one draw needn't show every extreme that they name: `segment_ids`: within a row, segment numbers never fall, and each molecule of a row has 1 to 128 tokens.
All inputs are finite; a program needn't handle non-finite values. No bound on the sum of `pad_flags` on one device may be relied on, other than what follows from the above.
Results may differ from the reference program's by a relative error of at most 0.015.
Values may be sent and summed in bfloat16 or wider, within the bound.
No kernel may reach another device: no remote copies, remote signals or barrier semaphores. Data moves between devices by JAX's collectives and lax.ppermute only.
A program may use at most 192 MiB of HBM per device.

```python
import math
import jax
import jax.numpy as jnp
import numpy as np
from jax import lax

D = 768
H = 32
HD = 24
FF = 768
SEQ = 832
ROWS_DEV = 2
ROWS = 16
MOLS = 17
MOST = 128
N_FSDP = 8


def place_ends(array, stream_key, low, largest):
    extent = array.shape
    place = [jax.random.randint(jax.random.fold_in(stream_key, axis), (), 0, extent[axis]) for axis in range(len(extent))]
    array = array.at[tuple(place)].set(low)
    longest = extent.index(max(extent))
    place[longest] = (place[longest] + 1) % extent[longest]
    return array.at[tuple(place)].set(largest)


def block_levels(stream_key, shape, pieces, smallest, high):
    level = 1.0
    for dim, blocks in pieces:
        draws = jax.random.uniform(jax.random.fold_in(jax.random.fold_in(stream_key, 6), dim), (blocks,), jnp.float32, smallest / len(pieces), high / len(pieces))
        level = level * jnp.repeat(jnp.exp(draws), shape[dim] // blocks).reshape((-1,) + (1,) * (len(shape) - 1 - dim))
    return level


def profile(number_of, total, bound, lean):
    portions = [(1 << 20) // math.isqrt(standing ** lean) + 1 for standing in range(2, number_of + 1)]
    spare, counts = total - bound - (number_of - 1), [1] * (number_of - 1)
    while spare > 0:
        movable = [i for i in range(number_of - 1) if counts[i] < bound]
        pool, budget = sum([portions[i] for i in movable]), spare
        for i in movable:
            more = min(bound - counts[i], max(1, budget * portions[i] // pool), spare)
            counts[i] = counts[i] + more
            spare = spare - more
    return np.array([bound] + counts)


def ragged(stream_key, amount, total, most, slope):
    if amount == 2:
        one = jax.random.randint(stream_key, (), max(1, total - most), min(most, total - 1) + 1)
        return jnp.stack([one, total - one])
    lengths = jnp.asarray(profile(amount, total, most, slope), jnp.int32)
    twos = (amount - 1) // 2
    donor, taker = lengths[1:1 + 2 * twos:2], lengths[2:2 + 2 * twos:2]
    room = jnp.minimum(donor - 1, most - taker)
    passed = jax.random.randint(jax.random.fold_in(stream_key, 1), (twos,), 0, 1 << 20) % (room + 1)
    lengths = lengths.at[1:1 + 2 * twos:2].set(donor - passed).at[2:2 + 2 * twos:2].set(taker + passed)
    return lengths[jax.random.permutation(jax.random.fold_in(stream_key, 2), amount)]


def centred(key, shape, scale, limit, cuts=(), kind=jnp.bfloat16):
    entries = jax.random.normal(key, shape, jnp.float32) * scale
    if len(cuts) > 0:
        entries = block_levels(key, shape, cuts, -0.22, 0.18) * entries
    return jnp.clip(entries, min=-limit, max=limit).astype(kind)


def setup_inputs(seed: int = 0) -> dict:
    key_of = jax.random.split(jax.random.key(seed), 20)
    return {
        "hidden_in": centred(key_of[0], (ROWS, SEQ, D), 1.0, 6.0, ((0, 8),)),
        "segment_ids": jax.vmap(lambda own: jnp.searchsorted(jnp.cumsum(ragged(own, MOLS, SEQ, MOST, 1)), jnp.arange(SEQ), side="right"))(jax.random.split(key_of[1], ROWS)).reshape((ROWS, SEQ)).astype(jnp.int32),
        "pad_flags": place_ends((jax.random.randint(key_of[2], (ROWS, SEQ), 0, 8) < 1).astype(jnp.int32), jax.random.fold_in(key_of[2], 1), 0, 1),
        "gain1": jnp.clip(1.0 + 0.1 * jax.random.normal(key_of[3], (D,), jnp.float32), 0.5, 1.5).astype(jnp.bfloat16),
        "shift1": centred(key_of[4], (D,), 0.3, 3.0, ((0, 8),)),
        "w_query": centred(key_of[5], (D, D), D ** -0.5, 0.21875, ((0, 8), (1, 4))),
        "b_query": centred(key_of[6], (D,), 0.3, 3.0, ((0, 4),)),
        "w_key": centred(key_of[7], (D, D), D ** -0.5, 0.21875, ((0, 8), (1, 4))),
        "w_value": centred(key_of[8], (D, D), D ** -0.5, 0.21875, ((0, 8), (1, 4))),
        "b_value": centred(key_of[9], (D,), 0.3, 3.0, ((0, 4),)),
        "w_out": centred(key_of[10], (D, D), (D // 32) ** -0.5, 1.25, ((0, 4), (1, 8))),
        "b_out": centred(key_of[11], (D,), 0.3, 3.0, ((0, 8),)),
        "gain2": jnp.clip(1.0 + 0.1 * jax.random.normal(key_of[12], (D,), jnp.float32), 0.5, 1.5).astype(jnp.bfloat16),
        "shift2": centred(key_of[13], (D,), 0.3, 3.0, ((0, 8),)),
        "w_up": centred(key_of[14], (D, FF), D ** -0.5, 0.21875, ((0, 8), (1, 4))),
        "b_up": centred(key_of[15], (FF,), 0.3, 3.0, ((0, 4),)),
        "w_down": centred(key_of[16], (FF, D), (FF // 2) ** -0.5, 0.3125, ((0, 4), (1, 8))),
        "b_down": centred(key_of[17], (D,), 0.3, 3.0, ((0, 8),)),
        "cotangent": centred(key_of[18], (ROWS, SEQ, D), 1.0, 6.0, ((0, 8),)),
    }


@jax.custom_vjp
def low(v):
    return lax.optimization_barrier(v.astype(jnp.bfloat16)).astype(jnp.float32)

@jax.custom_vjp
def low_back(v):
    return v

def low_keep(v):
    return (low(v), None)

def low_pass(kept, grad):
    return (grad,)

def back_keep(v):
    return (v, None)

def back_low(kept, grad):
    return (low(grad),)
low.defvjp(low_keep, low_pass)
low_back.defvjp(back_keep, back_low)
epsilon = 1e-05
highest = lax.Precision.HIGHEST

def layer_norm(values, gain, shift):
    centre = lax.optimization_barrier(jnp.mean(values, axis=-1, keepdims=True))
    centered = values - centre
    spread = lax.optimization_barrier(jnp.mean(centered * centered, axis=-1, keepdims=True))
    return centered * lax.rsqrt(spread + epsilon) * gain + shift

def project(values, weight):
    return jnp.einsum('rsd,de->rse', values, weight, precision=highest)

def attend_row(inputs):
    query_row, key_row, value_row, segment_row, pad_row = inputs
    scores = jnp.einsum('qhd,khd->hqk', query_row, key_row, precision=highest) / math.sqrt(HD)
    scores = low_back(scores)
    places = jnp.arange(SEQ, dtype=jnp.int32)
    allowed = (segment_row[:, None] == segment_row[None, :]) & ((pad_row[None, :] == 0) | (places[:, None] == places[None, :]))
    scores = jnp.where(allowed[None], scores, -1e+30)
    top_score = lax.optimization_barrier(jnp.max(scores, axis=-1, keepdims=True))
    weights = jnp.exp(scores - top_score)
    probs = low(weights / lax.optimization_barrier(jnp.sum(weights, axis=-1, keepdims=True)))
    return jnp.einsum('hqk,khd->qhd', probs, value_row, precision=highest)

def layer(hidden_rows, params, segments, pads):
    gain1, shift1, w_query, b_query, w_key, w_value, b_value, w_out, b_out, gain2, shift2, w_up, b_up, w_down, b_down = params
    normed1 = low(layer_norm(hidden_rows, gain1, shift1))
    query_all = low(low_back(project(normed1, w_query) + b_query))
    key_all = low(low_back(project(normed1, w_key)))
    value_all = low(low_back(project(normed1, w_value) + b_value))
    split = (ROWS_DEV, SEQ, H, HD)
    mixed = lax.map(jax.checkpoint(attend_row), (query_all.reshape(split), key_all.reshape(split), value_all.reshape(split), segments, pads))
    mixed = low(low_back(mixed.reshape(ROWS_DEV, SEQ, D)))
    middle_rows = hidden_rows + low_back(project(mixed, w_out)) + b_out
    normed2 = low(layer_norm(middle_rows, gain2, shift2))
    pre_act = low_back(project(normed2, w_up) + b_up)
    activated = low(jax.nn.gelu(pre_act))
    return middle_rows + low_back(project(activated, w_down)) + b_down

def reference(hidden_in, segment_ids, pad_flags, gain1, shift1, w_query, b_query, w_key, w_value, b_value, w_out, b_out, gain2, shift2, w_up, b_up, w_down, b_down, cotangent):
    params = tuple((item.astype(jnp.float32) for item in (gain1, shift1, w_query, b_query, w_key, w_value, b_value, w_out, b_out, gain2, shift2, w_up, b_up, w_down, b_down)))
    groups_x = hidden_in.astype(jnp.float32).reshape(N_FSDP, ROWS_DEV, SEQ, D)
    groups_c = cotangent.astype(jnp.float32).reshape(N_FSDP, ROWS_DEV, SEQ, D)
    groups_s = segment_ids.reshape(N_FSDP, ROWS_DEV, SEQ)
    groups_p = pad_flags.reshape(N_FSDP, ROWS_DEV, SEQ)

    def one_group(totals, piece):
        group_x, group_s, group_p, group_c = piece
        result, pull = jax.vjp(lambda values, weights: layer(values, weights, group_s, group_p), group_x, params)
        grad_x, grad_params = pull(group_c)
        totals = jax.tree.map(lambda left, right: left + right, totals, grad_params)
        return (totals, (result.astype(jnp.bfloat16), grad_x.astype(jnp.bfloat16)))
    zeros = tuple((jnp.zeros_like(item) for item in params))
    totals, (results, grads) = lax.scan(one_group, zeros, (groups_x, groups_s, groups_p, groups_c))
    out_hidden = results.reshape(ROWS, SEQ, D)
    grad_hidden = grads.reshape(ROWS, SEQ, D)
    return (out_hidden, grad_hidden, totals[0], totals[1], totals[2], totals[3], totals[4], totals[5], totals[6], totals[7], totals[8], totals[9], totals[10], totals[11], totals[12], totals[13], totals[14])
```

```python
import math

import jax
import jax.numpy as jnp
from jax import lax
from jax.sharding import PartitionSpec as P

HD = 24
MOST = 128
BOTH = ("fsdp", "mp")
EPS = 1e-05
F32 = jnp.float32
BF16 = jnp.bfloat16


def send(value, fs, mp, flip_f, flip_m):
    pairs = [(f * mp + m, (f ^ flip_f) * mp + (m ^ flip_m)) for f in range(fs) for m in range(mp)]
    return lax.ppermute(value, BOTH, pairs)


def high_groups(fs):
    groups, bit = [], 2
    while bit < fs:
        wide = 4 if bit * 2 < fs else 2
        groups.append([bit * step for step in range(1, wide)])
        bit *= wide
    return groups


def dot_nn(left, right):
    return lax.dot_general(left, right, (((1,), (0,)), ((), ())), preferred_element_type=F32)


def dot_nt(left, right):
    return lax.dot_general(left, right, (((1,), (1,)), ((), ())), preferred_element_type=F32)


def dot_tn(left, right):
    return lax.dot_general(left, right, (((0,), (0,)), ((), ())), preferred_element_type=F32)


def norm_parts(values):
    centre = jnp.mean(values, axis=-1, keepdims=True)
    centered = values - centre
    inverse = lax.rsqrt(jnp.mean(centered * centered, axis=-1, keepdims=True) + EPS)
    return centered * inverse, inverse


def norm_back(grad, normed, inverse, gain):
    scaled = grad * gain
    return inverse * (
        scaled
        - jnp.mean(scaled, axis=-1, keepdims=True)
        - normed * jnp.mean(scaled * normed, axis=-1, keepdims=True)
    )


def per_device(
    hidden_in,
    segment_ids,
    pad_flags,
    gain1,
    shift1,
    w_query,
    b_query,
    w_key,
    w_value,
    b_value,
    w_out,
    b_out,
    gain2,
    shift2,
    w_up,
    b_up,
    w_down,
    b_down,
    cotangent,
):
    fs, mp = lax.axis_size("fsdp"), lax.axis_size("mp")
    rows, length, width = hidden_in.shape
    wr, wc = w_query.shape
    half = wr // 2
    f, m = lax.axis_index("fsdp"), lax.axis_index("mp")
    core, y = m % 2, m // 2
    window = length // 2 + MOST // 2
    gap = length - window
    start = core * gap
    is0 = core == 0

    def gather_weights(blocks):
        stack = jnp.stack(blocks)
        count = len(blocks)
        mine = jnp.where(is0, stack[:, :half], stack[:, half:])
        theirs = jnp.where(is0, stack[:, half:], stack[:, :half])
        got = send(theirs, fs, mp, 0, 1)
        piece = jnp.where(
            is0, jnp.concatenate([mine, got], axis=2), jnp.concatenate([got, mine], axis=2)
        )
        piece = piece[None]
        for flips in high_groups(fs):
            parts = [piece] + [send(piece, fs, mp, flip, 0) for flip in flips]
            piece = jnp.concatenate(parts, axis=0)
        quads = [[piece, send(piece, fs, mp, 0, 2)], [send(piece, fs, mp, 1, 0), send(piece, fs, mp, 1, 2)]]
        full = []
        for yr in range(2):
            xs = []
            for xr in range(2):
                own = quads[xr][yr]
                other = send(own, fs, mp, 0, 1)
                xs.append(jnp.stack([own, other], axis=2))
            both = jnp.stack(xs, axis=1)
            full.append([both[:, :, w].reshape(width, 2 * wc) for w in range(count)])
        return [[full[0][w], full[1][w]] for w in range(count)]

    wq, wk, wv = gather_weights([w_query, w_key, w_value])
    wo, wu, wd = gather_weights([w_out.T, w_up, w_down.T])

    small = jnp.stack([gain1, shift1, b_out, gain2, shift2, b_down])
    small = jnp.where(is0, small, jnp.concatenate([small[:, half:], small[:, :half]], axis=1))
    small = small[:, None]
    for flips in high_groups(fs):
        small = jnp.concatenate([small] + [send(small, fs, mp, flip, 0) for flip in flips], axis=1)
    small = jnp.stack([small, send(small, fs, mp, 1, 0)], axis=2).reshape(6, width).astype(F32)
    g1, h1, bo, g2, h2, bd = [small[i] for i in range(6)]
    cols = jnp.stack([b_query, b_value, b_up])
    pair = send(cols, fs, mp, 0, 1)
    cols = jnp.where(is0, jnp.concatenate([cols, pair], axis=1), jnp.concatenate([pair, cols], axis=1))
    cols = [cols.astype(F32), send(cols, fs, mp, 0, 2).astype(F32)]

    def split_of(segments):
        middle = segments[length // 2]
        first = jnp.sum((segments < middle).astype(jnp.int32))
        last = jnp.sum((segments <= middle).astype(jnp.int32))
        return jnp.where(length // 2 - first <= last - length // 2, first, last)

    splits = jnp.stack([split_of(segment_ids[r]) for r in range(rows)])
    split = splits[y]
    place = start + lax.iota(jnp.int32, window)
    owned = jnp.where(is0, place < split, place >= split)
    segs = lax.dynamic_slice(segment_ids, (y, start), (1, window))[0]
    pads = lax.dynamic_slice(pad_flags, (y, start), (1, window))[0]
    swap = f * 2 + core
    here = lax.broadcasted_iota(jnp.int32, (width, width), 0)
    there = lax.broadcasted_iota(jnp.int32, (width, width), 1)
    perm = ((here // half == (there // half) ^ swap) & (here % half == there % half)).astype(BF16)
    x = dot_nn(lax.dynamic_slice(hidden_in, (y, start, 0), (1, window, width))[0], perm)
    ct = lax.dynamic_slice(cotangent, (y, start, 0), (1, window, width))[0]
    ct = dot_nn(jnp.where(owned[:, None], ct, jnp.zeros_like(ct)), perm)
    ct_low = ct.astype(BF16)

    xhat1, inv1 = norm_parts(x)
    normed1 = (xhat1 * g1 + h1).astype(BF16)
    heads = 2 * wc // HD
    scale = 1.0 / math.sqrt(HD)
    same = segs[:, None] == segs[None, :]
    ids = lax.iota(jnp.int32, window)
    allowed = same & ((pads[None, :] == 0) | (ids[:, None] == ids[None, :]))

    def four(value):
        return value.reshape(window, heads, HD)

    saved, attended = [], []
    for yr in range(2):
        q = (dot_nn(normed1, wq[yr]) + cols[yr][0]).astype(BF16)
        k = dot_nn(normed1, wk[yr]).astype(BF16)
        v = (dot_nn(normed1, wv[yr]) + cols[yr][1]).astype(BF16)
        scores = jnp.einsum("qhd,khd->hqk", four(q), four(k), preferred_element_type=F32) * scale
        scores = jnp.where(allowed[None], scores, -1e30)
        top = jnp.max(scores, axis=-1, keepdims=True)
        lse = top + jnp.log(jnp.sum(jnp.exp(scores - top), axis=-1, keepdims=True))
        probs = jnp.exp(scores - lse).astype(BF16)
        mixed = jnp.einsum("hqk,khd->qhd", probs, four(v), preferred_element_type=F32)
        attended.append(mixed.astype(BF16).reshape(window, 2 * wc))
        saved.append((q, k, v, lse))
    middle = x + dot_nt(attended[0], wo[0]) + dot_nt(attended[1], wo[1]) + bo
    xhat2, inv2 = norm_parts(middle)
    normed2 = (xhat2 * g2 + h2).astype(BF16)
    acts, pulls = [], []
    for yr in range(2):
        pre = dot_nn(normed2, wu[yr]) + cols[yr][2]
        act, pull = jax.vjp(jax.nn.gelu, pre)
        acts.append(act.astype(BF16))
        pulls.append(pull)
    result = middle + dot_nt(acts[0], wd[0]) + dot_nt(acts[1], wd[1]) + bd

    def share(value):
        value = dot_nn(value, perm).astype(BF16)
        beside = send(value, fs, mp, 0, 1)
        across = send(value, fs, mp, 0, 2)
        corner = send(across, fs, mp, 0, 1)
        own_split, other_split = split, splits[1 - y]

        def row(mine, theirs, cut):
            low, high = jnp.where(is0, mine, theirs), jnp.where(is0, theirs, mine)
            at = gap + lax.iota(jnp.int32, window - gap)
            seam = jnp.where((at < cut)[:, None], low[gap:], high[: window - gap])
            return jnp.concatenate([low[:gap], seam, high[window - gap :]], axis=0)

        a, b = row(value, beside, own_split), row(across, corner, other_split)
        return jnp.where(y == 0, jnp.stack([a, b]), jnp.stack([b, a]))

    out_hidden = share(result.astype(BF16))

    sum_b_down = jnp.sum(ct, axis=0)
    dpre, gwd, gwu = [], [], []
    for yr in range(2):
        gwd.append(dot_tn(ct_low, acts[yr]))
        d = pulls[yr](dot_nn(ct_low, wd[yr]))[0].astype(BF16)
        dpre.append(d)
        gwu.append(dot_tn(normed2, d))
    sum_b_up = jnp.concatenate([jnp.sum(d.astype(F32), axis=0) for d in dpre])
    dnorm2 = dot_nt(dpre[0], wu[0]) + dot_nt(dpre[1], wu[1])
    sum_g2 = jnp.sum(dnorm2 * xhat2, axis=0)
    sum_h2 = jnp.sum(dnorm2, axis=0)
    dmiddle = ct + norm_back(dnorm2, xhat2, inv2, g2)
    sum_b_out = jnp.sum(dmiddle, axis=0)
    dmiddle_low = dmiddle.astype(BF16)
    gwo = [dot_tn(dmiddle_low, attended[yr]) for yr in range(2)]
    gwq, gwk, gwv, dnorm1, sum_q, sum_v = [], [], [], 0.0, [], []
    for yr in range(2):
        q, k, v, lse = saved[yr]
        da = dot_nn(dmiddle_low, wo[yr]).astype(BF16)
        scores = jnp.einsum("qhd,khd->hqk", four(q), four(k), preferred_element_type=F32) * scale
        scores = jnp.where(allowed[None], scores, -1e30)
        probs = jnp.exp(scores - lse)
        dv = jnp.einsum("hqk,qhd->khd", probs.astype(BF16), four(da), preferred_element_type=F32)
        dprobs = jnp.einsum("qhd,khd->hqk", four(da), four(v), preferred_element_type=F32)
        centre = jnp.sum(probs * dprobs, axis=-1, keepdims=True)
        ds = (probs * (dprobs - centre)).astype(BF16)
        dq = jnp.einsum("hqk,khd->qhd", ds, four(k), preferred_element_type=F32) * scale
        dk = jnp.einsum("hqk,qhd->khd", ds, four(q), preferred_element_type=F32) * scale
        dq, dk, dv = [t.astype(BF16).reshape(window, 2 * wc) for t in (dq, dk, dv)]
        gwq.append(dot_tn(normed1, dq))
        gwk.append(dot_tn(normed1, dk))
        gwv.append(dot_tn(normed1, dv))
        dnorm1 = dnorm1 + dot_nt(dq, wq[yr]) + dot_nt(dk, wk[yr]) + dot_nt(dv, wv[yr])
        sum_q.append(jnp.sum(dq.astype(F32), axis=0))
        sum_v.append(jnp.sum(dv.astype(F32), axis=0))
    sum_g1 = jnp.sum(dnorm1 * xhat1, axis=0)
    sum_h1 = jnp.sum(dnorm1, axis=0)
    dx = dmiddle + norm_back(dnorm1, xhat1, inv1, g1)
    grad_hidden = share(dx.astype(BF16))

    def scatter_weights(grads):
        count = len(grads)
        whole = jnp.stack([jnp.stack(g) for g in grads])
        whole = whole.reshape(count, 2, fs // 2, 2, 2, half, 2 * wc)
        mine = whole[:, :, :, :, 0] + send(whole[:, :, :, :, 1].astype(BF16), fs, mp, 0, 1).astype(F32)
        low = mine.astype(BF16)
        total = mine[:, 0, :, 0]
        for xr, yr in ((1, 0), (0, 1), (1, 1)):
            total = total + send(low[:, yr, :, xr], fs, mp, xr, 2 * yr).astype(F32)
        for flips in reversed(high_groups(fs)):
            n = len(flips) + 1
            total = total.reshape(count, n, total.shape[1] // n, half, 2 * wc)
            low = total.astype(BF16)
            kept = total[:, 0]
            for i, flip in enumerate(flips):
                kept = kept + send(low[:, i + 1], fs, mp, flip, 0).astype(F32)
            total = kept
        total = total.reshape(count, half, 2 * wc)
        left, right = total[:, :, :wc], total[:, :, wc:]
        mine, theirs = jnp.where(is0, left, right), jnp.where(is0, right, left)
        got = send(theirs, fs, mp, 0, 1)
        final = jnp.where(is0, jnp.concatenate([mine, got], axis=1), jnp.concatenate([got, mine], axis=1))
        return [final[w] for w in range(count)]

    grad_out, grad_up, grad_down = scatter_weights([gwo, gwu, gwd])
    grad_q, grad_k, grad_v = scatter_weights([gwq, gwk, gwv])

    feats = jnp.stack([sum_g1, sum_h1, sum_b_out, sum_g2, sum_h2, sum_b_down])
    high = feats.astype(BF16)
    rest = feats - high.astype(F32)
    mid = rest.astype(BF16)
    last = (rest - mid.astype(F32)).astype(BF16)
    feats = dot_nn(high, perm) + dot_nn(mid, perm) + dot_nn(last, perm)
    units = jnp.stack([jnp.concatenate(sum_q), jnp.concatenate(sum_v), sum_b_up])
    units = jnp.where(y == 0, units, jnp.roll(units, 2 * wc, axis=1))
    sums = jnp.concatenate([feats, units], axis=0)
    sums = sums + send(sums, fs, mp, 0, 1)
    sums = sums + send(sums, fs, mp, 0, 2) + send(sums, fs, mp, 1, 0) + send(sums, fs, mp, 1, 2)
    for flips in high_groups(fs):
        new = sums
        for flip in flips:
            new = new + send(sums, fs, mp, flip, 0)
        sums = new
    mine_f = lax.dynamic_slice(sums, (0, f * wr), (6, wr))
    mine_u = lax.dynamic_slice(sums, (6, m * wc), (3, wc))
    return (
        out_hidden,
        grad_hidden,
        mine_f[0],
        mine_f[1],
        grad_q,
        mine_u[0],
        grad_k,
        grad_v,
        mine_u[1],
        grad_out.T,
        mine_f[2],
        mine_f[3],
        mine_f[4],
        grad_up,
        mine_u[2],
        grad_down.T,
        mine_f[5],
    )


def solution(mesh):
    return jax.shard_map(
        per_device,
        mesh=mesh,
        in_specs=(
            P("fsdp", None, None),
            P("fsdp", None),
            P("fsdp", None),
            P("fsdp"),
            P("fsdp"),
            P("fsdp", "mp"),
            P("mp"),
            P("fsdp", "mp"),
            P("fsdp", "mp"),
            P("mp"),
            P("mp", "fsdp"),
            P("fsdp"),
            P("fsdp"),
            P("fsdp"),
            P("fsdp", "mp"),
            P("mp"),
            P("mp", "fsdp"),
            P("fsdp"),
            P("fsdp", None, None),
        ),
        out_specs=(
            P("fsdp", None, None),
            P("fsdp", None, None),
            P("fsdp"),
            P("fsdp"),
            P("fsdp", "mp"),
            P("mp"),
            P("fsdp", "mp"),
            P("fsdp", "mp"),
            P("mp"),
            P("mp", "fsdp"),
            P("fsdp"),
            P("fsdp"),
            P("fsdp"),
            P("fsdp", "mp"),
            P("mp"),
            P("mp", "fsdp"),
            P("fsdp"),
        ),
        check_vma=False,
    )
```

```python
import functools
import math

import jax
import jax.numpy as jnp
from jax import lax
from jax.experimental import pallas as pl
from jax.experimental.pallas import tpu as pltpu
from jax.sharding import PartitionSpec as P

HD = 24
PAD = 32
MOST = 128
BOTH = ("fsdp", "mp")
EPS = 1e-05
F32 = jnp.float32
BF16 = jnp.bfloat16
LOG2 = math.log2(math.e) / math.sqrt(HD)
SCALE = 1.0 / math.sqrt(HD)
GELU = math.sqrt(2.0 / math.pi)


def send(value, fs, mp, flip_f, flip_m):
    pairs = [(f * mp + m, (f ^ flip_f) * mp + (m ^ flip_m)) for f in range(fs) for m in range(mp)]
    return lax.ppermute(value, BOTH, pairs)


def high_groups(fs):
    groups, bit = [], 2
    while bit < fs:
        wide = 4 if bit * 2 < fs else 2
        groups.append([bit * step for step in range(1, wide)])
        bit *= wide
    return groups


def dot_nn(left, right):
    return lax.dot_general(left, right, (((1,), (0,)), ((), ())), preferred_element_type=F32)


def dot_nt(left, right):
    return lax.dot_general(left, right, (((1,), (1,)), ((), ())), preferred_element_type=F32)


def dot_tn(left, right):
    return lax.dot_general(left, right, (((0,), (0,)), ((), ())), preferred_element_type=F32)


def norm_parts(values):
    centre = jnp.mean(values, axis=-1, keepdims=True)
    centered = values - centre
    inverse = lax.rsqrt(jnp.mean(centered * centered, axis=-1, keepdims=True) + EPS)
    return centered * inverse, inverse


def norm_back(grad, normed, inverse, gain):
    scaled = grad * gain
    return inverse * (
        scaled
        - jnp.mean(scaled, axis=-1, keepdims=True)
        - normed * jnp.mean(scaled * normed, axis=-1, keepdims=True)
    )


def call(body, outs, operands, scratch=(), scalars=0):
    whole = pl.BlockSpec(memory_space=pltpu.VMEM)
    few = pl.BlockSpec(memory_space=pltpu.SMEM)
    return pl.pallas_call(
        body,
        out_shape=tuple(jax.ShapeDtypeStruct(s, d) for s, d in outs),
        in_specs=[few] * scalars + [whole] * (len(operands) - scalars),
        out_specs=tuple(whole for _ in outs),
        scratch_shapes=list(scratch),
        compiler_params=pltpu.CompilerParams(vmem_limit_bytes=56 << 20),
    )(*operands)


def tiles(window):
    made = []
    for q0 in range(0, window, 256):
        qn = min(256, window - q0)
        k0 = max(0, q0 - MOST)
        made.append((q0, qn, k0, min(window, q0 + qn + MOST)))
    return made


def permutation(target):
    width = target.shape[1]
    return (lax.broadcasted_iota(jnp.int32, (width, width), 0) == target).astype(BF16)


def start_body(xw, cw, target, small, code, segs, x_o, c_o, n_o, nt_o, bias_o):
    perm = permutation(target[...])
    x = dot_nn(xw[...], perm)
    x_o[...] = x.astype(BF16)
    c_o[...] = dot_nn(cw[...], perm).astype(BF16)
    xhat, _ = norm_parts(x)
    normed = xhat * small[0:1] + small[1:2]
    n_o[...] = normed.astype(BF16)
    nt_o[...] = normed.T.astype(BF16)
    window = xw.shape[0]
    column = jnp.broadcast_to(code[...], (8, window)).T[:, 0:1]
    key = lax.broadcasted_iota(jnp.int32, (window, window), 0)
    query = lax.broadcasted_iota(jnp.int32, (window, window), 1)
    bias_o[...] = jnp.where((column == segs[...]) | (key == query), 0.0, -1e30)


def assemble(blocks, rows, weights):
    for block, places in zip(blocks, rows):
        count, kinds, high, _ = block.shape
        for z in range(count):
            for w in range(kinds):
                weights[w, places[z] : places[z] + high] = block[z, w]


def disassemble(value, w, outs, rows):
    for out, places in zip(outs, rows):
        count, _, high, _ = out.shape
        for z in range(count):
            out[z, w] = value[places[z] : places[z] + high].astype(out.dtype)


def by_head(value, fill=0.0):
    tokens, columns = value.shape
    parts = value.T.reshape(columns // HD, HD, tokens)
    row = lax.broadcasted_iota(jnp.int32, (columns // HD, PAD - HD, tokens), 1)
    extra = jnp.where(row == 0, fill, 0.0)
    return jnp.concatenate([parts, extra], axis=1).astype(BF16)


def flat_heads(value):
    heads, _, tokens = value.shape
    return value[:, :HD, :].reshape(heads * HD, tokens)


def forward_body(rows, n, *refs):
    blocks = refs[: len(rows)]
    cols, bias, qt, kt, vt, ot, att, lse, weights = refs[len(rows) :]
    assemble(blocks, rows, weights)
    normed = n[...]
    qt[...] = by_head(dot_nn(normed, weights[0]) + cols[0:1])
    kt[...] = by_head(dot_nn(normed, weights[1]))
    vt[...] = by_head(dot_nn(normed, weights[2]) + cols[1:2], 1.0)
    heads, _, window = qt.shape

    def head(h, carry):
        for q0, qn, k0, k1 in tiles(window):
            scores = dot_tn(kt[h, :, k0:k1], qt[h, :, q0 : q0 + qn])
            scores = scores * LOG2 + bias[k0:k1, q0 : q0 + qn]
            top = jnp.max(scores, axis=0, keepdims=True)
            weight = jnp.exp2(scores - top).astype(BF16)
            mixed = dot_nn(vt[h, :, k0:k1], weight)
            total = mixed[HD : HD + 1]
            ot[h, :, q0 : q0 + qn] = mixed / total
            lse[h, :, q0 : q0 + qn] = top + jnp.log2(total)
        return carry

    lax.fori_loop(0, heads, head, 0, unroll=2)
    att[...] = flat_heads(ot[...]).T.astype(BF16)


def feed_body(rows, half_blocks, x_r, c_r, a0, a1, small, cols, target, *refs):
    blocks = refs[: 2 * half_blocks]
    refs = refs[2 * half_blocks :]
    out_o, mid_o, d0, d1, sum_o, up_o = refs[:6]
    grads = refs[6 : 6 + 2 * half_blocks]
    w0, w1 = refs[6 + 2 * half_blocks :]
    weights = (w0, w1)
    for yr in range(2):
        assemble(blocks[yr * half_blocks : (yr + 1) * half_blocks], rows, weights[yr])
    att = (a0, a1)
    x = x_r[...].astype(F32)
    middle = x + dot_nt(a0[...], w0[0]) + dot_nt(a1[...], w1[0]) + small[2:3]
    xhat, inverse = norm_parts(middle)
    gain = small[3:4]
    normed = (xhat * gain + small[4:5]).astype(BF16)
    ct_low = c_r[...]
    result = middle + small[5:6]
    dnorm = jnp.zeros_like(middle)
    for yr in range(2):
        pre = dot_nn(normed, weights[yr][1]) + cols[3 * yr + 2 : 3 * yr + 3]
        square = pre * pre
        bent = jnp.tanh(GELU * (pre + 0.044715 * (pre * square)))
        act = (0.5 * pre * (1.0 + bent)).astype(BF16)
        slope = 0.5 * (1.0 + bent) + 0.5 * pre * (1.0 - bent * bent) * (GELU * (1.0 + 3.0 * 0.044715 * square))
        result = result + dot_nt(act, weights[yr][2])
        outs = grads[yr * half_blocks : (yr + 1) * half_blocks]
        disassemble(dot_tn(ct_low, act), 2, outs, rows)
        dpre = (dot_nn(ct_low, weights[yr][2]) * slope).astype(BF16)
        disassemble(dot_tn(normed, dpre), 1, outs, rows)
        up_o[yr] = jnp.sum(dpre.astype(F32), axis=0, keepdims=True)
        dnorm = dnorm + dot_nt(dpre, weights[yr][1])
    out_o[...] = dot_nn(result.astype(BF16), permutation(target[...])).astype(BF16)
    ct = ct_low.astype(F32)
    dmiddle = ct + norm_back(dnorm, xhat, inverse, gain)
    mid_o[...] = dmiddle
    sum_o[0:1] = jnp.sum(dmiddle, axis=0, keepdims=True)
    sum_o[1:2] = jnp.sum(dnorm * xhat, axis=0, keepdims=True)
    sum_o[2:3] = jnp.sum(dnorm, axis=0, keepdims=True)
    sum_o[3:4] = jnp.sum(ct, axis=0, keepdims=True)
    low = dmiddle.astype(BF16)
    for yr in range(2):
        outs = grads[yr * half_blocks : (yr + 1) * half_blocks]
        disassemble(dot_tn(low, att[yr][...]), 0, outs, rows)
        (d0, d1)[yr][...] = by_head(dot_nn(low, weights[yr][0]).astype(BF16).astype(F32))


def backward_body(rows, nt_r, *refs):
    blocks = refs[: len(rows)]
    qt, kt, vt, dt, ot, lse, bias = refs[len(rows) : len(rows) + 7]
    refs = refs[len(rows) + 7 :]
    dn, sums = refs[:2]
    grads = refs[2 : 2 + len(rows)]
    weights, dq, dk, dv = refs[2 + len(rows) :]
    assemble(blocks, rows, weights)
    heads, _, window = qt.shape
    made = tiles(window)

    def head(h, carry):
        delta = jnp.sum(dt[h].astype(F32) * ot[h], axis=0, keepdims=True)
        for ref in (dk, dv):
            ref[h] = jnp.zeros_like(ref[h])
        for q0, qn, k0, k1 in made:
            query, grad = qt[h, :, q0 : q0 + qn], dt[h, :, q0 : q0 + qn]
            scores = dot_tn(kt[h, :, k0:k1], query)
            dprobs = dot_tn(vt[h, :, k0:k1], grad)
            probs = jnp.exp2(scores * LOG2 + (bias[k0:k1, q0 : q0 + qn] - lse[h, :, q0 : q0 + qn]))
            dscores = (probs * (dprobs - delta[:, q0 : q0 + qn])).astype(BF16)
            dq[h, :, q0 : q0 + qn] = dot_nn(kt[h, :, k0:k1], dscores)
            dk[h, :, k0:k1] += dot_nt(query, dscores)
            dv[h, :, k0:k1] += dot_nt(grad, probs.astype(BF16))
        return carry

    lax.fori_loop(0, heads, head, 0, unroll=2)
    normed = nt_r[...]
    total = None
    ones = jnp.ones((8, window), BF16)
    for w, (ref, factor) in enumerate(((dq, SCALE), (dk, SCALE), (dv, 1.0))):
        low = (flat_heads(ref[...]) * factor).astype(BF16)
        disassemble(dot_nt(normed, low), w, grads, rows)
        part = dot_nn(weights[w], low)
        total = part if total is None else total + part
        if w != 1:
            sums[w // 2 : w // 2 + 1] = dot_nt(ones, low)[0:1]
    dn[...] = total


def finish_body(dn0, dn1, x_r, mid, small, target, sums, out_o, sum_o):
    perm = permutation(target[...])
    grad = (dn0[...] + dn1[...]).T
    xhat, inverse = norm_parts(x_r[...].astype(F32))
    dx = mid[...] + norm_back(grad, xhat, inverse, small[0:1])
    out_o[...] = dot_nn(dx.astype(BF16), perm).astype(BF16)
    feats = jnp.concatenate(
        [
            jnp.sum(grad * xhat, axis=0, keepdims=True),
            jnp.sum(grad, axis=0, keepdims=True),
            sums[0:4],
            jnp.zeros_like(sums[0:2]),
        ],
        axis=0,
    )
    high = feats.astype(BF16)
    rest = feats - high.astype(F32)
    mid_part = rest.astype(BF16)
    last = (rest - mid_part.astype(F32)).astype(BF16)
    sum_o[...] = dot_nn(high, perm) + dot_nn(mid_part, perm) + dot_nn(last, perm)


def join_body(info, own, beside, across, corner, out):
    core, y = info[0], info[1]
    length, window = out.shape[1], own.shape[0]
    gap = length - window

    def row(low, high, place, cut):
        out[place, 0:gap] = low[0:gap]
        at = gap + lax.broadcasted_iota(jnp.int32, (window - gap, 1), 0)
        seam = jnp.where(at < cut, low[gap:window].astype(F32), high[0 : window - gap].astype(F32))
        out[place, gap:window] = seam.astype(BF16)
        out[place, window:length] = high[window - gap : window]

    @pl.when(core == 0)
    def _():
        row(own, beside, y, info[2])
        row(across, corner, 1 - y, info[3])

    @pl.when(core != 0)
    def _():
        row(beside, own, y, info[2])
        row(corner, across, 1 - y, info[3])


def per_device(
    hidden_in,
    segment_ids,
    pad_flags,
    gain1,
    shift1,
    w_query,
    b_query,
    w_key,
    w_value,
    b_value,
    w_out,
    b_out,
    gain2,
    shift2,
    w_up,
    b_up,
    w_down,
    b_down,
    cotangent,
):
    fs, mp = lax.axis_size("fsdp"), lax.axis_size("mp")
    rows, length, width = hidden_in.shape
    wr, wc = w_query.shape
    half, cols = wr // 2, 2 * wc
    heads = cols // HD
    f, m = lax.axis_index("fsdp"), lax.axis_index("mp")
    core, y = m % 2, m // 2
    window = length // 2 + MOST // 2
    gap = length - window
    start = core * gap
    is0 = core == 0
    deep = fs // 2
    direct = half % 16 == 0
    if direct:
        places = [[((z * 2 + x) * 2 + c) * half for z in range(deep)] for x in range(2) for c in range(2)]
        block = (deep, 3, half, cols)
    else:
        places = [[0]]
        block = (1, 3, width, cols)
    n_blocks = len(places)

    def pair_up(blocks):
        stack = jnp.stack(blocks)
        mine = jnp.where(is0, stack[:, :half], stack[:, half:])
        theirs = jnp.where(is0, stack[:, half:], stack[:, :half])
        got = send(theirs, fs, mp, 0, 1)
        piece = jnp.where(
            is0, jnp.concatenate([mine, got], axis=2), jnp.concatenate([got, mine], axis=2)
        )
        return piece[None]

    def gather_high(piece):
        for flips in high_groups(fs):
            piece = jnp.concatenate([piece] + [send(piece, fs, mp, flip, 0) for flip in flips], axis=0)
        return piece

    def gather_low(piece):
        near = [piece, send(piece, fs, mp, 1, 0)]
        far = [send(piece, fs, mp, 0, 2), send(piece, fs, mp, 1, 2)]
        made = []
        for group in (near, far):
            blocks = []
            for own in group:
                blocks += [own, send(own, fs, mp, 0, 1)]
            if not direct:
                whole = jnp.stack(blocks).reshape(2, 2, deep, 3, half, cols).transpose(3, 2, 0, 1, 4, 5)
                blocks = [whole.reshape(1, 3, width, cols)]
            made.append(blocks)
        return made

    first = pair_up([w_query, w_key, w_value])
    first, hidden_in, cotangent, segment_ids, w_out, w_up, w_down, gain1 = lax.optimization_barrier(
        (first, hidden_in, cotangent, segment_ids, w_out, w_up, w_down, gain1)
    )
    first = gather_high(first)
    second = gather_high(pair_up([w_out.T, w_up, w_down.T]))
    wa = gather_low(first)
    wb = gather_low(second)

    small = jnp.stack([gain1, shift1, b_out, gain2, shift2, b_down])
    small = jnp.where(is0, small, jnp.concatenate([small[:, half:], small[:, :half]], axis=1))
    small = small[:, None]
    for flips in high_groups(fs):
        small = jnp.concatenate([small] + [send(small, fs, mp, flip, 0) for flip in flips], axis=1)
    small = jnp.stack([small, send(small, fs, mp, 1, 0)], axis=2).reshape(6, width).astype(F32)
    small = jnp.concatenate([small, jnp.zeros((2, width), F32)], axis=0)
    units = jnp.stack([b_query, b_value, b_up])
    pair = send(units, fs, mp, 0, 1)
    units = jnp.where(is0, jnp.concatenate([units, pair], axis=1), jnp.concatenate([pair, units], axis=1))
    units = [units.astype(F32), send(units, fs, mp, 0, 2).astype(F32)]

    def split_of(segments):
        middle = segments[length // 2]
        first = jnp.sum((segments < middle).astype(jnp.int32))
        last = jnp.sum((segments <= middle).astype(jnp.int32))
        return jnp.where(length // 2 - first <= last - length // 2, first, last)

    splits = jnp.stack([split_of(segment_ids[r]) for r in range(rows)])
    split, other_split = splits[y], splits[1 - y]
    info = jnp.stack([core, y, split, other_split]).astype(jnp.int32)
    place = start + lax.iota(jnp.int32, window)
    owned = jnp.where(is0, place < split, place >= split)
    segs = lax.dynamic_slice(segment_ids, (y, start), (1, window))
    pads = lax.dynamic_slice(pad_flags, (y, start), (1, window))
    code = jnp.where(pads == 0, segs, -1).astype(F32)
    segs = segs.astype(F32)
    swap = f * 2 + core
    feature = lax.iota(jnp.int32, width)
    target = (((feature // half) ^ swap) * half + feature % half)[None]
    xw = lax.dynamic_slice(hidden_in, (y, start, 0), (1, window, width))[0]
    cw = lax.dynamic_slice(cotangent, (y, start, 0), (1, window, width))[0]
    cw = jnp.where(owned[:, None], cw, jnp.zeros_like(cw))

    wide, tall = (window, width), (width, window)
    x, ct, normed, normed_t, bias = call(
        start_body,
        [(wide, BF16), (wide, BF16), (wide, BF16), (tall, BF16), ((window, window), F32)],
        [xw, cw, target, small, code, segs],
    )
    by_heads = (heads, PAD, window)
    weights = pltpu.VMEM((3, width, cols), BF16)
    saved, attended = [], []
    for yr in range(2):
        q, k, v, o, a, lse = call(
            functools.partial(forward_body, places),
            [(by_heads, BF16)] * 3
            + [(by_heads, F32), ((window, cols), BF16), ((heads, 1, window), F32)],
            [normed] + wa[yr] + [units[yr], bias],
            [weights],
        )
        saved.append((q, k, v, o, lse))
        attended.append(a)

    made = call(
        functools.partial(feed_body, places, n_blocks),
        [(wide, BF16), (wide, F32), (by_heads, BF16), (by_heads, BF16), ((4, width), F32), ((2, 1, cols), F32)]
        + [(block, BF16)] * (2 * n_blocks),
        [x, ct] + attended + [small, jnp.concatenate(units, axis=0), target] + wb[0] + wb[1],
        [weights, weights],
    )
    result, dmiddle, da0, da1, sum_mid, sum_up = made[:6]

    def share(value):
        beside = send(value, fs, mp, 0, 1)
        across = send(value, fs, mp, 0, 2)
        corner = send(across, fs, mp, 0, 1)
        return call(join_body, [((rows, length, width), BF16)], [info, value, beside, across, corner], (), 1)[0]

    def core_stage(blocks):
        if not direct:
            whole = blocks[0].reshape(3, deep, 2, 2, half, cols).transpose(2, 3, 1, 0, 4, 5)
            blocks = [whole[x, c] for x in range(2) for c in range(2)]
        return [
            blocks[2 * x].astype(F32) + send(blocks[2 * x + 1], fs, mp, 0, 1).astype(F32) for x in range(2)
        ]

    def far_stage(sums):
        return sum(send(sums[x].astype(BF16), fs, mp, x, 2).astype(F32) for x in range(2))

    def near_stage(sums):
        return sums[0] + send(sums[1].astype(BF16), fs, mp, 1, 0).astype(F32)

    def high_stage(total):
        for flips in reversed(high_groups(fs)):
            n = len(flips) + 1
            size = total.shape[0] // n
            low = total.astype(BF16)
            kept = total[:size]
            for i, flip in enumerate(flips):
                kept = kept + send(low[(i + 1) * size : (i + 2) * size], fs, mp, flip, 0).astype(F32)
            total = kept
        total = total[0]
        left, right = total[:, :, :wc], total[:, :, wc:]
        mine, theirs = jnp.where(is0, left, right), jnp.where(is0, right, left)
        got = send(theirs, fs, mp, 0, 1)
        final = jnp.where(is0, jnp.concatenate([mine, got], axis=1), jnp.concatenate([got, mine], axis=1))
        return [final[w] for w in range(3)]

    grads = made[6:]
    sums_b = [core_stage(grads[:n_blocks]), core_stage(grads[n_blocks:])]
    grad_out, grad_up, grad_down = high_stage(far_stage(sums_b[1]) + near_stage(sums_b[0]))
    out_hidden = share(result)

    partial, sum_qv, sums_a = [None, None], [None, None], [None, None]
    for yr in (1, 0):
        q, k, v, o, lse = saved[yr]
        got = call(
            functools.partial(backward_body, places),
            [(tall, F32), ((2, cols), F32)] + [(block, BF16)] * n_blocks,
            [normed_t] + wa[yr] + [q, k, v, (da0, da1)[yr], o, lse, bias],
            [weights] + [pltpu.VMEM(by_heads, F32)] * 3,
        )
        partial[yr], sum_qv[yr] = got[:2]
        sums_a[yr] = core_stage(got[2:])
        if yr == 1:
            far = far_stage(sums_a[1])
    grad_q, grad_k, grad_v = high_stage(far + near_stage(sums_a[0]))
    grad_window, feats = call(
        finish_body,
        [(wide, BF16), ((8, width), F32)],
        [partial[0], partial[1], x, dmiddle, small, target, sum_mid],
    )
    grad_hidden = share(grad_window)

    sum_e = [jnp.concatenate([sum_qv[yr], sum_up[yr]], axis=0) for yr in range(2)]
    sum_e = jnp.where(
        y == 0, jnp.concatenate(sum_e, axis=1), jnp.concatenate([sum_e[1], sum_e[0]], axis=1)
    )
    sums = jnp.concatenate([feats, sum_e], axis=0)
    sums = sums + send(sums, fs, mp, 0, 1)
    sums = sums + send(sums, fs, mp, 0, 2) + send(sums, fs, mp, 1, 0) + send(sums, fs, mp, 1, 2)
    for flips in high_groups(fs):
        new = sums
        for flip in flips:
            new = new + send(sums, fs, mp, flip, 0)
        sums = new
    mine_f = lax.dynamic_slice(sums, (0, f * wr), (6, wr))
    mine_u = lax.dynamic_slice(sums, (8, m * wc), (3, wc))
    return (
        out_hidden,
        grad_hidden,
        mine_f[0],
        mine_f[1],
        grad_q,
        mine_u[0],
        grad_k,
        grad_v,
        mine_u[1],
        grad_out.T,
        mine_f[2],
        mine_f[3],
        mine_f[4],
        grad_up,
        mine_u[2],
        grad_down.T,
        mine_f[5],
    )


def solution(mesh):
    return jax.shard_map(
        per_device,
        mesh=mesh,
        in_specs=(
            P("fsdp", None, None),
            P("fsdp", None),
            P("fsdp", None),
            P("fsdp"),
            P("fsdp"),
            P("fsdp", "mp"),
            P("mp"),
            P("fsdp", "mp"),
            P("fsdp", "mp"),
            P("mp"),
            P("mp", "fsdp"),
            P("fsdp"),
            P("fsdp"),
            P("fsdp"),
            P("fsdp", "mp"),
            P("mp"),
            P("mp", "fsdp"),
            P("fsdp"),
            P("fsdp", None, None),
        ),
        out_specs=(
            P("fsdp", None, None),
            P("fsdp", None, None),
            P("fsdp"),
            P("fsdp"),
            P("fsdp", "mp"),
            P("mp"),
            P("fsdp", "mp"),
            P("fsdp", "mp"),
            P("mp"),
            P("mp", "fsdp"),
            P("fsdp"),
            P("fsdp"),
            P("fsdp"),
            P("fsdp", "mp"),
            P("mp"),
            P("mp", "fsdp"),
            P("fsdp"),
        ),
        check_vma=False,
    )
```

```python
import functools
import math

import jax
import jax.numpy as jnp
from jax import lax
from jax.experimental import pallas as pl
from jax.experimental.pallas import tpu as pltpu
from jax.sharding import PartitionSpec as P

HD = 24
PAD = 32
MOST = 128
BOTH = ("fsdp", "mp")
EPS = 1e-05
F32 = jnp.float32
BF16 = jnp.bfloat16
LOG2 = math.log2(math.e) / math.sqrt(HD)
SCALE = 1.0 / math.sqrt(HD)
GELU = math.sqrt(2.0 / math.pi)


def send(value, fs, mp, flip_f, flip_m):
    pairs = [(f * mp + m, (f ^ flip_f) * mp + (m ^ flip_m)) for f in range(fs) for m in range(mp)]
    return lax.ppermute(value, BOTH, pairs)


def dot_nn(left, right):
    return lax.dot_general(left, right, (((1,), (0,)), ((), ())), preferred_element_type=F32)


def dot_nt(left, right):
    return lax.dot_general(left, right, (((1,), (1,)), ((), ())), preferred_element_type=F32)


def dot_tn(left, right):
    return lax.dot_general(left, right, (((0,), (0,)), ((), ())), preferred_element_type=F32)


def norm_parts(values):
    centre = jnp.mean(values, axis=-1, keepdims=True)
    centered = values - centre
    inverse = lax.rsqrt(jnp.mean(centered * centered, axis=-1, keepdims=True) + EPS)
    return centered * inverse, inverse


def norm_back(grad, normed, inverse, gain):
    scaled = grad * gain
    return inverse * (
        scaled
        - jnp.mean(scaled, axis=-1, keepdims=True)
        - normed * jnp.mean(scaled * normed, axis=-1, keepdims=True)
    )


def call(body, outs, operands, scratch=(), scalars=0, us=1.0, mib=8):
    whole = pl.BlockSpec(memory_space=pltpu.VMEM)
    few = pl.BlockSpec(memory_space=pltpu.SMEM)
    return pl.pallas_call(
        body,
        out_shape=tuple(jax.ShapeDtypeStruct(s, d) for s, d in outs),
        in_specs=[few] * scalars + [whole] * (len(operands) - scalars),
        out_specs=tuple(whole for _ in outs),
        scratch_shapes=list(scratch),
        compiler_params=pltpu.CompilerParams(vmem_limit_bytes=mib << 20),
        cost_estimate=pl.CostEstimate(
            flops=int(us * 2e9), transcendentals=0, bytes_accessed=int(us * 3e6)
        ),
    )(*operands)


def fence(*values):
    return lax.optimization_barrier(values)


def tiles(window):
    made = []
    for q0 in range(0, window, 256):
        qn = min(256, window - q0)
        k0 = max(0, q0 - MOST)
        made.append((q0, qn, k0, min(window, q0 + qn + MOST)))
    return made


def permutation(target):
    width = target.shape[1]
    return (lax.broadcasted_iota(jnp.int32, (width, width), 0) == target).astype(BF16)


def cuts_of(segments):
    middle = segments.shape[1] // 2
    held = segments[:, middle : middle + 1]
    first = jnp.sum((segments < held).astype(F32), axis=1, keepdims=True)
    last = jnp.sum((segments <= held).astype(F32), axis=1, keepdims=True)
    return jnp.where(middle - first <= last - middle, first, last)


def start_body(info, hidden, cotangent, segment_ids, pad_flags, target, x_o, c_o, xhat_o, bias_o):
    core, y = info[0], info[1]
    window = x_o.shape[0]
    gap = hidden.shape[1] - window
    start = pl.multiple_of(core * gap, 16)
    segments = segment_ids[...]
    cuts = cuts_of(segments)
    cut = jnp.where(y == 0, cuts[0:1], cuts[1:2])
    here = (start + lax.broadcasted_iota(jnp.int32, (window, 1), 0)).astype(F32)
    before = (here < cut).astype(F32)
    owned = jnp.where(core == 0, before, 1.0 - before)
    perm = permutation(target[...])
    x = dot_nn(hidden[y, pl.ds(start, window), :], perm)
    x_o[...] = x.astype(BF16)
    c_o[...] = (dot_nn(cotangent[y, pl.ds(start, window), :], perm) * owned).astype(BF16)
    xhat_o[...] = norm_parts(x)[0]
    segs = jnp.where(y == 0, segments[0:1], segments[1:2]).astype(F32)
    pads = pad_flags[...]
    pads = jnp.where(y == 0, pads[0:1], pads[1:2])
    code = jnp.where(pads == 0, segs, -1.0)
    segs = jnp.where(core == 0, segs[:, :window], segs[:, gap:])
    code = jnp.where(core == 0, code[:, :window], code[:, gap:])
    column = jnp.broadcast_to(code, (8, window)).T[:, 0:1]
    key = lax.broadcasted_iota(jnp.int32, (window, window), 0)
    query = lax.broadcasted_iota(jnp.int32, (window, window), 1)
    bias_o[...] = jnp.where((column == segs) | (key == query), 0.0, -1e30)


def assemble(blocks, places, high, weights):
    for block, rows in zip(blocks, places):
        for z, row in enumerate(rows):
            for w in range(3):
                weights[w, row : row + high] = block[z, w * high : (w + 1) * high]


def disassemble(value, outs, pick):
    value = value.astype(BF16)
    if len(outs) == 1:
        outs[0][pick] = value
        return
    _, deep, high, _ = outs[0].shape[-4:]
    half = high // 3
    yr, w = pick[:-1], pick[-1]
    for x in range(2):
        for z in range(deep):
            for c in range(2):
                at = ((z * 2 + x) * 2 + c) * half
                outs[c][yr + (x, z, pl.ds(w * half, half))] = value[at : at + half]


def common_order(rows, perm):
    high = rows.astype(BF16)
    rest = rows - high.astype(F32)
    mid = rest.astype(BF16)
    last = (rest - mid.astype(F32)).astype(BF16)
    return dot_nn(high, perm) + dot_nn(mid, perm) + dot_nn(last, perm)


def by_head(value, fill=0.0):
    tokens, columns = value.shape
    parts = value.T.reshape(columns // HD, HD, tokens)
    row = lax.broadcasted_iota(jnp.int32, (columns // HD, PAD - HD, tokens), 1)
    extra = jnp.where(row == 0, fill, 0.0)
    return jnp.concatenate([parts, extra], axis=1).astype(BF16)


def flat_heads(value):
    heads, _, tokens = value.shape
    return value[:, :HD, :].reshape(heads * HD, tokens)


def project_body(places, high, unpack, first, given, *refs):
    blocks = refs[: len(places)]
    refs = refs[len(places) :]
    if not unpack:
        small_i, shift_i = refs[:2]
        refs = refs[2:]
    qt, kt, vt, shift_o = refs[:4]
    weights = refs[-1]
    assemble(blocks, places, high, weights)
    if unpack:
        shifts = blocks[0][0, 3 * high : 3 * high + 16].astype(F32)[0:8]
    else:
        shifts = shift_i[...]
    shift_o[...] = shifts
    if first:
        small_o, n_o, nt_o = refs[4:7]
        if unpack:
            deep = blocks[0].shape[0]
            wide = blocks[0].shape[2] // 4
            rows = [
                [blocks[2 * x][z, 3 * high : 3 * high + 16].astype(F32) for x in range(2)]
                for z in range(deep)
            ]
            made = []
            for p in range(6):
                r, at = 8 + p // 4, p % 4 * wide
                made.append(
                    jnp.concatenate(
                        [rows[z][x][r : r + 1, at : at + wide] for z in range(deep) for x in range(2)],
                        axis=1,
                    )
                )
            made += [jnp.zeros_like(made[0])] * 2
            small = jnp.concatenate(made, axis=0)
        else:
            small = small_i[...]
        small_o[...] = small
        exact = given[...] * small[0:1] + small[1:2]
        normed = exact.astype(BF16)
        n_o[...] = normed
        nt_o[...] = exact.T.astype(BF16)
    else:
        normed = given[...]
    qt[...] = by_head(dot_nn(normed, weights[0]) + shifts[0:1])
    kt[...] = by_head(dot_nn(normed, weights[1]))
    vt[...] = by_head(dot_nn(normed, weights[2]) + shifts[1:2], 1.0)


def forward_body(first, qt, kt, vt, bias, ot, lse):
    heads, _, window = ot.shape

    def head(i, carry):
        h = first + i
        for q0, qn, k0, k1 in tiles(window):
            scores = dot_tn(kt[h, :, k0:k1], qt[h, :, q0 : q0 + qn])
            scores = scores * LOG2 + bias[k0:k1, q0 : q0 + qn]
            top = jnp.max(scores, axis=0, keepdims=True)
            weight = jnp.exp2(scores - top).astype(BF16)
            mixed = dot_nn(vt[h, :, k0:k1], weight)
            total = mixed[HD : HD + 1]
            ot[i, :, q0 : q0 + qn] = mixed / total
            lse[i, :, q0 : q0 + qn] = top + jnp.log2(total)
        return carry

    lax.fori_loop(0, heads, head, 0, unroll=2)


def feed_body(places, high, x_r, o00, o01, o10, o11, small, cols0, cols1, target, *refs):
    count = len(places)
    blocks = refs[: 2 * count]
    refs = refs[2 * count :]
    out_o, xhat_o, inv_o, n_o = refs[:4]
    atts, acts, slopes, weights = refs[4:6], refs[6:8], refs[8:10], refs[10:]
    for yr in range(2):
        assemble(blocks[yr * count : (yr + 1) * count], places, high, weights[yr])
    for out, a, b in zip(atts, (o00, o10), (o01, o11)):
        out[...] = jnp.concatenate([flat_heads(a[...]), flat_heads(b[...])], axis=0).T.astype(BF16)
    x = x_r[...].astype(F32)
    middle = x + dot_nt(atts[0][...], weights[0][0]) + dot_nt(atts[1][...], weights[1][0]) + small[2:3]
    xhat, inverse = norm_parts(middle)
    xhat_o[...] = xhat
    inv_o[...] = inverse
    normed = (xhat * small[3:4] + small[4:5]).astype(BF16)
    n_o[...] = normed
    result = middle + small[5:6]
    for yr, cols in enumerate((cols0, cols1)):
        pre = dot_nn(normed, weights[yr][1]) + cols[2:3]
        square = pre * pre
        bent = jnp.tanh(GELU * (pre + 0.044715 * (pre * square)))
        act = (0.5 * pre * (1.0 + bent)).astype(BF16)
        acts[yr][...] = act
        slopes[yr][...] = 0.5 * (1.0 + bent) + 0.5 * pre * (1.0 - bent * bent) * (
            GELU * (1.0 + 3.0 * 0.044715 * square)
        )
        result = result + dot_nt(act, weights[yr][2])
    out_o[...] = dot_nn(result.astype(BF16), permutation(target[...])).astype(BF16)


def rows_of(info, feats, units):
    width = feats.shape[1]
    cols = width // 2
    made = []
    for i in range(feats.shape[0]):
        made += [feats[i : i + 1, :cols], feats[i : i + 1, cols:]]
    for own, other in units:
        made += [jnp.where(info[1] == 0, own, other), jnp.where(info[1] == 0, other, own)]
    return jnp.concatenate(made, axis=0)


def feed_back_body(places, high, parts, info, c_r, xhat_r, inv_r, n_r, a0, a1, act0, act1, slope0, slope1, small, target, *refs):
    count = len(places)
    blocks = refs[: 2 * count]
    refs = refs[2 * count :]
    mid_o, d0, d1, sum_o = refs[:4]
    outs = refs[4 : 4 + parts]
    weights = refs[4 + parts :]
    for yr in range(2):
        assemble(blocks[yr * count : (yr + 1) * count], places, high, weights[yr])
    ct_low, normed = c_r[...], n_r[...]
    dnorm, ups = None, []
    for yr, (act, slope) in enumerate(((act0, slope0), (act1, slope1))):
        disassemble(dot_tn(ct_low, act[...]), outs, (yr, 2))
        dpre = (dot_nn(ct_low, weights[yr][2]) * slope[...]).astype(BF16)
        disassemble(dot_tn(normed, dpre), outs, (yr, 1))
        ups.append(jnp.sum(dpre.astype(F32), axis=0, keepdims=True))
        part = dot_nt(dpre, weights[yr][1])
        dnorm = part if dnorm is None else dnorm + part
    ct, xhat = ct_low.astype(F32), xhat_r[...]
    dmiddle = ct + norm_back(dnorm, xhat, inv_r[...], small[3:4])
    mid_o[...] = dmiddle
    sums = [jnp.sum(part, axis=0, keepdims=True) for part in (dmiddle, dnorm * xhat, dnorm, ct)]
    sums = common_order(
        jnp.concatenate(sums + [jnp.zeros((4, dnorm.shape[1]), F32)], axis=0), permutation(target[...])
    )
    sums = rows_of(info, sums[0:4], [ups])
    sum_o[...] = jnp.concatenate([sums, jnp.zeros_like(sums[0:6])], axis=0)
    low = dmiddle.astype(BF16)
    for yr, att in enumerate((a0, a1)):
        disassemble(dot_tn(low, att[...]), outs, (yr, 0))
        (d0, d1)[yr][...] = by_head(dot_nn(low, weights[yr][0]))


def backward_body(first, qt, kt, vt, dt, ot, lse, bias, dq_o, dk_o, dv_o, dq, dk, dv):
    heads, _, window = ot.shape
    made = tiles(window)

    def head(i, carry):
        h = first + i
        delta = jnp.sum(dt[h].astype(F32) * ot[i], axis=0, keepdims=True)
        for ref in (dk, dv):
            ref[i] = jnp.zeros_like(ref[i])
        for q0, qn, k0, k1 in made:
            query, grad = qt[h, :, q0 : q0 + qn], dt[h, :, q0 : q0 + qn]
            scores = dot_tn(kt[h, :, k0:k1], query)
            dprobs = dot_tn(vt[h, :, k0:k1], grad)
            probs = jnp.exp2(scores * LOG2 + (bias[k0:k1, q0 : q0 + qn] - lse[i, :, q0 : q0 + qn]))
            dscores = (probs * (dprobs - delta[:, q0 : q0 + qn])).astype(BF16)
            dq[i, :, q0 : q0 + qn] = dot_nn(kt[h, :, k0:k1], dscores)
            dk[i, :, k0:k1] += dot_nt(query, dscores)
            dv[i, :, k0:k1] += dot_nt(grad, probs.astype(BF16))
        return carry

    lax.fori_loop(0, heads, head, 0, unroll=2)
    for ref, out, factor in ((dq, dq_o, SCALE), (dk, dk_o, SCALE), (dv, dv_o, 1.0)):
        out[...] = (flat_heads(ref[...]) * factor).astype(BF16)


def weigh_body(places, high, parts, nt_r, qa, ka, va, qb, kb, vb, *refs):
    blocks = refs[: len(places)]
    refs = refs[len(places) :]
    dn, sums = refs[:2]
    outs = refs[2 : 2 + parts]
    weights = refs[2 + parts]
    assemble(blocks, places, high, weights)
    normed = nt_r[...]
    ones = jnp.ones((8, normed.shape[1]), BF16)
    total = None
    for w, (a, b) in enumerate(((qa, qb), (ka, kb), (va, vb))):
        low = jnp.concatenate([a[...], b[...]], axis=0)
        disassemble(dot_nt(normed, low), outs, (w,))
        part = dot_nn(weights[w], low)
        total = part if total is None else total + part
        if w != 1:
            sums[w // 2 : w // 2 + 1] = dot_nt(ones, low)[0:1]
    dn[...] = total


def finish_body(info, dn0, dn1, x_r, mid, small, target, qv0, qv1, out_o, sum_o):
    perm = permutation(target[...])
    grad = (dn0[...] + dn1[...]).T
    xhat, inverse = norm_parts(x_r[...].astype(F32))
    dx = mid[...] + norm_back(grad, xhat, inverse, small[0:1])
    out_o[...] = dot_nn(dx.astype(BF16), perm).astype(BF16)
    sums = [jnp.sum(part, axis=0, keepdims=True) for part in (grad * xhat, grad)]
    sums = common_order(jnp.concatenate(sums + [jnp.zeros((6, grad.shape[1]), F32)], axis=0), perm)
    sum_o[...] = rows_of(info, sums[0:2], [(qv0[w : w + 1], qv1[w : w + 1]) for w in range(2)])


def deal_body(info, wo, wu, wd, mine, theirs):
    half = mine.shape[1]
    values = [wo[...].astype(F32).T.astype(BF16), wu[...], wd[...].astype(F32).T.astype(BF16)]

    @pl.when(info[0] == 0)
    def _():
        for w, value in enumerate(values):
            mine[w], theirs[w] = value[:half], value[half:]

    @pl.when(info[0] != 0)
    def _():
        for w, value in enumerate(values):
            theirs[w], mine[w] = value[:half], value[half:]


def meet_a_body(info, wq, wk, wv, got, small, units, units_pair, first):
    half = got.shape[1]
    wr, wc = small.shape[1], units.shape[1]
    zeros = jnp.zeros((8, 4 * wr), F32)

    def meet(own_first, row):
        def pair(own, other):
            return jnp.concatenate([own, other] if own_first else [other, own], axis=1)

        for w, ref in enumerate((wq, wk, wv)):
            first[0, w * half : (w + 1) * half, :] = pair(ref[row : row + half], got[w])
        params = small[...].astype(F32)
        if not own_first:
            params = jnp.concatenate([params[:, half:], params[:, :half]], axis=1)
        above = jnp.concatenate([params[p : p + 1] for p in range(4)], axis=1)
        below = jnp.concatenate([params[4:5], params[5:6], zeros[0:1, : 2 * wr]], axis=1)
        both = pair(units[...], units_pair[...]).astype(F32)
        extra = jnp.concatenate([both, zeros[:5], above, below, zeros[:6]], axis=0)
        first[0, 3 * half : 3 * half + 16, :] = extra.astype(BF16)

    @pl.when(info[0] == 0)
    def _():
        meet(True, 0)

    @pl.when(info[0] != 0)
    def _():
        meet(False, half)


def meet_b_body(info, mine, got, second):
    half = got.shape[1]

    def meet(low, high):
        for w in range(3):
            second[0, w * half : (w + 1) * half, :] = jnp.concatenate([low[w], high[w]], axis=1)

    @pl.when(info[0] == 0)
    def _():
        meet(mine, got)

    @pl.when(info[0] != 0)
    def _():
        meet(got, mine)


def stack_body(*refs):
    out = refs[-1]
    for at, ref in enumerate(refs[:-1]):
        out[at] = ref[0]


def pack(out, row, sums):
    count = sums.shape[0]
    high = sums.astype(BF16)
    out[row : row + count] = high
    out[row + count : row + 2 * count] = (sums - high.astype(F32)).astype(BF16)


def unpack_sums(ref, row, count):
    both = ref[row : row + 2 * count].astype(F32)
    return both[:count] + both[count:]


def far_b_body(keep, got, sums, sums_got, out, sum_o):
    total = sums[...] + sums_got[...]
    sum_o[...] = total
    far_rows(keep.at[1], got.at[1], out)
    pack(out, out.shape[0] - 32, total)


def far_rows(keep, got, out):
    _, deep, high, _ = keep.shape
    for x in range(2):
        for z in range(deep):
            total = keep[x, z].astype(F32) + got[x, z].astype(F32)
            row = (x * deep + z) * high
            out[row : row + high] = total.astype(BF16)


def far_a_body(keep, got, out):
    far_rows(keep, got, out)


def near_rows(keep, got, far, own, out):
    _, deep, high, _ = keep.shape
    for x in range(2):
        for z in range(deep):
            row = (x * deep + z) * high
            total = keep[x, z].astype(F32) + got[x, z].astype(F32) + far[row : row + high].astype(F32)
            if x == 0:
                own[z] = total
            else:
                out[z * high : (z + 1) * high] = total.astype(BF16)


def near_b_body(keep, got, far, sums, own, out, sum_o):
    near_rows(keep.at[0], got.at[0], far, own, out)
    total = sums[...] + unpack_sums(far, far.shape[0] - 32, 16)
    sum_o[...] = total
    pack(out, out.shape[0] - 32, total)


def near_a_body(keep, got, far, sums, sums_got, own, out, sum_o):
    near_rows(keep, got, far, own, out)
    total = sums[...] + sums_got[...]
    sum_o[...] = total
    pack(out, out.shape[0] - 16, total)


def high_body(own, got, sums, *outs):
    deep, high, _ = own.shape
    total = sums[...] + unpack_sums(got, deep * high, sums.shape[0])
    outs[-1][...] = total
    for z in range(deep):
        value = own[z] + got[z * high : (z + 1) * high].astype(F32)
        if z == 0:
            outs[0][...] = value
        else:
            outs[z][0:high] = value.astype(BF16)
            pack(outs[z], high, total)


def last_body(info, own, sums, *refs):
    parts, (mine, theirs, sum_o) = refs[:-3], refs[-3:]
    high = own.shape[0]
    half = high // 3
    total, wide = own[...], sums[...]
    for part in parts:
        total = total + part[0:high].astype(F32)
        wide = wide + unpack_sums(part, high, sums.shape[0])
    sum_o[...] = wide
    wc = mine.shape[2]

    def give(low, upper):
        for w in range(3):
            low[w] = total[w * half : (w + 1) * half, :wc]
            upper[w] = total[w * half : (w + 1) * half, wc:]

    @pl.when(info[0] == 0)
    def _():
        give(mine, theirs)

    @pl.when(info[0] != 0)
    def _():
        give(theirs, mine)


def deliver_body(turned, info, mine, got, *outs):
    half = mine.shape[1]

    def deliver(low, high):
        for w, out in enumerate(outs):
            if turned[w]:
                out[...] = jnp.concatenate([low[w], high[w]], axis=0).T
            else:
                out[0:half] = low[w]
                out[half:] = high[w]

    @pl.when(info[0] == 0)
    def _():
        deliver(mine, got)

    @pl.when(info[0] != 0)
    def _():
        deliver(got, mine)


def join_body(info, segment_ids, own, beside, across, corner, out):
    core, y = info[0], info[1]
    length, window = out.shape[1], own.shape[0]
    gap = length - window
    cuts = cuts_of(segment_ids[...])
    own_cut = jnp.where(y == 0, cuts[0:1], cuts[1:2])
    other_cut = jnp.where(y == 0, cuts[1:2], cuts[0:1])

    def row(low, high, place, cut):
        out[place, 0:gap] = low[0:gap]
        at = (gap + lax.broadcasted_iota(jnp.int32, (window - gap, 1), 0)).astype(F32)
        seam = jnp.where(at < cut, low[gap:window].astype(F32), high[0 : window - gap].astype(F32))
        out[place, gap:window] = seam.astype(BF16)
        out[place, window:length] = high[window - gap : window]

    @pl.when(core == 0)
    def _():
        row(own, beside, y, own_cut)
        row(across, corner, 1 - y, other_cut)

    @pl.when(core != 0)
    def _():
        row(beside, own, y, own_cut)
        row(corner, across, 1 - y, other_cut)


def per_device(
    hidden_in,
    segment_ids,
    pad_flags,
    gain1,
    shift1,
    w_query,
    b_query,
    w_key,
    w_value,
    b_value,
    w_out,
    b_out,
    gain2,
    shift2,
    w_up,
    b_up,
    w_down,
    b_down,
    cotangent,
):
    fs, mp = lax.axis_size("fsdp"), lax.axis_size("mp")
    rows, length, width = hidden_in.shape
    wr, wc = w_query.shape
    half, cols = wr // 2, 2 * wc
    heads = cols // HD
    f, m = lax.axis_index("fsdp"), lax.axis_index("mp")
    core, y = m % 2, m // 2
    side = jnp.stack([core, y])
    window = length // 2 + MOST // 2
    deep = fs // 2
    flips = [2 * z for z in range(1, deep)]
    staged = half % 16 == 0 and deep == 4
    if staged:
        places = [[((z * 2 + x) * 2 + c) * half for z in range(deep)] for x in range(2) for c in range(2)]
        high, parts = half, 2
    else:
        places, high, parts = [[0]], width, 1
    wide, tall = (window, width), (width, window)
    by_heads, by_few = (heads, PAD, window), (heads // 2, PAD, window)
    weights = pltpu.VMEM((3, width, cols), BF16)

    def to(value, flip_f, flip_m):
        return send(value, fs, mp, flip_f, flip_m)

    def begin(target):
        return call(
            start_body,
            [(wide, BF16), (wide, BF16), (wide, F32), ((window, window), F32)],
            [side, hidden_in, cotangent, segment_ids, pad_flags, target],
            (),
            1,
            us=3,
            mib=10,
        )

    def project(given, blocks, first, extra=()):
        outs = [(by_heads, BF16)] * 3 + [((8, cols), F32)]
        if first:
            outs += [((8, width), F32), (wide, BF16), (tall, BF16)]
        return call(
            functools.partial(project_body, places, high, not extra, first),
            outs,
            [given] + blocks + list(extra),
            [weights],
            us=2,
            mib=10,
        )

    def attend(part, qkv_heads, bias):
        return call(
            functools.partial(forward_body, part * (heads // 2)),
            [(by_few, F32), ((heads // 2, 1, window), F32)],
            list(qkv_heads) + [bias],
            us=5,
        )

    def feed(x, mixed, small, shifts, target, blocks):
        units_shape = (window, cols)
        return call(
            functools.partial(feed_body, places, high),
            [(wide, BF16), (wide, F32), ((window, 1), F32), (wide, BF16)]
            + [(units_shape, BF16)] * 4
            + [(units_shape, F32)] * 2,
            [x] + mixed + [small] + shifts + [target] + blocks,
            [weights, weights],
            us=5,
            mib=14,
        )

    def feed_back(side, ct, made, small, target, blocks):
        if staged:
            grads = [((2, 2, deep, 3 * half, cols), BF16)] * 2
        else:
            grads = [((2, 3, width, cols), BF16)]
        return call(
            functools.partial(feed_back_body, places, high, parts),
            [(wide, F32), (by_heads, BF16), (by_heads, BF16), ((16, cols), F32)] + grads,
            [side, ct] + list(made) + [small, target] + blocks,
            [weights, weights],
            1,
            us=7,
            mib=14,
        )

    def backward(part, qkv_heads, da, o, lse, bias):
        return call(
            functools.partial(backward_body, part * (heads // 2)),
            [((heads // 2 * HD, window), BF16)] * 3,
            list(qkv_heads) + [da, o, lse, bias],
            [pltpu.VMEM(by_few, F32)] * 3,
            us=6,
        )

    def weigh(normed_t, blocks, low_a, low_b):
        if staged:
            grads = [((2, deep, 3 * half, cols), BF16)] * 2
        else:
            grads = [((3, width, cols), BF16)]
        return call(
            functools.partial(weigh_body, places, high, parts),
            [(tall, F32), ((2, cols), F32)] + grads,
            [normed_t] + list(low_a) + list(low_b) + blocks,
            [weights],
            us=4,
        )

    def finish(side, dn0, dn1, x, dmiddle, small, target, qv0, qv1):
        return call(
            finish_body,
            [(wide, BF16), ((8, cols), F32)],
            [side, dn0, dn1, x, dmiddle, small, target, qv0, qv1],
            (),
            1,
            us=4,
            mib=10,
        )

    def join(own, beside, across, corner):
        operands = [side, segment_ids, own, beside, across, corner]
        return call(join_body, [((rows, length, width), BF16)], operands, (), 1, us=4)[0]

    if not staged:

        def gathered(blocks):
            full = []
            for block in blocks:
                block = lax.all_gather(block, "fsdp", axis=0, tiled=True)
                full.append(lax.all_gather(block, "mp", axis=1, tiled=True))
            full = jnp.stack(full)
            return [full[:, :, yr * cols : (yr + 1) * cols].reshape(1, 3 * width, cols) for yr in range(2)]

        target = lax.iota(jnp.int32, width)[None]
        wa = gathered([w_query, w_key, w_value])
        wb = gathered([w_out.T, w_up, w_down.T])
        small = jnp.stack([gain1, shift1, b_out, gain2, shift2, b_down] + [jnp.zeros_like(gain1)] * 2)
        small = lax.all_gather(small, "fsdp", axis=1, tiled=True).astype(F32)
        units = jnp.stack([b_query, b_value, b_up] + [jnp.zeros_like(b_up)] * 5)
        units = lax.all_gather(units, "mp", axis=1, tiled=True).astype(F32)
        units = [units[:, :cols], units[:, cols:]]
        x, ct, xhat, bias = begin(target)
        *heads0, _, _, normed, normed_t = project(xhat, [wa[0]], True, (small, units[0]))
        *heads1, _ = project(normed, [wa[1]], False, (small, units[1]))
        both = (heads0, heads1)
        mixed = [attend(part, both[yr], bias) for yr in range(2) for part in range(2)]
        made = feed(x, [o for o, _ in mixed], small, units, target, wb)
        result = made[0]
        none = jnp.zeros_like(side)
        dmiddle, da0, da1, sums_b, grads_b = feed_back(none, ct, made[1:], small, target, wb)
        dn, qv, grads_a = [], [], []
        for yr, da in enumerate((da0, da1)):
            lows = [backward(part, both[yr], da, *mixed[2 * yr + part], bias) for part in range(2)]
            got = weigh(normed_t, [wa[yr]], *lows)
            dn.append(got[0])
            qv.append(got[1])
            grads_a.append(got[2])
        grad_window, sums_a = finish(none, dn[0], dn[1], x, dmiddle, small, target, *qv)

        def scattered(pair):
            full = jnp.concatenate(pair, axis=2).astype(F32)
            full = lax.psum_scatter(full, "mp", scatter_dimension=2, tiled=True)
            return lax.psum_scatter(full, "fsdp", scatter_dimension=1, tiled=True)

        grad_q, grad_k, grad_v = scattered(grads_a)
        grad_out, grad_up, grad_down = scattered([grads_b[0], grads_b[1]])
        grad_out, grad_down = grad_out.T, grad_down.T
        sums_a, sums_b = sums_a.reshape(4, width), sums_b.reshape(8, width)
        sums = jnp.concatenate([sums_a[0:2], sums_b[0:4], sums_a[2:4], sums_b[4:5]])
        sums = lax.psum(sums, BOTH)
        mine_f = lax.dynamic_slice(sums, (0, f * wr), (6, wr))
        mine_u = lax.dynamic_slice(sums, (6, m * wc), (3, wc))

        def shared(value):
            across = to(value, 0, 2)
            return join(value, to(value, 0, 1), across, to(across, 0, 1))

        out_hidden, grad_hidden = shared(result), shared(grad_window)
    else:
        piece_a, piece_b = (1, 3 * half + 16, cols), (1, 3 * half, cols)

        def stacked(pieces):
            return call(stack_body, [((deep,) + pieces[0].shape[1:], BF16)], pieces)[0]

        def away(block):
            return lax.dynamic_slice(block, ((1 - core) * half, 0), (half, wc))

        theirs = jnp.stack([away(w) for w in (w_query, w_key, w_value)])
        got = to(theirs, 0, 1)
        theirs, gain1, b_query, w_out = fence(theirs, gain1, b_query, w_out)
        small = jnp.stack([gain1, shift1, b_out, gain2, shift2, b_down])
        units = jnp.stack([b_query, b_value, b_up])
        units_pair = to(units, 0, 1)
        feature = lax.iota(jnp.int32, width)
        target = (((feature // half) ^ (f * 2 + core)) * half + feature % half)[None]
        got, units_pair, small, w_out = fence(got, units_pair, small, w_out)

        first = call(
            meet_a_body, [(piece_a, BF16)], [side, w_query, w_key, w_value, got, small, units, units_pair], (), 1
        )[0]
        first_parts = [to(first, flip, 0) for flip in flips]
        mine, theirs = call(deal_body, [((3, half, wc), BF16)] * 2, [side, w_out, w_up, w_down], (), 1)
        got = to(theirs, 0, 1)
        second = call(meet_b_body, [(piece_b, BF16)], [side, mine, got], (), 1)[0]
        first, first_parts, second, hidden_in, target = fence(first, first_parts, second, hidden_in, target)

        qkv = stacked([first] + first_parts)
        qkv_x, qkv_y = to(qkv, 1, 0), to(qkv, 0, 2)
        second_parts = [to(second, flip, 0) for flip in flips]
        x, ct, xhat, bias = begin(target)
        second_parts, second, qkv, qkv_x, qkv_y, xhat = fence(second_parts, second, qkv, qkv_x, qkv_y, xhat)
        qkv_xy = to(qkv, 1, 2)

        qkv_c, qkv_xc = to(qkv, 0, 1), to(qkv_x, 0, 1)
        odu = stacked([second] + second_parts)
        near = [qkv, qkv_c, qkv_x, qkv_xc]
        *heads0, shift0, small, normed, normed_t = project(xhat, near, True)
        heads0, qkv_y, odu = fence(heads0, qkv_y, odu)
        qkv_yc, odu_x, odu_y = to(qkv_y, 0, 1), to(odu, 1, 0), to(odu, 0, 2)
        o00, l00 = attend(0, heads0, bias)
        o00, heads0, qkv_yc, qkv_xy, odu = fence(o00, heads0, qkv_yc, qkv_xy, odu)
        qkv_xyc, odu_xy, odu_c = to(qkv_xy, 0, 1), to(odu, 1, 2), to(odu, 0, 1)
        o01, l01 = attend(1, heads0, bias)
        o01, qkv_xyc, odu_c, normed = fence(o01, qkv_xyc, odu_c, normed)
        far = [qkv_y, qkv_yc, qkv_xy, qkv_xyc]
        *heads1, shift1u = project(normed, far, False)
        o10, l10 = attend(0, heads1, bias)
        o10, heads1, odu_x, odu_y = fence(o10, heads1, odu_x, odu_y)
        odu_xc, odu_yc = to(odu_x, 0, 1), to(odu_y, 0, 1)
        o11, l11 = attend(1, heads1, bias)
        o11, odu_xc, odu_yc, odu_xy = fence(o11, odu_xc, odu_yc, odu_xy)
        odu_xyc = to(odu_xy, 0, 1)

        odu_blocks = [odu, odu_c, odu_x, odu_xc, odu_y, odu_yc, odu_xy, odu_xyc]
        made = fence(*feed(x, [o00, o01, o10, o11], small, [shift0, shift1u], target, odu_blocks))
        result = made[0]
        res_c, res_y = to(result, 0, 1), to(result, 0, 2)
        made = feed_back(side, ct, made[1:], small, target, odu_blocks)
        dmiddle, da0, da1, b_sums, b_keep, b_send, res_c = fence(*made, res_c)

        n_far, n_near = 2 * deep * 3 * half, deep * 3 * half
        f32_16, f32_8 = ((16, cols), F32), ((8, cols), F32)
        b_got, b_sums_got = to(b_send, 0, 1), to(b_sums, 0, 1)
        low10 = backward(0, heads1, da1, o10, l10, bias)
        low10, heads1, b_got, b_sums_got = fence(low10, heads1, b_got, b_sums_got)
        b_far, b_sums = call(
            far_b_body,
            [((n_far + 32, cols), BF16), f32_16],
            [b_keep, b_got, b_sums, b_sums_got],
        )
        b_far = to(b_far, 0, 2)
        low11 = backward(1, heads1, da1, o11, l11, bias)
        low11, normed_t, res_y = fence(low11, normed_t, res_y)
        res_yc = to(res_y, 0, 1)
        dn1, qv1, keep1, send1 = weigh(normed_t, far, low10, low11)
        dn1, keep1, send1, da0, res_yc = fence(dn1, keep1, send1, da0, res_yc)
        got1 = to(send1, 0, 1)
        low00 = backward(0, heads0, da0, o00, l00, bias)
        low00, heads0, got1, b_far = fence(low00, heads0, got1, b_far)
        a_far = call(far_a_body, [((n_far, cols), BF16)], [keep1, got1])[0]
        a_far = to(a_far, 0, 2)
        b_own, b_x, b_sums = call(
            near_b_body,
            [((deep, 3 * half, cols), F32), ((n_near + 32, cols), BF16), f32_16],
            [b_keep, b_got, b_far, b_sums],
        )
        b_x = to(b_x, 1, 0)
        low01 = backward(1, heads0, da0, o01, l01, bias)
        low01, normed_t, b_x = fence(low01, normed_t, b_x)
        b_split = call(
            high_body,
            [((3 * half, cols), F32)] + [((3 * half + 32, cols), BF16)] * (deep - 1) + [f32_16],
            [b_own, b_x, b_sums],
        )
        b_high = [to(part, flip, 0) for part, flip in zip(b_split[1:-1], flips)]
        dn0, qv0, keep0, send0 = weigh(normed_t, near, low00, low01)
        dn0, keep0, send0, dmiddle = fence(dn0, keep0, send0, dmiddle)
        got0 = to(send0, 0, 1)
        grad_window, a_sums = finish(side, dn0, dn1, x, dmiddle, small, target, qv0, qv1)
        grad_window, a_sums, got0, b_high = fence(grad_window, a_sums, got0, b_high)

        gw_y, gw_c = to(grad_window, 0, 2), to(grad_window, 0, 1)
        a_sums_got = to(a_sums, 0, 1)
        a_own, a_x, a_sums = call(
            near_a_body,
            [((deep, 3 * half, cols), F32), ((n_near + 16, cols), BF16), f32_8],
            [keep0, got0, a_far, a_sums, a_sums_got],
        )
        a_x = to(a_x, 1, 0)

        def last(own, sums, got, kind):
            return call(last_body, [((3, half, wc), F32)] * 2 + [kind], [side, own, sums] + got, (), 1)

        def deliver(mine, got, turned):
            shapes = [((wc, wr) if t else (wr, wc), F32) for t in turned]
            return call(functools.partial(deliver_body, turned), shapes, [side, mine, got], (), 1)

        b_mine, b_theirs, b_sums = last(b_split[0], b_split[-1], b_high, f32_16)
        b_last = to(b_theirs, 0, 1)
        result, gw_c = fence(result, gw_c)
        out_hidden = join(result, res_c, res_y, res_yc)
        grad_out, grad_up, grad_down = deliver(b_mine, b_last, (True, False, True))
        a_x, a_own, out_hidden = fence(a_x, a_own, out_hidden)
        a_split = call(
            high_body,
            [((3 * half, cols), F32)] + [((3 * half + 16, cols), BF16)] * (deep - 1) + [f32_8],
            [a_own, a_x, a_sums],
        )
        a_high = [to(part, flip, 0) for part, flip in zip(a_split[1:-1], flips)]
        gw_yc = to(gw_y, 0, 1)
        grad_hidden = join(grad_window, gw_c, gw_y, gw_yc)
        grad_hidden, a_own, a_high = fence(grad_hidden, a_split[0], a_high)
        a_mine, a_theirs, a_sums = last(a_own, a_split[-1], a_high, f32_8)
        a_last = to(a_theirs, 0, 1)
        a_sums = a_sums + to(a_sums, 0, 2)
        grad_q, grad_k, grad_v = deliver(a_mine, a_last, (False, False, False))
        sums = jnp.concatenate(
            [
                a_sums.reshape(4, width)[0:2],
                b_sums.reshape(8, width)[0:4],
                a_sums.reshape(4, width)[2:4],
                b_sums.reshape(8, width)[4:5],
            ]
        )
        mine_f = lax.dynamic_slice(sums, (0, f * wr), (6, wr))
        mine_u = lax.dynamic_slice(sums, (6, m * wc), (3, wc))
    return (
        out_hidden,
        grad_hidden,
        mine_f[0],
        mine_f[1],
        grad_q,
        mine_u[0],
        grad_k,
        grad_v,
        mine_u[1],
        grad_out,
        mine_f[2],
        mine_f[3],
        mine_f[4],
        grad_up,
        mine_u[2],
        grad_down,
        mine_f[5],
    )


def solution(mesh):
    return jax.shard_map(
        per_device,
        mesh=mesh,
        in_specs=(
            P("fsdp", None, None),
            P("fsdp", None),
            P("fsdp", None),
            P("fsdp"),
            P("fsdp"),
            P("fsdp", "mp"),
            P("mp"),
            P("fsdp", "mp"),
            P("fsdp", "mp"),
            P("mp"),
            P("mp", "fsdp"),
            P("fsdp"),
            P("fsdp"),
            P("fsdp"),
            P("fsdp", "mp"),
            P("mp"),
            P("mp", "fsdp"),
            P("fsdp"),
            P("fsdp", None, None),
        ),
        out_specs=(
            P("fsdp", None, None),
            P("fsdp", None, None),
            P("fsdp"),
            P("fsdp"),
            P("fsdp", "mp"),
            P("mp"),
            P("fsdp", "mp"),
            P("fsdp", "mp"),
            P("mp"),
            P("mp", "fsdp"),
            P("fsdp"),
            P("fsdp"),
            P("fsdp"),
            P("fsdp", "mp"),
            P("mp"),
            P("mp", "fsdp"),
            P("fsdp"),
        ),
        check_vma=False,
    )
```

```python
import functools
import math

import jax
import jax.numpy as jnp
from jax import lax
from jax.experimental import pallas as pl
from jax.experimental.pallas import tpu as pltpu
from jax.sharding import PartitionSpec as P

HD = 24
PAD = 32
MOST = 128
BOTH = ("fsdp", "mp")
EPS = 1e-05
F32 = jnp.float32
BF16 = jnp.bfloat16
LOG2 = math.log2(math.e) / math.sqrt(HD)
SCALE = 1.0 / math.sqrt(HD)
GELU = math.sqrt(2.0 / math.pi)


def send(value, fs, mp, flip_f, flip_m):
    pairs = [(f * mp + m, (f ^ flip_f) * mp + (m ^ flip_m)) for f in range(fs) for m in range(mp)]
    return lax.ppermute(value, BOTH, pairs)


def dot_nn(left, right):
    return lax.dot_general(left, right, (((1,), (0,)), ((), ())), preferred_element_type=F32)


def dot_nt(left, right):
    return lax.dot_general(left, right, (((1,), (1,)), ((), ())), preferred_element_type=F32)


def dot_tn(left, right):
    return lax.dot_general(left, right, (((0,), (0,)), ((), ())), preferred_element_type=F32)


def norm_parts(values):
    centre = jnp.mean(values, axis=-1, keepdims=True)
    centered = values - centre
    inverse = lax.rsqrt(jnp.mean(centered * centered, axis=-1, keepdims=True) + EPS)
    return centered * inverse, inverse


def norm_back(grad, normed, inverse, gain):
    scaled = grad * gain
    return inverse * (
        scaled
        - jnp.mean(scaled, axis=-1, keepdims=True)
        - normed * jnp.mean(scaled * normed, axis=-1, keepdims=True)
    )


def call(body, outs, operands, scratch=(), scalars=0, us=0.1, mib=6):
    whole = pl.BlockSpec(memory_space=pltpu.VMEM)
    few = pl.BlockSpec(memory_space=pltpu.SMEM)
    return pl.pallas_call(
        body,
        out_shape=tuple(jax.ShapeDtypeStruct(s, d) for s, d in outs),
        in_specs=[few] * scalars + [whole] * (len(operands) - scalars),
        out_specs=tuple(whole for _ in outs),
        scratch_shapes=list(scratch),
        name=getattr(body, "func", body).__name__,
        compiler_params=pltpu.CompilerParams(vmem_limit_bytes=mib << 20),
        cost_estimate=pl.CostEstimate(
            flops=int(us * 2e9), transcendentals=0, bytes_accessed=int(us * 3e6)
        ),
    )(*operands)


def fence(*values):
    return lax.optimization_barrier(values)


def tiles(window):
    made = []
    for q0 in range(0, window, 256):
        qn = min(256, window - q0)
        k0 = max(0, q0 - MOST)
        made.append((q0, qn, k0, min(window, q0 + qn + MOST)))
    return made


def permutation(target):
    width = target.shape[1]
    return (lax.broadcasted_iota(jnp.int32, (width, width), 0) == target).astype(BF16)


def cuts_of(segments):
    middle = segments.shape[1] // 2
    held = segments[:, middle : middle + 1]
    first = jnp.sum((segments < held).astype(F32), axis=1, keepdims=True)
    last = jnp.sum((segments <= held).astype(F32), axis=1, keepdims=True)
    return jnp.where(middle - first <= last - middle, first, last)


def start_body(info, hidden, cotangent, segment_ids, pad_flags, target, x_o, c_o, xhat_o, bias_o):
    core, y = info[0], info[1]
    window = x_o.shape[0]
    gap = hidden.shape[1] - window
    start = pl.multiple_of(core * gap, 16)
    segments = segment_ids[...]
    cuts = cuts_of(segments)
    cut = jnp.where(y == 0, cuts[0:1], cuts[1:2])
    here = (start + lax.broadcasted_iota(jnp.int32, (window, 1), 0)).astype(F32)
    before = (here < cut).astype(F32)
    owned = jnp.where(core == 0, before, 1.0 - before)
    perm = permutation(target[...])
    x = dot_nn(hidden[y, pl.ds(start, window), :], perm)
    x_o[...] = x.astype(BF16)
    c_o[...] = (dot_nn(cotangent[y, pl.ds(start, window), :], perm) * owned).astype(BF16)
    xhat_o[...] = norm_parts(x)[0]
    segs = jnp.where(y == 0, segments[0:1], segments[1:2]).astype(F32)
    pads = pad_flags[...]
    pads = jnp.where(y == 0, pads[0:1], pads[1:2])
    code = jnp.where(pads == 0, segs, -1.0)
    segs = jnp.where(core == 0, segs[:, :window], segs[:, gap:])
    code = jnp.where(core == 0, code[:, :window], code[:, gap:])
    column = jnp.broadcast_to(code, (8, window)).T[:, 0:1]
    key = lax.broadcasted_iota(jnp.int32, (window, window), 0)
    query = lax.broadcasted_iota(jnp.int32, (window, window), 1)
    bias_o[...] = jnp.where((column == segs) | (key == query), 0.0, -1e30)


def assemble(blocks, places, high, weights):
    for block, rows in zip(blocks, places):
        for z, row in enumerate(rows):
            for w in range(3):
                weights[w, row : row + high] = block[z, w * high : (w + 1) * high]


def disassemble(value, outs, pick):
    value = value.astype(BF16)
    if len(outs) == 1:
        outs[0][pick] = value
        return
    _, deep, high, _ = outs[0].shape[-4:]
    half = high // 3
    yr, w = pick[:-1], pick[-1]
    for x in range(2):
        for z in range(deep):
            for c in range(2):
                at = ((z * 2 + x) * 2 + c) * half
                outs[c][yr + (x, z, pl.ds(w * half, half))] = value[at : at + half]


def common_order(rows, perm):
    high = rows.astype(BF16)
    rest = rows - high.astype(F32)
    mid = rest.astype(BF16)
    last = (rest - mid.astype(F32)).astype(BF16)
    return dot_nn(high, perm) + dot_nn(mid, perm) + dot_nn(last, perm)


def by_head(value, fill=0.0):
    tokens, columns = value.shape
    parts = value.T.reshape(columns // HD, HD, tokens)
    row = lax.broadcasted_iota(jnp.int32, (columns // HD, PAD - HD, tokens), 1)
    extra = jnp.where(row == 0, fill, 0.0)
    return jnp.concatenate([parts, extra], axis=1).astype(BF16)


def flat_heads(value):
    heads, _, tokens = value.shape
    return value[:, :HD, :].reshape(heads * HD, tokens)


def project_body(places, high, unpack, first, given, *refs):
    blocks = refs[: len(places)]
    refs = refs[len(places) :]
    if not unpack:
        small_i, shift_i = refs[:2]
        refs = refs[2:]
    qt, kt, vt, shift_o = refs[:4]
    weights = refs[-1]
    assemble(blocks, places, high, weights)
    if unpack:
        shifts = blocks[0][0, 3 * high : 3 * high + 16].astype(F32)[0:8]
    else:
        shifts = shift_i[...]
    shift_o[...] = shifts
    if first:
        small_o, n_o, nt_o = refs[4:7]
        if unpack:
            deep = blocks[0].shape[0]
            wide = blocks[0].shape[2] // 4
            rows = [
                [blocks[2 * x][z, 3 * high : 3 * high + 16].astype(F32) for x in range(2)]
                for z in range(deep)
            ]
            made = []
            for p in range(6):
                r, at = 8 + p // 4, p % 4 * wide
                made.append(
                    jnp.concatenate(
                        [rows[z][x][r : r + 1, at : at + wide] for z in range(deep) for x in range(2)],
                        axis=1,
                    )
                )
            made += [jnp.zeros_like(made[0])] * 2
            small = jnp.concatenate(made, axis=0)
        else:
            small = small_i[...]
        small_o[...] = small
        exact = given[...] * small[0:1] + small[1:2]
        normed = exact.astype(BF16)
        n_o[...] = normed
        nt_o[...] = exact.T.astype(BF16)
    else:
        normed = given[...]
    qt[...] = by_head(dot_nn(normed, weights[0]) + shifts[0:1])
    kt[...] = by_head(dot_nn(normed, weights[1]))
    vt[...] = by_head(dot_nn(normed, weights[2]) + shifts[1:2], 1.0)


def forward_body(first, qt, kt, vt, bias, ot, lse):
    heads, _, window = ot.shape

    def head(i, carry):
        h = first + i
        for q0, qn, k0, k1 in tiles(window):
            scores = dot_tn(kt[h, :, k0:k1], qt[h, :, q0 : q0 + qn])
            scores = scores * LOG2 + bias[k0:k1, q0 : q0 + qn]
            top = jnp.max(scores, axis=0, keepdims=True)
            weight = jnp.exp2(scores - top).astype(BF16)
            mixed = dot_nn(vt[h, :, k0:k1], weight)
            total = mixed[HD : HD + 1]
            ot[i, :, q0 : q0 + qn] = mixed / total
            lse[i, :, q0 : q0 + qn] = top + jnp.log2(total)
        return carry

    lax.fori_loop(0, heads, head, 0, unroll=2)


def feed_body(places, high, x_r, o00, o01, o10, o11, small, cols0, cols1, target, *refs):
    count = len(places)
    blocks = refs[: 2 * count]
    refs = refs[2 * count :]
    out_o, xhat_o, inv_o, n_o = refs[:4]
    atts, acts, slopes, weights = refs[4:6], refs[6:8], refs[8:10], refs[10:]
    for yr in range(2):
        assemble(blocks[yr * count : (yr + 1) * count], places, high, weights[yr])
    for out, a, b in zip(atts, (o00, o10), (o01, o11)):
        out[...] = jnp.concatenate([flat_heads(a[...]), flat_heads(b[...])], axis=0).T.astype(BF16)
    x = x_r[...].astype(F32)
    middle = x + dot_nt(atts[0][...], weights[0][0]) + dot_nt(atts[1][...], weights[1][0]) + small[2:3]
    xhat, inverse = norm_parts(middle)
    xhat_o[...] = xhat
    inv_o[...] = inverse
    normed = (xhat * small[3:4] + small[4:5]).astype(BF16)
    n_o[...] = normed
    result = middle + small[5:6]
    for yr, cols in enumerate((cols0, cols1)):
        pre = dot_nn(normed, weights[yr][1]) + cols[2:3]
        square = pre * pre
        bent = jnp.tanh(GELU * (pre + 0.044715 * (pre * square)))
        act = (0.5 * pre * (1.0 + bent)).astype(BF16)
        acts[yr][...] = act
        slopes[yr][...] = 0.5 * (1.0 + bent) + 0.5 * pre * (1.0 - bent * bent) * (
            GELU * (1.0 + 3.0 * 0.044715 * square)
        )
        result = result + dot_nt(act, weights[yr][2])
    out_o[...] = dot_nn(result.astype(BF16), permutation(target[...])).astype(BF16)


def rows_of(info, feats, units):
    width = feats.shape[1]
    cols = width // 2
    made = []
    for i in range(feats.shape[0]):
        made += [feats[i : i + 1, :cols], feats[i : i + 1, cols:]]
    for own, other in units:
        made += [jnp.where(info[1] == 0, own, other), jnp.where(info[1] == 0, other, own)]
    return jnp.concatenate(made, axis=0)


def feed_back_body(places, high, parts, info, c_r, xhat_r, inv_r, n_r, a0, a1, act0, act1, slope0, slope1, small, target, *refs):
    count = len(places)
    blocks = refs[: 2 * count]
    refs = refs[2 * count :]
    mid_o, d0, d1, sum_o = refs[:4]
    outs = refs[4 : 4 + parts]
    weights = refs[4 + parts :]
    for yr in range(2):
        assemble(blocks[yr * count : (yr + 1) * count], places, high, weights[yr])
    ct_low, normed = c_r[...], n_r[...]
    dnorm, ups = None, []
    for yr, (act, slope) in enumerate(((act0, slope0), (act1, slope1))):
        disassemble(dot_tn(ct_low, act[...]), outs, (yr, 2))
        dpre = (dot_nn(ct_low, weights[yr][2]) * slope[...]).astype(BF16)
        disassemble(dot_tn(normed, dpre), outs, (yr, 1))
        ups.append(jnp.sum(dpre.astype(F32), axis=0, keepdims=True))
        part = dot_nt(dpre, weights[yr][1])
        dnorm = part if dnorm is None else dnorm + part
    ct, xhat = ct_low.astype(F32), xhat_r[...]
    dmiddle = ct + norm_back(dnorm, xhat, inv_r[...], small[3:4])
    mid_o[...] = dmiddle
    sums = [jnp.sum(part, axis=0, keepdims=True) for part in (dmiddle, dnorm * xhat, dnorm, ct)]
    sums = common_order(
        jnp.concatenate(sums + [jnp.zeros((4, dnorm.shape[1]), F32)], axis=0), permutation(target[...])
    )
    sums = rows_of(info, sums[0:4], [ups])
    sum_o[...] = jnp.concatenate([sums, jnp.zeros_like(sums[0:6])], axis=0)
    low = dmiddle.astype(BF16)
    for yr, att in enumerate((a0, a1)):
        disassemble(dot_tn(low, att[...]), outs, (yr, 0))
        (d0, d1)[yr][...] = by_head(dot_nn(low, weights[yr][0]))


def backward_body(first, qt, kt, vt, dt, ot, lse, bias, dq_o, dk_o, dv_o, dq, dk, dv):
    heads, _, window = ot.shape
    made = tiles(window)

    def head(i, carry):
        h = first + i
        delta = jnp.sum(dt[h].astype(F32) * ot[i], axis=0, keepdims=True)
        for ref in (dk, dv):
            ref[i] = jnp.zeros_like(ref[i])
        for q0, qn, k0, k1 in made:
            query, grad = qt[h, :, q0 : q0 + qn], dt[h, :, q0 : q0 + qn]
            scores = dot_tn(kt[h, :, k0:k1], query)
            dprobs = dot_tn(vt[h, :, k0:k1], grad)
            probs = jnp.exp2(scores * LOG2 + (bias[k0:k1, q0 : q0 + qn] - lse[i, :, q0 : q0 + qn]))
            dscores = (probs * (dprobs - delta[:, q0 : q0 + qn])).astype(BF16)
            dq[i, :, q0 : q0 + qn] = dot_nn(kt[h, :, k0:k1], dscores)
            dk[i, :, k0:k1] += dot_nt(query, dscores)
            dv[i, :, k0:k1] += dot_nt(grad, probs.astype(BF16))
        return carry

    lax.fori_loop(0, heads, head, 0, unroll=1)
    for ref, out, factor in ((dq, dq_o, SCALE), (dk, dk_o, SCALE), (dv, dv_o, 1.0)):
        out[...] = (flat_heads(ref[...]) * factor).astype(BF16)


def weigh_body(places, high, parts, nt_r, qa, ka, va, qb, kb, vb, *refs):
    blocks = refs[: len(places)]
    refs = refs[len(places) :]
    dn, sums = refs[:2]
    outs = refs[2 : 2 + parts]
    weights = refs[2 + parts]
    assemble(blocks, places, high, weights)
    normed = nt_r[...]
    ones = jnp.ones((8, normed.shape[1]), BF16)
    total = None
    for w, (a, b) in enumerate(((qa, qb), (ka, kb), (va, vb))):
        low = jnp.concatenate([a[...], b[...]], axis=0)
        disassemble(dot_nt(normed, low), outs, (w,))
        part = dot_nn(weights[w], low)
        total = part if total is None else total + part
        if w != 1:
            sums[w // 2 : w // 2 + 1] = dot_nt(ones, low)[0:1]
    dn[...] = total


def finish_body(info, dn0, dn1, x_r, mid, small, target, qv0, qv1, out_o, sum_o):
    perm = permutation(target[...])
    grad = (dn0[...] + dn1[...]).T
    xhat, inverse = norm_parts(x_r[...].astype(F32))
    dx = mid[...] + norm_back(grad, xhat, inverse, small[0:1])
    out_o[...] = dot_nn(dx.astype(BF16), perm).astype(BF16)
    sums = [jnp.sum(part, axis=0, keepdims=True) for part in (grad * xhat, grad)]
    sums = common_order(jnp.concatenate(sums + [jnp.zeros((6, grad.shape[1]), F32)], axis=0), perm)
    sum_o[...] = rows_of(info, sums[0:2], [(qv0[w : w + 1], qv1[w : w + 1]) for w in range(2)])


def deal_body(info, wo, wu, wd, mine, theirs):
    half = mine.shape[1]
    values = [wo[...].astype(F32).T.astype(BF16), wu[...], wd[...].astype(F32).T.astype(BF16)]

    @pl.when(info[0] == 0)
    def _():
        for w, value in enumerate(values):
            mine[w], theirs[w] = value[:half], value[half:]

    @pl.when(info[0] != 0)
    def _():
        for w, value in enumerate(values):
            theirs[w], mine[w] = value[:half], value[half:]


def meet_a_body(info, mine, got, small, units, units_pair, first):
    half = got.shape[1]
    wr, wc = small.shape[1], units.shape[1]
    zeros = jnp.zeros((8, 4 * wr), F32)

    def meet(own_first):
        def pair(own, other):
            return jnp.concatenate([own, other] if own_first else [other, own], axis=1)

        for w in range(3):
            first[0, w * half : (w + 1) * half, :] = pair(mine[w], got[w])
        params = small[...].astype(F32)
        if not own_first:
            params = jnp.concatenate([params[:, half:], params[:, :half]], axis=1)
        above = jnp.concatenate([params[p : p + 1] for p in range(4)], axis=1)
        below = jnp.concatenate([params[4:5], params[5:6], zeros[0:1, : 2 * wr]], axis=1)
        both = pair(units[...], units_pair[...]).astype(F32)
        extra = jnp.concatenate([both, zeros[:5], above, below, zeros[:6]], axis=0)
        first[0, 3 * half : 3 * half + 16, :] = extra.astype(BF16)

    @pl.when(info[0] == 0)
    def _():
        meet(True)

    @pl.when(info[0] != 0)
    def _():
        meet(False)


def meet_b_body(info, mine, got, second):
    half = got.shape[1]

    def meet(low, high):
        for w in range(3):
            second[0, w * half : (w + 1) * half, :] = jnp.concatenate([low[w], high[w]], axis=1)

    @pl.when(info[0] == 0)
    def _():
        meet(mine, got)

    @pl.when(info[0] != 0)
    def _():
        meet(got, mine)


def stack_body(*refs):
    out = refs[-1]
    for at, ref in enumerate(refs[:-1]):
        out[at] = ref[0]


def pack(out, row, sums):
    count = sums.shape[0]
    high = sums.astype(BF16)
    out[row : row + count] = high
    out[row + count : row + 2 * count] = (sums - high.astype(F32)).astype(BF16)


def unpack_sums(ref, row, count):
    both = ref[row : row + 2 * count].astype(F32)
    return both[:count] + both[count:]


def block_sums(keep, got, out, row):
    deep, high, _ = keep.shape
    for z in range(deep):
        total = keep[z].astype(F32) + got[z].astype(F32)
        out[row + z * high : row + (z + 1) * high] = total.astype(BF16)


def far_b_body(keep, got, sums, sums_got, out, sum_o):
    total = sums[...] + sums_got[...]
    sum_o[...] = total
    for x in range(2):
        block_sums(keep.at[1, x], got.at[1, x], out, x * (out.shape[0] - 32) // 2)
    pack(out, out.shape[0] - 32, total)


def far_a_body(keep, got, out0, out1):
    block_sums(keep.at[0], got.at[0], out0, 0)
    block_sums(keep.at[1], got.at[1], out1, 0)


def pass_on(keep, got, far, out):
    deep, high, _ = keep.shape
    for z in range(deep):
        rows = slice(z * high, (z + 1) * high)
        total = keep[z].astype(F32) + got[z].astype(F32) + far[rows].astype(F32)
        out[rows] = total.astype(BF16)


def near_b_body(keep, got, far, sums, out, sum_o):
    count = out.shape[0] - 32
    pass_on(keep.at[0, 1], got.at[0, 1], far.at[count : 2 * count], out)
    total = sums[...] + unpack_sums(far, 2 * count, 16)
    sum_o[...] = total
    pack(out, count, total)


def near_a_body(keep, got, far, sums, sums_got, out, sum_o):
    pass_on(keep.at[1], got.at[1], far, out)
    total = sums[...] + sums_got[...]
    sum_o[...] = total
    pack(out, out.shape[0] - 16, total)


def block_total(keep, got, far, passed, z):
    rows = slice(z * keep.shape[1], (z + 1) * keep.shape[1])
    return keep[z].astype(F32) + got[z].astype(F32) + far[rows].astype(F32) + passed[rows].astype(F32)


def high_b_body(keep, got, far, passed, sums, own, out, sum_o):
    kept, given = keep.at[0, 0], got.at[0, 0]
    deep, high, _ = kept.shape
    total = sums[...] + unpack_sums(passed, deep * high, sums.shape[0])
    sum_o[...] = total
    for z in range(deep):
        value = block_total(kept, given, far, passed, z)
        if z < deep // 2:
            own[z] = value
        else:
            out[(z - deep // 2) * high : (z - deep // 2 + 1) * high] = value.astype(BF16)
    pack(out, deep // 2 * high, total)


def middle_b_body(own, got, sums, own_o, out, sum_o):
    _, high, _ = own.shape
    total = sums[...] + unpack_sums(got, 2 * high, sums.shape[0])
    sum_o[...] = total
    own_o[...] = own[0] + got[0:high].astype(F32)
    out[0:high] = (own[1] + got[high : 2 * high].astype(F32)).astype(BF16)
    pack(out, high, total)


def high_a_body(keep, got, far, passed, sums, *outs):
    kept, given = keep.at[0], got.at[0]
    deep, high, _ = kept.shape
    total = sums[...] + unpack_sums(passed, deep * high, sums.shape[0])
    outs[-1][...] = total
    for z in range(deep):
        value = block_total(kept, given, far, passed, z)
        if z == 0:
            outs[0][...] = value
        else:
            outs[z][0:high] = value.astype(BF16)
            pack(outs[z], high, total)


def last_body(info, own, sums, *refs):
    parts, (mine, theirs, sum_o) = refs[:-3], refs[-3:]
    high = own.shape[0]
    half = high // 3
    total, wide = own[...], sums[...]
    for part in parts:
        total = total + part[0:high].astype(F32)
        wide = wide + unpack_sums(part, high, sums.shape[0])
    sum_o[...] = wide
    wc = mine.shape[2]

    def give(low, upper):
        for w in range(3):
            low[w] = total[w * half : (w + 1) * half, :wc]
            upper[w] = total[w * half : (w + 1) * half, wc:]

    @pl.when(info[0] == 0)
    def _():
        give(mine, theirs)

    @pl.when(info[0] != 0)
    def _():
        give(theirs, mine)


def deliver_body(turned, info, mine, got, *outs):
    half = mine.shape[1]

    def deliver(low, high):
        for w, out in enumerate(outs):
            if turned[w]:
                out[...] = jnp.concatenate([low[w], high[w]], axis=0).T
            else:
                out[0:half] = low[w]
                out[half:] = high[w]

    @pl.when(info[0] == 0)
    def _():
        deliver(mine, got)

    @pl.when(info[0] != 0)
    def _():
        deliver(got, mine)


def join_body(info, segment_ids, own, beside, across, corner, out):
    core, y = info[0], info[1]
    length, window = out.shape[1], own.shape[0]
    gap = length - window
    cuts = cuts_of(segment_ids[...])
    own_cut = jnp.where(y == 0, cuts[0:1], cuts[1:2])
    other_cut = jnp.where(y == 0, cuts[1:2], cuts[0:1])

    def row(low, high, place, cut):
        out[place, 0:gap] = low[0:gap]
        at = (gap + lax.broadcasted_iota(jnp.int32, (window - gap, 1), 0)).astype(F32)
        seam = jnp.where(at < cut, low[gap:window].astype(F32), high[0 : window - gap].astype(F32))
        out[place, gap:window] = seam.astype(BF16)
        out[place, window:length] = high[window - gap : window]

    @pl.when(core == 0)
    def _():
        row(own, beside, y, own_cut)
        row(across, corner, 1 - y, other_cut)

    @pl.when(core != 0)
    def _():
        row(beside, own, y, own_cut)
        row(corner, across, 1 - y, other_cut)


def per_device(
    hidden_in,
    segment_ids,
    pad_flags,
    gain1,
    shift1,
    w_query,
    b_query,
    w_key,
    w_value,
    b_value,
    w_out,
    b_out,
    gain2,
    shift2,
    w_up,
    b_up,
    w_down,
    b_down,
    cotangent,
):
    fs, mp = lax.axis_size("fsdp"), lax.axis_size("mp")
    rows, length, width = hidden_in.shape
    wr, wc = w_query.shape
    half, cols = wr // 2, 2 * wc
    heads = cols // HD
    f, m = lax.axis_index("fsdp"), lax.axis_index("mp")
    core, y = m % 2, m // 2
    side = jnp.stack([core, y])
    window = length // 2 + MOST // 2
    deep = fs // 2
    flips = [2 * z for z in range(1, deep)]
    staged = half % 16 == 0 and deep == 4
    if staged:
        places = [[((z * 2 + x) * 2 + c) * half for z in range(deep)] for x in range(2) for c in range(2)]
        high, parts = half, 2
    else:
        places, high, parts = [[0]], width, 1
    wide, tall = (window, width), (width, window)
    by_heads, by_few = (heads, PAD, window), (heads // 2, PAD, window)
    weights = pltpu.VMEM((3, width, cols), BF16)

    def to(value, flip_f, flip_m):
        return send(value, fs, mp, flip_f, flip_m)

    def begin(target):
        return call(
            start_body,
            [(wide, BF16), (wide, BF16), (wide, F32), ((window, window), F32)],
            [side, hidden_in, cotangent, segment_ids, pad_flags, target],
            (),
            1,
            us=3,
            mib=4,
        )

    def project(given, blocks, first, extra=()):
        outs = [(by_heads, BF16)] * 3 + [((8, cols), F32)]
        if first:
            outs += [((8, width), F32), (wide, BF16), (tall, BF16)]
        return call(
            functools.partial(project_body, places, high, not extra, first),
            outs,
            [given] + blocks + list(extra),
            [weights],
            us=2,
            mib=4,
        )

    def attend(part, qkv_heads, bias):
        return call(
            functools.partial(forward_body, part * (heads // 2)),
            [(by_few, F32), ((heads // 2, 1, window), F32)],
            list(qkv_heads) + [bias],
            us=5,
        )

    def feed(x, mixed, small, shifts, target, blocks):
        units_shape = (window, cols)
        return call(
            functools.partial(feed_body, places, high),
            [(wide, BF16), (wide, F32), ((window, 1), F32), (wide, BF16)]
            + [(units_shape, BF16)] * 4
            + [(units_shape, F32)] * 2,
            [x] + mixed + [small] + shifts + [target] + blocks,
            [weights, weights],
            us=5,
            mib=7,
        )

    def feed_back(side, ct, made, small, target, blocks):
        if staged:
            grads = [((2, 2, deep, 3 * half, cols), BF16)] * 2
        else:
            grads = [((2, 3, width, cols), BF16)]
        return call(
            functools.partial(feed_back_body, places, high, parts),
            [(wide, F32), (by_heads, BF16), (by_heads, BF16), ((16, cols), F32)] + grads,
            [side, ct] + list(made) + [small, target] + blocks,
            [weights, weights],
            1,
            us=7,
            mib=7,
        )

    def backward(part, qkv_heads, da, o, lse, bias):
        return call(
            functools.partial(backward_body, part * (heads // 2)),
            [((heads // 2 * HD, window), BF16)] * 3,
            list(qkv_heads) + [da, o, lse, bias],
            [pltpu.VMEM(by_few, F32)] * 3,
            us=15,
        )

    def weigh(normed_t, blocks, low_a, low_b):
        if staged:
            grads = [((2, deep, 3 * half, cols), BF16)] * 2
        else:
            grads = [((3, width, cols), BF16)]
        return call(
            functools.partial(weigh_body, places, high, parts),
            [(tall, F32), ((2, cols), F32)] + grads,
            [normed_t] + list(low_a) + list(low_b) + blocks,
            [weights],
            us=0.1,
        )

    def finish(side, dn0, dn1, x, dmiddle, small, target, qv0, qv1):
        return call(
            finish_body,
            [(wide, BF16), ((8, cols), F32)],
            [side, dn0, dn1, x, dmiddle, small, target, qv0, qv1],
            (),
            1,
            us=20,
            mib=5,
        )

    def join(own, beside, across, corner):
        operands = [side, segment_ids, own, beside, across, corner]
        return call(join_body, [((rows, length, width), BF16)], operands, (), 1, us=20)[0]

    if not staged:

        def gathered(blocks):
            full = []
            for block in blocks:
                block = lax.all_gather(block, "fsdp", axis=0, tiled=True)
                full.append(lax.all_gather(block, "mp", axis=1, tiled=True))
            full = jnp.stack(full)
            return [full[:, :, yr * cols : (yr + 1) * cols].reshape(1, 3 * width, cols) for yr in range(2)]

        target = lax.iota(jnp.int32, width)[None]
        wa = gathered([w_query, w_key, w_value])
        wb = gathered([w_out.T, w_up, w_down.T])
        small = jnp.stack([gain1, shift1, b_out, gain2, shift2, b_down] + [jnp.zeros_like(gain1)] * 2)
        small = lax.all_gather(small, "fsdp", axis=1, tiled=True).astype(F32)
        units = jnp.stack([b_query, b_value, b_up] + [jnp.zeros_like(b_up)] * 5)
        units = lax.all_gather(units, "mp", axis=1, tiled=True).astype(F32)
        units = [units[:, :cols], units[:, cols:]]
        x, ct, xhat, bias = begin(target)
        *heads0, _, _, normed, normed_t = project(xhat, [wa[0]], True, (small, units[0]))
        *heads1, _ = project(normed, [wa[1]], False, (small, units[1]))
        both = (heads0, heads1)
        mixed = [attend(part, both[yr], bias) for yr in range(2) for part in range(2)]
        made = feed(x, [o for o, _ in mixed], small, units, target, wb)
        result = made[0]
        none = jnp.zeros_like(side)
        dmiddle, da0, da1, sums_b, grads_b = feed_back(none, ct, made[1:], small, target, wb)
        dn, qv, grads_a = [], [], []
        for yr, da in enumerate((da0, da1)):
            lows = [backward(part, both[yr], da, *mixed[2 * yr + part], bias) for part in range(2)]
            got = weigh(normed_t, [wa[yr]], *lows)
            dn.append(got[0])
            qv.append(got[1])
            grads_a.append(got[2])
        grad_window, sums_a = finish(none, dn[0], dn[1], x, dmiddle, small, target, *qv)

        def scattered(pair):
            full = jnp.concatenate(pair, axis=2).astype(F32)
            full = lax.psum_scatter(full, "mp", scatter_dimension=2, tiled=True)
            return lax.psum_scatter(full, "fsdp", scatter_dimension=1, tiled=True)

        grad_q, grad_k, grad_v = scattered(grads_a)
        grad_out, grad_up, grad_down = scattered([grads_b[0], grads_b[1]])
        grad_out, grad_down = grad_out.T, grad_down.T
        sums_a, sums_b = sums_a.reshape(4, width), sums_b.reshape(8, width)
        sums = jnp.concatenate([sums_a[0:2], sums_b[0:4], sums_a[2:4], sums_b[4:5]])
        sums = lax.psum(sums, BOTH)
        mine_f = lax.dynamic_slice(sums, (0, f * wr), (6, wr))
        mine_u = lax.dynamic_slice(sums, (6, m * wc), (3, wc))

        def shared(value):
            across = to(value, 0, 2)
            return join(value, to(value, 0, 1), across, to(across, 0, 1))

        out_hidden, grad_hidden = shared(result), shared(grad_window)
    else:
        piece_a, piece_b = (1, 3 * half + 16, cols), (1, 3 * half, cols)

        def stacked(pieces):
            return call(stack_body, [((deep,) + pieces[0].shape[1:], BF16)], pieces)[0]

        def part(block, of):
            return lax.dynamic_slice(block, (of * half, 0), (half, wc))

        theirs = jnp.stack([part(w, 1 - core) for w in (w_query, w_key, w_value)])
        got = to(theirs, 0, 1)
        theirs, gain1, b_query, w_query, w_key, w_value = fence(theirs, gain1, b_query, w_query, w_key, w_value)
        mine = jnp.stack([part(w, core) for w in (w_query, w_key, w_value)])
        small = jnp.stack([gain1, shift1, b_out, gain2, shift2, b_down])
        units = jnp.stack([b_query, b_value, b_up])
        units_pair = to(units, 0, 1)
        feature = lax.iota(jnp.int32, width)
        target = (((feature // half) ^ (f * 2 + core)) * half + feature % half)[None]
        got, units_pair, small, mine = fence(got, units_pair, small, mine)

        first = call(
            meet_a_body, [(piece_a, BF16)], [side, mine, got, small, units, units_pair], (), 1
        )[0]
        first_parts = [to(first, flip, 0) for flip in flips]
        first, w_out, w_up, w_down = fence(first, w_out, w_up, w_down)
        mine, theirs = call(deal_body, [((3, half, wc), BF16)] * 2, [side, w_out, w_up, w_down], (), 1)
        got = to(theirs, 0, 1)
        second = call(meet_b_body, [(piece_b, BF16)], [side, mine, got], (), 1)[0]
        first, first_parts, second, hidden_in, target = fence(first, first_parts, second, hidden_in, target)

        qkv = stacked([first] + first_parts)
        qkv_x, qkv_y = to(qkv, 1, 0), to(qkv, 0, 2)
        second_parts = [to(second, flip, 0) for flip in flips]
        x, ct, xhat, bias = begin(target)
        second_parts, second, qkv, qkv_x, qkv_y, xhat = fence(second_parts, second, qkv, qkv_x, qkv_y, xhat)
        qkv_xy = to(qkv, 1, 2)

        qkv_c, qkv_xc = to(qkv, 0, 1), to(qkv_x, 0, 1)
        odu = stacked([second] + second_parts)
        near = [qkv, qkv_c, qkv_x, qkv_xc]
        *heads0, shift0, small, normed, normed_t = project(xhat, near, True)
        heads0, qkv_y, odu = fence(heads0, qkv_y, odu)
        qkv_yc, odu_x, odu_y = to(qkv_y, 0, 1), to(odu, 1, 0), to(odu, 0, 2)
        o00, l00 = attend(0, heads0, bias)
        o00, heads0, qkv_yc, qkv_xy, odu = fence(o00, heads0, qkv_yc, qkv_xy, odu)
        qkv_xyc, odu_xy, odu_c = to(qkv_xy, 0, 1), to(odu, 1, 2), to(odu, 0, 1)
        o01, l01 = attend(1, heads0, bias)
        o01, qkv_xyc, odu_c, normed = fence(o01, qkv_xyc, odu_c, normed)
        far = [qkv_y, qkv_yc, qkv_xy, qkv_xyc]
        *heads1, shift1u = project(normed, far, False)
        o10, l10 = attend(0, heads1, bias)
        o10, heads1, odu_x, odu_y = fence(o10, heads1, odu_x, odu_y)
        odu_xc, odu_yc = to(odu_x, 0, 1), to(odu_y, 0, 1)
        o11, l11 = attend(1, heads1, bias)
        o11, odu_xc, odu_yc, odu_xy = fence(o11, odu_xc, odu_yc, odu_xy)
        odu_xyc = to(odu_xy, 0, 1)

        odu_blocks = [odu, odu_c, odu_x, odu_xc, odu_y, odu_yc, odu_xy, odu_xyc]
        made = fence(*feed(x, [o00, o01, o10, o11], small, [shift0, shift1u], target, odu_blocks))
        result = made[0]
        res_c, res_y = to(result, 0, 1), to(result, 0, 2)
        made = feed_back(side, ct, made[1:], small, target, odu_blocks)
        dmiddle, da0, da1, b_sums, b_keep, b_send, res_c = fence(*made, res_c)

        n_far, n_near = 2 * deep * 3 * half, deep * 3 * half
        f32_16, f32_8 = ((16, cols), F32), ((8, cols), F32)
        b_got, b_sums_got = to(b_send, 0, 1), to(b_sums, 0, 1)
        low10 = backward(0, heads1, da1, o10, l10, bias)
        low10, heads1, b_got, b_sums_got = fence(low10, heads1, b_got, b_sums_got)
        b_far, b_sums = call(
            far_b_body,
            [((n_far + 32, cols), BF16), f32_16],
            [b_keep, b_got, b_sums, b_sums_got],
        )
        b_far = to(b_far, 0, 2)
        low11 = backward(1, heads1, da1, o11, l11, bias)
        low11, normed_t = fence(low11, normed_t)
        dn1, qv1, keep1, send1 = weigh(normed_t, far, low10, low11)
        dn1, keep1, send1, da0, res_y = fence(dn1, keep1, send1, da0, res_y)
        got1, res_yc = to(send1, 0, 1), to(res_y, 0, 1)
        low00 = backward(0, heads0, da0, o00, l00, bias)
        low00, heads0, got1, res_yc = fence(low00, heads0, got1, res_yc)
        a_far0, a_far1 = call(far_a_body, [((n_near, cols), BF16)] * 2, [keep1, got1])
        a_far0, a_far1, heads0 = fence(a_far0, a_far1, heads0)
        a_far1, a_far0 = to(a_far1, 0, 2), to(a_far0, 0, 2)
        low01 = backward(1, heads0, da0, o01, l01, bias)
        low01, normed_t, b_far = fence(low01, normed_t, b_far)
        b_x, b_sums = call(
            near_b_body, [((n_near + 32, cols), BF16), f32_16], [b_keep, b_got, b_far, b_sums]
        )
        b_x = to(b_x, 1, 0)
        dn0, qv0, keep0, send0 = weigh(normed_t, near, low00, low01)
        dn0, keep0, send0, dmiddle = fence(dn0, keep0, send0, dmiddle)
        got0 = to(send0, 0, 1)
        n_two = 2 * 3 * half
        grad_window, a_sums = finish(side, dn0, dn1, x, dmiddle, small, target, qv0, qv1)
        grad_window, a_sums, got0, a_far1, b_x = fence(grad_window, a_sums, got0, a_far1, b_x)

        gw_y, gw_c, a_sums_got = to(grad_window, 0, 2), to(grad_window, 0, 1), to(a_sums, 0, 1)
        a_sums_got, gw_c, keep0 = fence(a_sums_got, gw_c, keep0)
        a_x, a_sums = call(
            near_a_body, [((n_near + 16, cols), BF16), f32_8], [keep0, got0, a_far1, a_sums, a_sums_got]
        )
        a_x, b_keep = fence(a_x, b_keep)
        a_x = to(a_x, 1, 0)
        b_own, b_z2, b_sums = call(
            high_b_body,
            [((2, 3 * half, cols), F32), ((n_two + 32, cols), BF16), f32_16],
            [b_keep, b_got, b_far, b_x, b_sums],
        )
        b_z2, result = fence(b_z2, result)
        b_z2 = to(b_z2, 4, 0)
        out_hidden = join(result, res_c, res_y, res_yc)
        b_z2, out_hidden = fence(b_z2, out_hidden)

        def last(own, sums, got, kind):
            return call(last_body, [((3, half, wc), F32)] * 2 + [kind], [side, own, sums] + got, (), 1, us=20)

        def deliver(mine, got, turned):
            shapes = [((wc, wr) if t else (wr, wc), F32) for t in turned]
            return call(functools.partial(deliver_body, turned), shapes, [side, mine, got], (), 1)

        b_own, b_z1, b_sums = call(
            middle_b_body,
            [((3 * half, cols), F32), ((3 * half + 32, cols), BF16), f32_16],
            [b_own, b_z2, b_sums],
            us=20,
        )
        b_z1, a_x, a_far0, keep0 = fence(b_z1, a_x, a_far0, keep0)
        a_split = call(
            high_a_body,
            [((3 * half, cols), F32)] + [((3 * half + 16, cols), BF16)] * (deep - 1) + [f32_8],
            [keep0, got0, a_far0, a_x, a_sums],
        )
        a_split, b_z1, b_own = fence(a_split, b_z1, b_own)
        a_high = [to(part, flip, 0) for part, flip in zip(a_split[1:-1], flips)]
        b_z1 = to(b_z1, 2, 0)
        b_z1, gw_y = fence(b_z1, gw_y)
        b_mine, b_theirs, b_sums = last(b_own, b_sums, [b_z1], f32_16)
        b_last, gw_yc = to(b_theirs, 0, 1), to(gw_y, 0, 1)
        grad_hidden = join(grad_window, gw_c, gw_y, gw_yc)
        b_last, grad_hidden = fence(b_last, grad_hidden)
        grad_out, grad_up, grad_down = deliver(b_mine, b_last, (True, False, True))
        a_own, a_high, grad_out, grad_hidden = fence(a_split[0], a_high, grad_out, grad_hidden)
        a_mine, a_theirs, a_sums = last(a_own, a_split[-1], a_high, f32_8)
        a_last = to(a_theirs, 0, 1)
        a_sums = a_sums + to(a_sums, 0, 2)
        grad_q, grad_k, grad_v = deliver(a_mine, a_last, (False, False, False))
        sums = jnp.concatenate(
            [
                a_sums.reshape(4, width)[0:2],
                b_sums.reshape(8, width)[0:4],
                a_sums.reshape(4, width)[2:4],
                b_sums.reshape(8, width)[4:5],
            ]
        )
        mine_f = lax.dynamic_slice(sums, (0, f * wr), (6, wr))
        mine_u = lax.dynamic_slice(sums, (6, m * wc), (3, wc))
    return (
        out_hidden,
        grad_hidden,
        mine_f[0],
        mine_f[1],
        grad_q,
        mine_u[0],
        grad_k,
        grad_v,
        mine_u[1],
        grad_out,
        mine_f[2],
        mine_f[3],
        mine_f[4],
        grad_up,
        mine_u[2],
        grad_down,
        mine_f[5],
    )


def solution(mesh):
    return jax.shard_map(
        per_device,
        mesh=mesh,
        in_specs=(
            P("fsdp", None, None),
            P("fsdp", None),
            P("fsdp", None),
            P("fsdp"),
            P("fsdp"),
            P("fsdp", "mp"),
            P("mp"),
            P("fsdp", "mp"),
            P("fsdp", "mp"),
            P("mp"),
            P("mp", "fsdp"),
            P("fsdp"),
            P("fsdp"),
            P("fsdp"),
            P("fsdp", "mp"),
            P("mp"),
            P("mp", "fsdp"),
            P("fsdp"),
            P("fsdp", None, None),
        ),
        out_specs=(
            P("fsdp", None, None),
            P("fsdp", None, None),
            P("fsdp"),
            P("fsdp"),
            P("fsdp", "mp"),
            P("mp"),
            P("fsdp", "mp"),
            P("fsdp", "mp"),
            P("mp"),
            P("mp", "fsdp"),
            P("fsdp"),
            P("fsdp"),
            P("fsdp"),
            P("fsdp", "mp"),
            P("mp"),
            P("mp", "fsdp"),
            P("fsdp"),
        ),
        check_vma=False,
    )
```

```python
import functools
import math

import jax
import jax.numpy as jnp
from jax import lax
from jax.experimental import pallas as pl
from jax.experimental.pallas import tpu as pltpu
from jax.sharding import PartitionSpec as P

HD = 24
PAD = 32
MOST = 128
BOTH = ("fsdp", "mp")
EPS = 1e-05
F32 = jnp.float32
BF16 = jnp.bfloat16
LOG2 = math.log2(math.e) / math.sqrt(HD)
SCALE = 1.0 / math.sqrt(HD)
GELU = math.sqrt(2.0 / math.pi)


def send(value, fs, mp, flip_f, flip_m):
    pairs = [(f * mp + m, (f ^ flip_f) * mp + (m ^ flip_m)) for f in range(fs) for m in range(mp)]
    return lax.ppermute(value, BOTH, pairs)


def dot_nn(left, right):
    return lax.dot_general(left, right, (((1,), (0,)), ((), ())), preferred_element_type=F32)


def dot_nt(left, right):
    return lax.dot_general(left, right, (((1,), (1,)), ((), ())), preferred_element_type=F32)


def dot_tn(left, right):
    return lax.dot_general(left, right, (((0,), (0,)), ((), ())), preferred_element_type=F32)


def norm_parts(values):
    centre = jnp.mean(values, axis=-1, keepdims=True)
    centered = values - centre
    inverse = lax.rsqrt(jnp.mean(centered * centered, axis=-1, keepdims=True) + EPS)
    return centered * inverse, inverse


def norm_back(grad, normed, inverse, gain):
    scaled = grad * gain
    return inverse * (
        scaled
        - jnp.mean(scaled, axis=-1, keepdims=True)
        - normed * jnp.mean(scaled * normed, axis=-1, keepdims=True)
    )


def call(body, outs, operands, scratch=(), scalars=0, us=0.1, mib=6):
    whole = pl.BlockSpec(memory_space=pltpu.VMEM)
    few = pl.BlockSpec(memory_space=pltpu.SMEM)
    return pl.pallas_call(
        body,
        out_shape=tuple(jax.ShapeDtypeStruct(s, d) for s, d in outs),
        in_specs=[few] * scalars + [whole] * (len(operands) - scalars),
        out_specs=tuple(whole for _ in outs),
        scratch_shapes=list(scratch),
        name=getattr(body, "func", body).__name__,
        compiler_params=pltpu.CompilerParams(vmem_limit_bytes=mib << 20),
        cost_estimate=pl.CostEstimate(
            flops=int(us * 2e9), transcendentals=0, bytes_accessed=int(us * 3e6)
        ),
    )(*operands)


def fence(*values):
    return lax.optimization_barrier(values)


def tiles(window):
    made = []
    for q0 in range(0, window, 256):
        qn = min(256, window - q0)
        k0 = max(0, q0 - MOST)
        made.append((q0, qn, k0, min(window, q0 + qn + MOST)))
    return made


def permutation(target):
    width = target.shape[1]
    return (lax.broadcasted_iota(jnp.int32, (width, width), 0) == target).astype(BF16)


def cuts_of(segments):
    middle = segments.shape[1] // 2
    held = segments[:, middle : middle + 1]
    first = jnp.sum((segments < held).astype(F32), axis=1, keepdims=True)
    last = jnp.sum((segments <= held).astype(F32), axis=1, keepdims=True)
    return jnp.where(middle - first <= last - middle, first, last)


def start_body(info, hidden, cotangent, segment_ids, pad_flags, target, x_o, c_o, xhat_o, bias_o):
    core, y = info[0], info[1]
    window = x_o.shape[0]
    gap = hidden.shape[1] - window
    start = pl.multiple_of(core * gap, 16)
    segments = segment_ids[...]
    cuts = cuts_of(segments)
    cut = jnp.where(y == 0, cuts[0:1], cuts[1:2])
    here = (start + lax.broadcasted_iota(jnp.int32, (window, 1), 0)).astype(F32)
    before = (here < cut).astype(F32)
    owned = jnp.where(core == 0, before, 1.0 - before)
    perm = permutation(target[...])
    x = dot_nn(hidden[y, pl.ds(start, window), :], perm)
    x_o[...] = x.astype(BF16)
    c_o[...] = (dot_nn(cotangent[y, pl.ds(start, window), :], perm) * owned).astype(BF16)
    xhat_o[...] = norm_parts(x)[0]
    segs = jnp.where(y == 0, segments[0:1], segments[1:2]).astype(F32)
    pads = pad_flags[...]
    pads = jnp.where(y == 0, pads[0:1], pads[1:2])
    code = jnp.where(pads == 0, segs, -1.0)
    segs = jnp.where(core == 0, segs[:, :window], segs[:, gap:])
    wide = bias_o.shape[1]
    if wide > window:
        segs = jnp.concatenate([segs, jnp.full((1, wide - window), -2.0, F32)], axis=1)
    code = jnp.where(core == 0, code[:, :window], code[:, gap:])
    column = jnp.broadcast_to(code, (8, window)).T[:, 0:1]
    key = lax.broadcasted_iota(jnp.int32, (window, wide), 0)
    query = lax.broadcasted_iota(jnp.int32, (window, wide), 1)
    bias_o[...] = jnp.where((column == segs) | (key == query), 0.0, -1e30)


def assemble(blocks, places, high, weights):
    for block, rows in zip(blocks, places):
        for z, row in enumerate(rows):
            for w in range(3):
                weights[w, row : row + high] = block[z, w * high : (w + 1) * high]


def disassemble(value, outs, pick):
    value = value.astype(BF16)
    if len(outs) == 1:
        outs[0][pick] = value
        return
    _, deep, high, _ = outs[0].shape[-4:]
    half = high // 3
    yr, w = pick[:-1], pick[-1]
    for x in range(2):
        for z in range(deep):
            for c in range(2):
                at = ((z * 2 + x) * 2 + c) * half
                outs[c][yr + (x, z, pl.ds(w * half, half))] = value[at : at + half]


def common_order(rows, perm):
    high = rows.astype(BF16)
    rest = rows - high.astype(F32)
    mid = rest.astype(BF16)
    last = (rest - mid.astype(F32)).astype(BF16)
    return dot_nn(high, perm) + dot_nn(mid, perm) + dot_nn(last, perm)


def by_head(value, fill=0.0):
    tokens, columns = value.shape
    parts = value.T.reshape(columns // HD, HD, tokens)
    row = lax.broadcasted_iota(jnp.int32, (columns // HD, PAD - HD, tokens), 1)
    extra = jnp.where(row == 0, fill, 0.0)
    return jnp.concatenate([parts, extra], axis=1).astype(BF16)


def flat_heads(value):
    heads, _, tokens = value.shape
    return value[:, :HD, :].reshape(heads * HD, tokens)


def project_body(places, high, unpack, first, given, *refs):
    blocks = refs[: len(places)]
    refs = refs[len(places) :]
    if not unpack:
        small_i, shift_i = refs[:2]
        refs = refs[2:]
    qt, kt, vt, shift_o = refs[:4]
    weights = refs[-1]
    assemble(blocks, places, high, weights)
    if unpack:
        shifts = blocks[0][0, 3 * high : 3 * high + 16].astype(F32)[0:8]
    else:
        shifts = shift_i[...]
    shift_o[...] = shifts
    if first:
        small_o, n_o, nt_o = refs[4:7]
        if unpack:
            deep = blocks[0].shape[0]
            wide = blocks[0].shape[2] // 4
            rows = [
                [blocks[2 * x][z, 3 * high : 3 * high + 16].astype(F32) for x in range(2)]
                for z in range(deep)
            ]
            made = []
            for p in range(6):
                r, at = 8 + p // 4, p % 4 * wide
                made.append(
                    jnp.concatenate(
                        [rows[z][x][r : r + 1, at : at + wide] for z in range(deep) for x in range(2)],
                        axis=1,
                    )
                )
            made += [jnp.zeros_like(made[0])] * 2
            small = jnp.concatenate(made, axis=0)
        else:
            small = small_i[...]
        small_o[...] = small
        exact = given[...] * small[0:1] + small[1:2]
        normed = exact.astype(BF16)
        n_o[...] = normed
        nt_o[...] = exact.T.astype(BF16)
    else:
        normed = given[...]
    qt[...] = by_head(dot_nn(normed, weights[0]) + shifts[0:1])
    kt[...] = by_head(dot_nn(normed, weights[1]))
    vt[...] = by_head(dot_nn(normed, weights[2]) + shifts[1:2], 1.0)


def forward_body(first, qt, kt, vt, bias, ot, lse):
    heads, _, window = ot.shape
    rows = 4 * PAD

    def four(i, carry):
        h = first + 4 * i
        for q0, qn, k0, k1 in tiles(window):
            query = qt[pl.ds(h, 4), :, q0 : q0 + qn].reshape(rows, qn).astype(F32)
            if qn < 256:
                query = jnp.concatenate([query, jnp.zeros((rows, 256 - qn), F32)], axis=1)
            own = lax.broadcasted_iota(jnp.int32, (rows, 256), 0) // PAD
            block = [jnp.where(own == n, query, 0.0).astype(BF16) for n in range(4)]
            keys = kt[pl.ds(h, 4), :, k0:k1].reshape(rows, k1 - k0)
            values = vt[pl.ds(h, 4), :, k0:k1].reshape(rows, k1 - k0)
            scores = dot_tn(keys, jnp.concatenate(block, axis=1))
            tops, weights = [], []
            for n in range(4):
                part = scores[:, n * 256 : (n + 1) * 256] * LOG2 + bias[k0:k1, q0 : q0 + 256]
                top = jnp.max(part, axis=0, keepdims=True)
                tops.append(top)
                weights.append(jnp.exp2(part - top).astype(BF16))
            mixed = dot_nn(values, jnp.concatenate(weights, axis=1))
            for n in range(4):
                own_mixed = mixed[n * PAD : (n + 1) * PAD, n * 256 : n * 256 + qn]
                total = own_mixed[HD : HD + 1]
                ot[4 * i + n, :, q0 : q0 + qn] = own_mixed / total
                lse[4 * i + n, :, q0 : q0 + qn] = tops[n][:, :qn] + jnp.log2(total)
        return carry

    lax.fori_loop(0, heads // 4, four, 0)


def feed_body(places, high, x_r, o00, o01, o10, o11, small, cols0, cols1, target, *refs):
    count = len(places)
    blocks = refs[: 2 * count]
    refs = refs[2 * count :]
    out_o, xhat_o, inv_o, n_o = refs[:4]
    atts, acts, slopes, weights = refs[4:6], refs[6:8], refs[8:10], refs[10:]
    for yr in range(2):
        assemble(blocks[yr * count : (yr + 1) * count], places, high, weights[yr])
    for out, a, b in zip(atts, (o00, o10), (o01, o11)):
        out[...] = jnp.concatenate([flat_heads(a[...]), flat_heads(b[...])], axis=0).T.astype(BF16)
    x = x_r[...].astype(F32)
    middle = x + dot_nt(atts[0][...], weights[0][0]) + dot_nt(atts[1][...], weights[1][0]) + small[2:3]
    xhat, inverse = norm_parts(middle)
    xhat_o[...] = xhat
    inv_o[...] = inverse
    normed = (xhat * small[3:4] + small[4:5]).astype(BF16)
    n_o[...] = normed
    result = middle + small[5:6]
    for yr, cols in enumerate((cols0, cols1)):
        pre = dot_nn(normed, weights[yr][1]) + cols[2:3]
        square = pre * pre
        bent = jnp.tanh(GELU * (pre + 0.044715 * (pre * square)))
        act = (0.5 * pre * (1.0 + bent)).astype(BF16)
        acts[yr][...] = act
        slopes[yr][...] = 0.5 * (1.0 + bent) + 0.5 * pre * (1.0 - bent * bent) * (
            GELU * (1.0 + 3.0 * 0.044715 * square)
        )
        result = result + dot_nt(act, weights[yr][2])
    out_o[...] = dot_nn(result.astype(BF16), permutation(target[...])).astype(BF16)


def rows_of(info, feats, units):
    width = feats.shape[1]
    cols = width // 2
    made = []
    for i in range(feats.shape[0]):
        made += [feats[i : i + 1, :cols], feats[i : i + 1, cols:]]
    for own, other in units:
        made += [jnp.where(info[1] == 0, own, other), jnp.where(info[1] == 0, other, own)]
    return jnp.concatenate(made, axis=0)


def feed_back_body(places, high, parts, info, c_r, xhat_r, inv_r, n_r, a0, a1, act0, act1, slope0, slope1, small, target, *refs):
    count = len(places)
    blocks = refs[: 2 * count]
    refs = refs[2 * count :]
    mid_o, d0, d1, sum_o = refs[:4]
    outs = refs[4 : 4 + parts]
    weights = refs[4 + parts :]
    for yr in range(2):
        assemble(blocks[yr * count : (yr + 1) * count], places, high, weights[yr])
    ct_low, normed = c_r[...], n_r[...]
    cols = act0.shape[1]

    def both(left, right, w):
        grads = dot_tn(left, jnp.concatenate(right, axis=1))
        for yr in range(2):
            disassemble(grads[:, yr * cols : (yr + 1) * cols], outs, (yr, w))

    both(ct_low, [act0[...], act1[...]], 2)
    dpres = [
        (dot_nn(ct_low, weights[yr][2]) * slope[...]).astype(BF16) for yr, slope in enumerate((slope0, slope1))
    ]
    both(normed, dpres, 1)
    ups = [jnp.sum(dpre.astype(F32), axis=0, keepdims=True) for dpre in dpres]
    dnorm = dot_nt(dpres[0], weights[0][1]) + dot_nt(dpres[1], weights[1][1])
    ct, xhat = ct_low.astype(F32), xhat_r[...]
    dmiddle = ct + norm_back(dnorm, xhat, inv_r[...], small[3:4])
    mid_o[...] = dmiddle
    sums = [jnp.sum(part, axis=0, keepdims=True) for part in (dmiddle, dnorm * xhat, dnorm, ct)]
    sums = common_order(
        jnp.concatenate(sums + [jnp.zeros((4, dnorm.shape[1]), F32)], axis=0), permutation(target[...])
    )
    sums = rows_of(info, sums[0:4], [ups])
    sum_o[...] = jnp.concatenate([sums, jnp.zeros_like(sums[0:6])], axis=0)
    low = dmiddle.astype(BF16)
    both(low, [a0[...], a1[...]], 0)
    for yr in range(2):
        (d0, d1)[yr][...] = by_head(dot_nn(low, weights[yr][0]))


def backward_body(first, qt, kt, vt, dt, ot, lse, bias, dq_o, dk_o, dv_o, dq, dk, dv):
    heads, _, window = ot.shape
    made = tiles(window)

    def head(i, carry):
        h = first + i
        delta = jnp.sum(dt[h].astype(F32) * ot[i], axis=0, keepdims=True)
        for ref in (dk, dv):
            ref[i] = jnp.zeros_like(ref[i])
        for q0, qn, k0, k1 in made:
            query, grad = qt[h, :, q0 : q0 + qn], dt[h, :, q0 : q0 + qn]
            scores = dot_tn(kt[h, :, k0:k1], query)
            dprobs = dot_tn(vt[h, :, k0:k1], grad)
            probs = jnp.exp2(scores * LOG2 + (bias[k0:k1, q0 : q0 + qn] - lse[i, :, q0 : q0 + qn]))
            dscores = (probs * (dprobs - delta[:, q0 : q0 + qn])).astype(BF16)
            dq[i, :, q0 : q0 + qn] = dot_nn(kt[h, :, k0:k1], dscores)
            dk[i, :, k0:k1] += dot_nt(query, dscores)
            dv[i, :, k0:k1] += dot_nt(grad, probs.astype(BF16))
        return carry

    lax.fori_loop(0, heads, head, 0, unroll=1)
    for ref, out, factor in ((dq, dq_o, SCALE), (dk, dk_o, SCALE), (dv, dv_o, 1.0)):
        out[...] = (flat_heads(ref[...]) * factor).astype(BF16)


def weigh_body(places, high, parts, nt_r, qa, ka, va, qb, kb, vb, *refs):
    blocks = refs[: len(places)]
    refs = refs[len(places) :]
    dn, sums = refs[:2]
    outs = refs[2 : 2 + parts]
    weights = refs[2 + parts]
    assemble(blocks, places, high, weights)
    normed = nt_r[...]
    ones = jnp.ones((8, normed.shape[1]), BF16)
    total = None
    for w, (a, b) in enumerate(((qa, qb), (ka, kb), (va, vb))):
        low = jnp.concatenate([a[...], b[...]], axis=0)
        disassemble(dot_nt(normed, low), outs, (w,))
        part = dot_nn(weights[w], low)
        total = part if total is None else total + part
        if w != 1:
            sums[w // 2 : w // 2 + 1] = dot_nt(ones, low)[0:1]
    dn[...] = total


def finish_body(info, dn0, dn1, x_r, mid, small, target, qv0, qv1, out_o, sum_o):
    perm = permutation(target[...])
    grad = (dn0[...] + dn1[...]).T
    xhat, inverse = norm_parts(x_r[...].astype(F32))
    dx = mid[...] + norm_back(grad, xhat, inverse, small[0:1])
    out_o[...] = dot_nn(dx.astype(BF16), perm).astype(BF16)
    sums = [jnp.sum(part, axis=0, keepdims=True) for part in (grad * xhat, grad)]
    sums = common_order(jnp.concatenate(sums + [jnp.zeros((6, grad.shape[1]), F32)], axis=0), perm)
    sum_o[...] = rows_of(info, sums[0:2], [(qv0[w : w + 1], qv1[w : w + 1]) for w in range(2)])


def deal_body(info, wo, wu, wd, mine, theirs):
    half = mine.shape[1]
    values = [wo[...].astype(F32).T.astype(BF16), wu[...], wd[...].astype(F32).T.astype(BF16)]

    @pl.when(info[0] == 0)
    def _():
        for w, value in enumerate(values):
            mine[w], theirs[w] = value[:half], value[half:]

    @pl.when(info[0] != 0)
    def _():
        for w, value in enumerate(values):
            theirs[w], mine[w] = value[:half], value[half:]


def meet_a_body(info, mine, got, small, units, units_pair, first):
    half = got.shape[1]
    wr, wc = small.shape[1], units.shape[1]
    zeros = jnp.zeros((8, 4 * wr), F32)

    def meet(own_first):
        def pair(own, other):
            return jnp.concatenate([own, other] if own_first else [other, own], axis=1)

        for w in range(3):
            first[0, w * half : (w + 1) * half, :] = pair(mine[w], got[w])
        params = small[...].astype(F32)
        if not own_first:
            params = jnp.concatenate([params[:, half:], params[:, :half]], axis=1)
        above = jnp.concatenate([params[p : p + 1] for p in range(4)], axis=1)
        below = jnp.concatenate([params[4:5], params[5:6], zeros[0:1, : 2 * wr]], axis=1)
        both = pair(units[...], units_pair[...]).astype(F32)
        extra = jnp.concatenate([both, zeros[:5], above, below, zeros[:6]], axis=0)
        first[0, 3 * half : 3 * half + 16, :] = extra.astype(BF16)

    @pl.when(info[0] == 0)
    def _():
        meet(True)

    @pl.when(info[0] != 0)
    def _():
        meet(False)


def meet_b_body(info, mine, got, second):
    half = got.shape[1]

    def meet(low, high):
        for w in range(3):
            second[0, w * half : (w + 1) * half, :] = jnp.concatenate([low[w], high[w]], axis=1)

    @pl.when(info[0] == 0)
    def _():
        meet(mine, got)

    @pl.when(info[0] != 0)
    def _():
        meet(got, mine)


def stack_body(*refs):
    out = refs[-1]
    for at, ref in enumerate(refs[:-1]):
        out[at] = ref[0]


def pack(out, row, sums):
    count = sums.shape[0]
    high = sums.astype(BF16)
    out[row : row + count] = high
    out[row + count : row + 2 * count] = (sums - high.astype(F32)).astype(BF16)


def unpack_sums(ref, row, count):
    both = ref[row : row + 2 * count].astype(F32)
    return both[:count] + both[count:]


def block_sums(keep, got, out, row):
    deep, high, _ = keep.shape
    for z in range(deep):
        total = keep[z].astype(F32) + got[z].astype(F32)
        out[row + z * high : row + (z + 1) * high] = total.astype(BF16)


def far_b_body(keep, got, sums, sums_got, out, sum_o):
    total = sums[...] + sums_got[...]
    sum_o[...] = total
    for x in range(2):
        block_sums(keep.at[1, x], got.at[1, x], out, x * (out.shape[0] - 32) // 2)
    pack(out, out.shape[0] - 32, total)


def far_a_body(keep, got, out0, out1):
    block_sums(keep.at[0], got.at[0], out0, 0)
    block_sums(keep.at[1], got.at[1], out1, 0)


def pass_on(keep, got, far, out):
    deep, high, _ = keep.shape
    for z in range(deep):
        rows = slice(z * high, (z + 1) * high)
        total = keep[z].astype(F32) + got[z].astype(F32) + far[rows].astype(F32)
        out[rows] = total.astype(BF16)


def near_b_body(keep, got, far, sums, out, sum_o):
    count = out.shape[0] - 32
    pass_on(keep.at[0, 1], got.at[0, 1], far.at[count : 2 * count], out)
    total = sums[...] + unpack_sums(far, 2 * count, 16)
    sum_o[...] = total
    pack(out, count, total)


def near_a_body(keep, got, far, sums, sums_got, out, sum_o):
    pass_on(keep.at[1], got.at[1], far, out)
    total = sums[...] + sums_got[...]
    sum_o[...] = total
    pack(out, out.shape[0] - 16, total)


def block_total(keep, got, far, passed, z):
    rows = slice(z * keep.shape[1], (z + 1) * keep.shape[1])
    return keep[z].astype(F32) + got[z].astype(F32) + far[rows].astype(F32) + passed[rows].astype(F32)


def high_b_body(keep, got, far, passed, sums, own, out, sum_o):
    kept, given = keep.at[0, 0], got.at[0, 0]
    deep, high, _ = kept.shape
    total = sums[...] + unpack_sums(passed, deep * high, sums.shape[0])
    sum_o[...] = total
    for z in range(deep):
        value = block_total(kept, given, far, passed, z)
        if z < deep // 2:
            own[z] = value
        else:
            out[(z - deep // 2) * high : (z - deep // 2 + 1) * high] = value.astype(BF16)
    pack(out, deep // 2 * high, total)


def middle_b_body(own, got, sums, own_o, out, sum_o):
    _, high, _ = own.shape
    total = sums[...] + unpack_sums(got, 2 * high, sums.shape[0])
    sum_o[...] = total
    own_o[...] = own[0] + got[0:high].astype(F32)
    out[0:high] = (own[1] + got[high : 2 * high].astype(F32)).astype(BF16)
    pack(out, high, total)


def high_a_body(keep, got, far, passed, sums, *outs):
    kept, given = keep.at[0], got.at[0]
    deep, high, _ = kept.shape
    total = sums[...] + unpack_sums(passed, deep * high, sums.shape[0])
    outs[-1][...] = total
    for z in range(deep):
        value = block_total(kept, given, far, passed, z)
        if z == 0:
            outs[0][...] = value
        else:
            outs[z][0:high] = value.astype(BF16)
            pack(outs[z], high, total)


def last_body(info, own, sums, *refs):
    parts, (mine, theirs, sum_o) = refs[:-3], refs[-3:]
    high = own.shape[0]
    half = high // 3
    total, wide = own[...], sums[...]
    for part in parts:
        total = total + part[0:high].astype(F32)
        wide = wide + unpack_sums(part, high, sums.shape[0])
    sum_o[...] = wide
    wc = mine.shape[2]

    def give(low, upper):
        for w in range(3):
            low[w] = total[w * half : (w + 1) * half, :wc]
            upper[w] = total[w * half : (w + 1) * half, wc:]

    @pl.when(info[0] == 0)
    def _():
        give(mine, theirs)

    @pl.when(info[0] != 0)
    def _():
        give(theirs, mine)


def deliver_body(turned, info, mine, got, *outs):
    half = mine.shape[1]

    def deliver(low, high):
        for w, out in enumerate(outs):
            if turned[w]:
                out[...] = jnp.concatenate([low[w], high[w]], axis=0).T
            else:
                out[0:half] = low[w]
                out[half:] = high[w]

    @pl.when(info[0] == 0)
    def _():
        deliver(mine, got)

    @pl.when(info[0] != 0)
    def _():
        deliver(got, mine)


def join_body(info, segment_ids, own, beside, across, corner, out):
    core, y = info[0], info[1]
    length, window = out.shape[1], own.shape[0]
    gap = length - window
    cuts = cuts_of(segment_ids[...])
    own_cut = jnp.where(y == 0, cuts[0:1], cuts[1:2])
    other_cut = jnp.where(y == 0, cuts[1:2], cuts[0:1])

    def row(low, high, place, cut):
        out[place, 0:gap] = low[0:gap]
        at = (gap + lax.broadcasted_iota(jnp.int32, (window - gap, 1), 0)).astype(F32)
        seam = jnp.where(at < cut, low[gap:window].astype(F32), high[0 : window - gap].astype(F32))
        out[place, gap:window] = seam.astype(BF16)
        out[place, window:length] = high[window - gap : window]

    @pl.when(core == 0)
    def _():
        row(own, beside, y, own_cut)
        row(across, corner, 1 - y, other_cut)

    @pl.when(core != 0)
    def _():
        row(beside, own, y, own_cut)
        row(corner, across, 1 - y, other_cut)


def per_device(
    hidden_in,
    segment_ids,
    pad_flags,
    gain1,
    shift1,
    w_query,
    b_query,
    w_key,
    w_value,
    b_value,
    w_out,
    b_out,
    gain2,
    shift2,
    w_up,
    b_up,
    w_down,
    b_down,
    cotangent,
):
    fs, mp = lax.axis_size("fsdp"), lax.axis_size("mp")
    rows, length, width = hidden_in.shape
    wr, wc = w_query.shape
    half, cols = wr // 2, 2 * wc
    heads = cols // HD
    f, m = lax.axis_index("fsdp"), lax.axis_index("mp")
    core, y = m % 2, m // 2
    side = jnp.stack([core, y])
    window = length // 2 + MOST // 2
    deep = fs // 2
    flips = [2 * z for z in range(1, deep)]
    staged = half % 16 == 0 and deep == 4
    if staged:
        places = [[((z * 2 + x) * 2 + c) * half for z in range(deep)] for x in range(2) for c in range(2)]
        high, parts = half, 2
    else:
        places, high, parts = [[0]], width, 1
    wide, tall = (window, width), (width, window)
    by_heads, by_few = (heads, PAD, window), (heads // 2, PAD, window)
    weights = pltpu.VMEM((3, width, cols), BF16)

    def to(value, flip_f, flip_m):
        return send(value, fs, mp, flip_f, flip_m)

    def begin(target):
        return call(
            start_body,
            [(wide, BF16), (wide, BF16), (wide, F32), ((window, -(-window // 256) * 256), F32)],
            [side, hidden_in, cotangent, segment_ids, pad_flags, target],
            (),
            1,
            us=3,
            mib=4,
        )

    def project(given, blocks, first, extra=()):
        outs = [(by_heads, BF16)] * 3 + [((8, cols), F32)]
        if first:
            outs += [((8, width), F32), (wide, BF16), (tall, BF16)]
        return call(
            functools.partial(project_body, places, high, not extra, first),
            outs,
            [given] + blocks + list(extra),
            [weights],
            us=2,
            mib=4,
        )

    def attend(part, qkv_heads, bias):
        return call(
            functools.partial(forward_body, part * (heads // 2)),
            [(by_few, F32), ((heads // 2, 1, window), F32)],
            list(qkv_heads) + [bias],
            us=5,
        )

    def feed(x, mixed, small, shifts, target, blocks):
        units_shape = (window, cols)
        return call(
            functools.partial(feed_body, places, high),
            [(wide, BF16), (wide, F32), ((window, 1), F32), (wide, BF16)]
            + [(units_shape, BF16)] * 4
            + [(units_shape, F32)] * 2,
            [x] + mixed + [small] + shifts + [target] + blocks,
            [weights, weights],
            us=5,
            mib=7,
        )

    def feed_back(side, ct, made, small, target, blocks):
        if staged:
            grads = [((2, 2, deep, 3 * half, cols), BF16)] * 2
        else:
            grads = [((2, 3, width, cols), BF16)]
        return call(
            functools.partial(feed_back_body, places, high, parts),
            [(wide, F32), (by_heads, BF16), (by_heads, BF16), ((16, cols), F32)] + grads,
            [side, ct] + list(made) + [small, target] + blocks,
            [weights, weights],
            1,
            us=7,
            mib=10,
        )

    def backward(part, qkv_heads, da, o, lse, bias):
        return call(
            functools.partial(backward_body, part * (heads // 2)),
            [((heads // 2 * HD, window), BF16)] * 3,
            list(qkv_heads) + [da, o, lse, bias],
            [pltpu.VMEM(by_few, F32)] * 3,
            us=15,
        )

    def weigh(normed_t, blocks, low_a, low_b):
        if staged:
            grads = [((2, deep, 3 * half, cols), BF16)] * 2
        else:
            grads = [((3, width, cols), BF16)]
        return call(
            functools.partial(weigh_body, places, high, parts),
            [(tall, F32), ((2, cols), F32)] + grads,
            [normed_t] + list(low_a) + list(low_b) + blocks,
            [weights],
            us=0.1,
        )

    def finish(side, dn0, dn1, x, dmiddle, small, target, qv0, qv1):
        return call(
            finish_body,
            [(wide, BF16), ((8, cols), F32)],
            [side, dn0, dn1, x, dmiddle, small, target, qv0, qv1],
            (),
            1,
            us=20,
            mib=5,
        )

    def join(own, beside, across, corner):
        operands = [side, segment_ids, own, beside, across, corner]
        return call(join_body, [((rows, length, width), BF16)], operands, (), 1, us=20)[0]

    if not staged:

        def gathered(blocks):
            full = []
            for block in blocks:
                block = lax.all_gather(block, "fsdp", axis=0, tiled=True)
                full.append(lax.all_gather(block, "mp", axis=1, tiled=True))
            full = jnp.stack(full)
            return [full[:, :, yr * cols : (yr + 1) * cols].reshape(1, 3 * width, cols) for yr in range(2)]

        target = lax.iota(jnp.int32, width)[None]
        wa = gathered([w_query, w_key, w_value])
        wb = gathered([w_out.T, w_up, w_down.T])
        small = jnp.stack([gain1, shift1, b_out, gain2, shift2, b_down] + [jnp.zeros_like(gain1)] * 2)
        small = lax.all_gather(small, "fsdp", axis=1, tiled=True).astype(F32)
        units = jnp.stack([b_query, b_value, b_up] + [jnp.zeros_like(b_up)] * 5)
        units = lax.all_gather(units, "mp", axis=1, tiled=True).astype(F32)
        units = [units[:, :cols], units[:, cols:]]
        x, ct, xhat, bias = begin(target)
        *heads0, _, _, normed, normed_t = project(xhat, [wa[0]], True, (small, units[0]))
        *heads1, _ = project(normed, [wa[1]], False, (small, units[1]))
        both = (heads0, heads1)
        mixed = [attend(part, both[yr], bias) for yr in range(2) for part in range(2)]
        made = feed(x, [o for o, _ in mixed], small, units, target, wb)
        result = made[0]
        none = jnp.zeros_like(side)
        dmiddle, da0, da1, sums_b, grads_b = feed_back(none, ct, made[1:], small, target, wb)
        dn, qv, grads_a = [], [], []
        for yr, da in enumerate((da0, da1)):
            lows = [backward(part, both[yr], da, *mixed[2 * yr + part], bias) for part in range(2)]
            got = weigh(normed_t, [wa[yr]], *lows)
            dn.append(got[0])
            qv.append(got[1])
            grads_a.append(got[2])
        grad_window, sums_a = finish(none, dn[0], dn[1], x, dmiddle, small, target, *qv)

        def scattered(pair):
            full = jnp.concatenate(pair, axis=2).astype(F32)
            full = lax.psum_scatter(full, "mp", scatter_dimension=2, tiled=True)
            return lax.psum_scatter(full, "fsdp", scatter_dimension=1, tiled=True)

        grad_q, grad_k, grad_v = scattered(grads_a)
        grad_out, grad_up, grad_down = scattered([grads_b[0], grads_b[1]])
        grad_out, grad_down = grad_out.T, grad_down.T
        sums_a, sums_b = sums_a.reshape(4, width), sums_b.reshape(8, width)
        sums = jnp.concatenate([sums_a[0:2], sums_b[0:4], sums_a[2:4], sums_b[4:5]])
        sums = lax.psum(sums, BOTH)
        mine_f = lax.dynamic_slice(sums, (0, f * wr), (6, wr))
        mine_u = lax.dynamic_slice(sums, (6, m * wc), (3, wc))

        def shared(value):
            across = to(value, 0, 2)
            return join(value, to(value, 0, 1), across, to(across, 0, 1))

        out_hidden, grad_hidden = shared(result), shared(grad_window)
    else:
        piece_a, piece_b = (1, 3 * half + 16, cols), (1, 3 * half, cols)

        def stacked(pieces):
            return call(stack_body, [((deep,) + pieces[0].shape[1:], BF16)], pieces)[0]

        def part(block, of):
            return lax.dynamic_slice(block, (of * half, 0), (half, wc))

        theirs = jnp.stack([part(w, 1 - core) for w in (w_query, w_key, w_value)])
        got = to(theirs, 0, 1)
        theirs, gain1, b_query, w_query, w_key, w_value = fence(theirs, gain1, b_query, w_query, w_key, w_value)
        mine = jnp.stack([part(w, core) for w in (w_query, w_key, w_value)])
        small = jnp.stack([gain1, shift1, b_out, gain2, shift2, b_down])
        units = jnp.stack([b_query, b_value, b_up])
        units_pair = to(units, 0, 1)
        feature = lax.iota(jnp.int32, width)
        target = (((feature // half) ^ (f * 2 + core)) * half + feature % half)[None]
        got, units_pair, small, mine = fence(got, units_pair, small, mine)

        first = call(
            meet_a_body, [(piece_a, BF16)], [side, mine, got, small, units, units_pair], (), 1
        )[0]
        first_parts = [to(first, flip, 0) for flip in flips]
        first, w_out, w_up, w_down = fence(first, w_out, w_up, w_down)
        mine, theirs = call(deal_body, [((3, half, wc), BF16)] * 2, [side, w_out, w_up, w_down], (), 1)
        got = to(theirs, 0, 1)
        second = call(meet_b_body, [(piece_b, BF16)], [side, mine, got], (), 1)[0]
        first, first_parts, second, hidden_in, target = fence(first, first_parts, second, hidden_in, target)

        qkv = stacked([first] + first_parts)
        qkv_x, qkv_y = to(qkv, 1, 0), to(qkv, 0, 2)
        second_parts = [to(second, flip, 0) for flip in flips]
        x, ct, xhat, bias = begin(target)
        second_parts, second, qkv, qkv_x, qkv_y, xhat = fence(second_parts, second, qkv, qkv_x, qkv_y, xhat)
        qkv_xy = to(qkv, 1, 2)

        qkv_c, qkv_xc = to(qkv, 0, 1), to(qkv_x, 0, 1)
        odu = stacked([second] + second_parts)
        near = [qkv, qkv_c, qkv_x, qkv_xc]
        *heads0, shift0, small, normed, normed_t = project(xhat, near, True)
        heads0, qkv_y, odu = fence(heads0, qkv_y, odu)
        qkv_yc, odu_x, odu_y, odu_xy = to(qkv_y, 0, 1), to(odu, 1, 0), to(odu, 0, 2), to(odu, 1, 2)
        o00, l00 = attend(0, heads0, bias)
        o00, heads0, qkv_yc, qkv_xy, odu = fence(o00, heads0, qkv_yc, qkv_xy, odu)
        qkv_xyc, odu_c = to(qkv_xy, 0, 1), to(odu, 0, 1)
        o01, l01 = attend(1, heads0, bias)
        o01, qkv_xyc, odu_c, normed = fence(o01, qkv_xyc, odu_c, normed)
        far = [qkv_y, qkv_yc, qkv_xy, qkv_xyc]
        *heads1, shift1u = project(normed, far, False)
        o10, l10 = attend(0, heads1, bias)
        o10, heads1, odu_x, odu_y = fence(o10, heads1, odu_x, odu_y)
        odu_xc, odu_yc = to(odu_x, 0, 1), to(odu_y, 0, 1)
        o11, l11 = attend(1, heads1, bias)
        o11, odu_xc, odu_yc, odu_xy = fence(o11, odu_xc, odu_yc, odu_xy)
        odu_xyc = to(odu_xy, 0, 1)

        odu_blocks = [odu, odu_c, odu_x, odu_xc, odu_y, odu_yc, odu_xy, odu_xyc]
        made = fence(*feed(x, [o00, o01, o10, o11], small, [shift0, shift1u], target, odu_blocks))
        result = made[0]
        res_c, res_y = to(result, 0, 1), to(result, 0, 2)
        made = feed_back(side, ct, made[1:], small, target, odu_blocks)
        dmiddle, da0, da1, b_sums, b_keep, b_send, res_c = fence(*made, res_c)

        n_far, n_near = 2 * deep * 3 * half, deep * 3 * half
        f32_16, f32_8 = ((16, cols), F32), ((8, cols), F32)
        b_got, b_sums_got = to(b_send, 0, 1), to(b_sums, 0, 1)
        low10 = backward(0, heads1, da1, o10, l10, bias)
        low10, heads1, b_got, b_sums_got = fence(low10, heads1, b_got, b_sums_got)
        b_far, b_sums = call(
            far_b_body,
            [((n_far + 32, cols), BF16), f32_16],
            [b_keep, b_got, b_sums, b_sums_got],
        )
        b_far = to(b_far, 0, 2)
        low11 = backward(1, heads1, da1, o11, l11, bias)
        low11, normed_t = fence(low11, normed_t)
        dn1, qv1, keep1, send1 = weigh(normed_t, far, low10, low11)
        dn1, keep1, send1, da0, res_y = fence(dn1, keep1, send1, da0, res_y)
        got1, res_yc = to(send1, 0, 1), to(res_y, 0, 1)
        low00 = backward(0, heads0, da0, o00, l00, bias)
        low00, heads0, got1, res_yc = fence(low00, heads0, got1, res_yc)
        a_far0, a_far1 = call(far_a_body, [((n_near, cols), BF16)] * 2, [keep1, got1])
        a_far0, a_far1, heads0 = fence(a_far0, a_far1, heads0)
        a_far1, a_far0 = to(a_far1, 0, 2), to(a_far0, 0, 2)
        low01 = backward(1, heads0, da0, o01, l01, bias)
        low01, normed_t, b_far = fence(low01, normed_t, b_far)
        b_x, b_sums = call(
            near_b_body, [((n_near + 32, cols), BF16), f32_16], [b_keep, b_got, b_far, b_sums]
        )
        b_x = to(b_x, 1, 0)
        dn0, qv0, keep0, send0 = weigh(normed_t, near, low00, low01)
        dn0, keep0, send0, dmiddle = fence(dn0, keep0, send0, dmiddle)
        got0 = to(send0, 0, 1)
        n_two = 2 * 3 * half
        grad_window, a_sums = finish(side, dn0, dn1, x, dmiddle, small, target, qv0, qv1)
        grad_window, a_sums, got0, a_far1, b_x = fence(grad_window, a_sums, got0, a_far1, b_x)

        gw_y, gw_c, a_sums_got = to(grad_window, 0, 2), to(grad_window, 0, 1), to(a_sums, 0, 1)
        a_sums_got, gw_c, keep0 = fence(a_sums_got, gw_c, keep0)
        a_x, a_sums = call(
            near_a_body, [((n_near + 16, cols), BF16), f32_8], [keep0, got0, a_far1, a_sums, a_sums_got]
        )
        a_x, b_keep = fence(a_x, b_keep)
        a_x = to(a_x, 1, 0)
        b_own, b_z2, b_sums = call(
            high_b_body,
            [((2, 3 * half, cols), F32), ((n_two + 32, cols), BF16), f32_16],
            [b_keep, b_got, b_far, b_x, b_sums],
        )
        b_z2, result = fence(b_z2, result)
        b_z2 = to(b_z2, 4, 0)
        out_hidden = join(result, res_c, res_y, res_yc)
        b_z2, out_hidden = fence(b_z2, out_hidden)

        def last(own, sums, got, kind):
            return call(last_body, [((3, half, wc), F32)] * 2 + [kind], [side, own, sums] + got, (), 1, us=20)

        def deliver(mine, got, turned):
            shapes = [((wc, wr) if t else (wr, wc), F32) for t in turned]
            return call(functools.partial(deliver_body, turned), shapes, [side, mine, got], (), 1)

        b_own, b_z1, b_sums = call(
            middle_b_body,
            [((3 * half, cols), F32), ((3 * half + 32, cols), BF16), f32_16],
            [b_own, b_z2, b_sums],
            us=20,
        )
        b_z1, a_x, a_far0, keep0 = fence(b_z1, a_x, a_far0, keep0)
        a_split = call(
            high_a_body,
            [((3 * half, cols), F32)] + [((3 * half + 16, cols), BF16)] * (deep - 1) + [f32_8],
            [keep0, got0, a_far0, a_x, a_sums],
        )
        a_split, b_z1, b_own = fence(a_split, b_z1, b_own)
        a_high = [to(part, flip, 0) for part, flip in zip(a_split[1:-1], flips)]
        b_z1 = to(b_z1, 2, 0)
        b_z1, gw_y = fence(b_z1, gw_y)
        b_mine, b_theirs, b_sums = last(b_own, b_sums, [b_z1], f32_16)
        b_last, gw_yc = to(b_theirs, 0, 1), to(gw_y, 0, 1)
        grad_hidden = join(grad_window, gw_c, gw_y, gw_yc)
        b_last, grad_hidden = fence(b_last, grad_hidden)
        grad_out, grad_up, grad_down = deliver(b_mine, b_last, (True, False, True))
        a_own, a_high, grad_out, grad_hidden = fence(a_split[0], a_high, grad_out, grad_hidden)
        a_mine, a_theirs, a_sums = last(a_own, a_split[-1], a_high, f32_8)
        a_last = to(a_theirs, 0, 1)
        a_sums = a_sums + to(a_sums, 0, 2)
        grad_q, grad_k, grad_v = deliver(a_mine, a_last, (False, False, False))
        sums = jnp.concatenate(
            [
                a_sums.reshape(4, width)[0:2],
                b_sums.reshape(8, width)[0:4],
                a_sums.reshape(4, width)[2:4],
                b_sums.reshape(8, width)[4:5],
            ]
        )
        mine_f = lax.dynamic_slice(sums, (0, f * wr), (6, wr))
        mine_u = lax.dynamic_slice(sums, (6, m * wc), (3, wc))
    return (
        out_hidden,
        grad_hidden,
        mine_f[0],
        mine_f[1],
        grad_q,
        mine_u[0],
        grad_k,
        grad_v,
        mine_u[1],
        grad_out,
        mine_f[2],
        mine_f[3],
        mine_f[4],
        grad_up,
        mine_u[2],
        grad_down,
        mine_f[5],
    )


def solution(mesh):
    return jax.shard_map(
        per_device,
        mesh=mesh,
        in_specs=(
            P("fsdp", None, None),
            P("fsdp", None),
            P("fsdp", None),
            P("fsdp"),
            P("fsdp"),
            P("fsdp", "mp"),
            P("mp"),
            P("fsdp", "mp"),
            P("fsdp", "mp"),
            P("mp"),
            P("mp", "fsdp"),
            P("fsdp"),
            P("fsdp"),
            P("fsdp"),
            P("fsdp", "mp"),
            P("mp"),
            P("mp", "fsdp"),
            P("fsdp"),
            P("fsdp", None, None),
        ),
        out_specs=(
            P("fsdp", None, None),
            P("fsdp", None, None),
            P("fsdp"),
            P("fsdp"),
            P("fsdp", "mp"),
            P("mp"),
            P("fsdp", "mp"),
            P("fsdp", "mp"),
            P("mp"),
            P("mp", "fsdp"),
            P("fsdp"),
            P("fsdp"),
            P("fsdp"),
            P("fsdp", "mp"),
            P("mp"),
            P("mp", "fsdp"),
            P("fsdp"),
        ),
        check_vma=False,
    )
```

```python
import functools
import math

import jax
import jax.numpy as jnp
from jax import lax
from jax.experimental import pallas as pl
from jax.experimental.pallas import tpu as pltpu
from jax.sharding import PartitionSpec as P

HD = 24
PAD = 32
MOST = 128
BOTH = ("fsdp", "mp")
EPS = 1e-05
F32 = jnp.float32
BF16 = jnp.bfloat16
LOG2 = math.log2(math.e) / math.sqrt(HD)
SCALE = 1.0 / math.sqrt(HD)
GELU = math.sqrt(2.0 / math.pi)


def send(value, fs, mp, flip_f, flip_m):
    pairs = [(f * mp + m, (f ^ flip_f) * mp + (m ^ flip_m)) for f in range(fs) for m in range(mp)]
    return lax.ppermute(value, BOTH, pairs)


def dot_nn(left, right):
    return lax.dot_general(left, right, (((1,), (0,)), ((), ())), preferred_element_type=F32)


def dot_nt(left, right):
    return lax.dot_general(left, right, (((1,), (1,)), ((), ())), preferred_element_type=F32)


def dot_tn(left, right):
    return lax.dot_general(left, right, (((0,), (0,)), ((), ())), preferred_element_type=F32)


def norm_parts(values):
    centre = jnp.mean(values, axis=-1, keepdims=True)
    centered = values - centre
    inverse = lax.rsqrt(jnp.mean(centered * centered, axis=-1, keepdims=True) + EPS)
    return centered * inverse, inverse


def norm_back(grad, normed, inverse, gain):
    scaled = grad * gain
    return inverse * (
        scaled
        - jnp.mean(scaled, axis=-1, keepdims=True)
        - normed * jnp.mean(scaled * normed, axis=-1, keepdims=True)
    )


def call(body, outs, operands, scratch=(), scalars=0, us=0.1, mib=6):
    whole = pl.BlockSpec(memory_space=pltpu.VMEM)
    few = pl.BlockSpec(memory_space=pltpu.SMEM)
    return pl.pallas_call(
        body,
        out_shape=tuple(jax.ShapeDtypeStruct(s, d) for s, d in outs),
        in_specs=[few] * scalars + [whole] * (len(operands) - scalars),
        out_specs=tuple(whole for _ in outs),
        scratch_shapes=list(scratch),
        name=getattr(body, "func", body).__name__,
        compiler_params=pltpu.CompilerParams(vmem_limit_bytes=mib << 20),
        cost_estimate=pl.CostEstimate(
            flops=int(us * 2e9), transcendentals=0, bytes_accessed=int(us * 3e6)
        ),
    )(*operands)


def fence(*values):
    return lax.optimization_barrier(values)


def tiles(window):
    made = []
    for q0 in range(0, window, 256):
        qn = min(256, window - q0)
        k0 = max(0, q0 - MOST)
        made.append((q0, qn, k0, min(window, q0 + qn + MOST)))
    return made


def permutation(target):
    width = target.shape[1]
    return (lax.broadcasted_iota(jnp.int32, (width, width), 0) == target).astype(BF16)


def cuts_of(segments):
    middle = segments.shape[1] // 2
    held = segments[:, middle : middle + 1]
    first = jnp.sum((segments < held).astype(F32), axis=1, keepdims=True)
    last = jnp.sum((segments <= held).astype(F32), axis=1, keepdims=True)
    return jnp.where(middle - first <= last - middle, first, last)


def start_body(info, hidden, cotangent, segment_ids, pad_flags, target, x_o, c_o, xhat_o, bias_o):
    core, y = info[0], info[1]
    window = x_o.shape[0]
    gap = hidden.shape[1] - window
    start = pl.multiple_of(core * gap, 16)
    segments = segment_ids[...]
    cuts = cuts_of(segments)
    cut = jnp.where(y == 0, cuts[0:1], cuts[1:2])
    here = (start + lax.broadcasted_iota(jnp.int32, (window, 1), 0)).astype(F32)
    before = (here < cut).astype(F32)
    owned = jnp.where(core == 0, before, 1.0 - before)
    perm = permutation(target[...])
    x = dot_nn(hidden[y, pl.ds(start, window), :], perm)
    x_o[...] = x.astype(BF16)
    c_o[...] = (dot_nn(cotangent[y, pl.ds(start, window), :], perm) * owned).astype(BF16)
    xhat_o[...] = norm_parts(x)[0]
    segs = jnp.where(y == 0, segments[0:1], segments[1:2]).astype(F32)
    pads = pad_flags[...]
    pads = jnp.where(y == 0, pads[0:1], pads[1:2])
    code = jnp.where(pads == 0, segs, -1.0)
    segs = jnp.where(core == 0, segs[:, :window], segs[:, gap:])
    wide = bias_o.shape[1]
    if wide > window:
        segs = jnp.concatenate([segs, jnp.full((1, wide - window), -2.0, F32)], axis=1)
    code = jnp.where(core == 0, code[:, :window], code[:, gap:])
    column = jnp.broadcast_to(code, (8, window)).T[:, 0:1]
    key = lax.broadcasted_iota(jnp.int32, (window, wide), 0)
    query = lax.broadcasted_iota(jnp.int32, (window, wide), 1)
    bias_o[...] = jnp.where((column == segs) | (key == query), 0.0, -1e30)


def assemble(blocks, places, high, weights):
    for block, rows in zip(blocks, places):
        for z, row in enumerate(rows):
            for w in range(3):
                weights[w, row : row + high] = block[z, w * high : (w + 1) * high]


def disassemble(value, outs, pick):
    value = value.astype(BF16)
    if len(outs) == 1:
        outs[0][pick] = value
        return
    _, deep, high, _ = outs[0].shape[-4:]
    half = high // 3
    yr, w = pick[:-1], pick[-1]
    for x in range(2):
        for z in range(deep):
            for c in range(2):
                at = ((z * 2 + x) * 2 + c) * half
                outs[c][yr + (x, z, pl.ds(w * half, half))] = value[at : at + half]


def common_order(rows, perm):
    high = rows.astype(BF16)
    rest = rows - high.astype(F32)
    mid = rest.astype(BF16)
    last = (rest - mid.astype(F32)).astype(BF16)
    return dot_nn(high, perm) + dot_nn(mid, perm) + dot_nn(last, perm)


def by_head(value, fill=0.0):
    tokens, columns = value.shape
    parts = value.T.reshape(columns // HD, HD, tokens)
    row = lax.broadcasted_iota(jnp.int32, (columns // HD, PAD - HD, tokens), 1)
    extra = jnp.where(row == 0, fill, 0.0)
    return jnp.concatenate([parts, extra], axis=1).astype(BF16)


def flat_heads(value):
    heads, _, tokens = value.shape
    return value[:, :HD, :].reshape(heads * HD, tokens)


def project_body(places, high, unpack, first, given, *refs):
    blocks = refs[: len(places)]
    refs = refs[len(places) :]
    if not unpack:
        small_i, shift_i = refs[:2]
        refs = refs[2:]
    qt, kt, vt, shift_o = refs[:4]
    weights = refs[-1]
    assemble(blocks, places, high, weights)
    if unpack:
        shifts = blocks[0][0, 3 * high : 3 * high + 16].astype(F32)[0:8]
    else:
        shifts = shift_i[...]
    shift_o[...] = shifts
    if first:
        small_o, n_o, nt_o = refs[4:7]
        if unpack:
            deep = blocks[0].shape[0]
            wide = blocks[0].shape[2] // 4
            rows = [
                [blocks[2 * x][z, 3 * high : 3 * high + 16].astype(F32) for x in range(2)]
                for z in range(deep)
            ]
            made = []
            for p in range(6):
                r, at = 8 + p // 4, p % 4 * wide
                made.append(
                    jnp.concatenate(
                        [rows[z][x][r : r + 1, at : at + wide] for z in range(deep) for x in range(2)],
                        axis=1,
                    )
                )
            made += [jnp.zeros_like(made[0])] * 2
            small = jnp.concatenate(made, axis=0)
        else:
            small = small_i[...]
        small_o[...] = small
        exact = given[...] * small[0:1] + small[1:2]
        normed = exact.astype(BF16)
        n_o[...] = normed
        nt_o[...] = exact.T.astype(BF16)
    else:
        normed = given[...]
    qt[...] = by_head(dot_nn(normed, weights[0]) + shifts[0:1])
    kt[...] = by_head(dot_nn(normed, weights[1]))
    vt[...] = by_head(dot_nn(normed, weights[2]) + shifts[1:2], 1.0)


def forward_body(first, qt, kt, vt, bias, ot, lse):
    heads, _, window = ot.shape
    rows = 4 * PAD

    def four(i, carry):
        h = first + 4 * i
        for q0, qn, k0, k1 in tiles(window):
            query = qt[pl.ds(h, 4), :, q0 : q0 + qn].reshape(rows, qn).astype(F32)
            if qn < 256:
                query = jnp.concatenate([query, jnp.zeros((rows, 256 - qn), F32)], axis=1)
            own = lax.broadcasted_iota(jnp.int32, (rows, 256), 0) // PAD
            block = [jnp.where(own == n, query, 0.0).astype(BF16) for n in range(4)]
            keys = kt[pl.ds(h, 4), :, k0:k1].reshape(rows, k1 - k0)
            values = vt[pl.ds(h, 4), :, k0:k1].reshape(rows, k1 - k0)
            scores = dot_tn(keys, jnp.concatenate(block, axis=1))
            tops, weights = [], []
            for n in range(4):
                part = scores[:, n * 256 : (n + 1) * 256] * LOG2 + bias[k0:k1, q0 : q0 + 256]
                top = jnp.max(part, axis=0, keepdims=True)
                tops.append(top)
                weights.append(jnp.exp2(part - top).astype(BF16))
            mixed = dot_nn(values, jnp.concatenate(weights, axis=1))
            for n in range(4):
                own_mixed = mixed[n * PAD : (n + 1) * PAD, n * 256 : n * 256 + qn]
                total = own_mixed[HD : HD + 1]
                ot[4 * i + n, :, q0 : q0 + qn] = own_mixed / total
                lse[4 * i + n, :, q0 : q0 + qn] = tops[n][:, :qn] + jnp.log2(total)
        return carry

    lax.fori_loop(0, heads // 4, four, 0)


def feed_body(places, high, x_r, o00, o01, o1, small, cols0, cols1, target, *refs):
    count = len(places)
    blocks = refs[: 2 * count]
    refs = refs[2 * count :]
    out_o, xhat_o, inv_o, n_o = refs[:4]
    atts, acts, slopes, weights = refs[4:6], refs[6:8], refs[8:10], refs[10:]
    for yr in range(2):
        assemble(blocks[yr * count : (yr + 1) * count], places, high, weights[yr])
    atts[0][...] = jnp.concatenate([flat_heads(o00[...]), flat_heads(o01[...])], axis=0).T.astype(BF16)
    atts[1][...] = flat_heads(o1[...]).T.astype(BF16)
    x = x_r[...].astype(F32)
    middle = x + dot_nt(atts[0][...], weights[0][0]) + dot_nt(atts[1][...], weights[1][0]) + small[2:3]
    xhat, inverse = norm_parts(middle)
    xhat_o[...] = xhat
    inv_o[...] = inverse
    normed = (xhat * small[3:4] + small[4:5]).astype(BF16)
    n_o[...] = normed
    result = middle + small[5:6]
    for yr, cols in enumerate((cols0, cols1)):
        pre = dot_nn(normed, weights[yr][1]) + cols[2:3]
        square = pre * pre
        bent = jnp.tanh(GELU * (pre + 0.044715 * (pre * square)))
        act = (0.5 * pre * (1.0 + bent)).astype(BF16)
        acts[yr][...] = act
        slopes[yr][...] = 0.5 * (1.0 + bent) + 0.5 * pre * (1.0 - bent * bent) * (
            GELU * (1.0 + 3.0 * 0.044715 * square)
        )
        result = result + dot_nt(act, weights[yr][2])
    out_o[...] = dot_nn(result.astype(BF16), permutation(target[...])).astype(BF16)


def rows_of(info, feats, units):
    width = feats.shape[1]
    cols = width // 2
    made = []
    for i in range(feats.shape[0]):
        made += [feats[i : i + 1, :cols], feats[i : i + 1, cols:]]
    for own, other in units:
        made += [jnp.where(info[1] == 0, own, other), jnp.where(info[1] == 0, other, own)]
    return jnp.concatenate(made, axis=0)


def feed_back_body(places, high, parts, info, c_r, xhat_r, inv_r, n_r, a0, a1, act0, act1, slope0, slope1, small, target, *refs):
    count = len(places)
    blocks = refs[: 2 * count]
    refs = refs[2 * count :]
    mid_o, d0, d1, sum_o = refs[:4]
    outs = refs[4 : 4 + parts]
    weights = refs[4 + parts :]
    for yr in range(2):
        assemble(blocks[yr * count : (yr + 1) * count], places, high, weights[yr])
    ct_low, normed = c_r[...], n_r[...]
    cols = act0.shape[1]

    def both(left, right, w):
        grads = dot_tn(left, jnp.concatenate(right, axis=1))
        for yr in range(2):
            disassemble(grads[:, yr * cols : (yr + 1) * cols], outs, (yr, w))

    both(ct_low, [act0[...], act1[...]], 2)
    dpres = [
        (dot_nn(ct_low, weights[yr][2]) * slope[...]).astype(BF16) for yr, slope in enumerate((slope0, slope1))
    ]
    both(normed, dpres, 1)
    ups = [jnp.sum(dpre.astype(F32), axis=0, keepdims=True) for dpre in dpres]
    dnorm = dot_nt(dpres[0], weights[0][1]) + dot_nt(dpres[1], weights[1][1])
    ct, xhat = ct_low.astype(F32), xhat_r[...]
    dmiddle = ct + norm_back(dnorm, xhat, inv_r[...], small[3:4])
    mid_o[...] = dmiddle
    sums = [jnp.sum(part, axis=0, keepdims=True) for part in (dmiddle, dnorm * xhat, dnorm, ct)]
    sums = common_order(
        jnp.concatenate(sums + [jnp.zeros((4, dnorm.shape[1]), F32)], axis=0), permutation(target[...])
    )
    sums = rows_of(info, sums[0:4], [ups])
    sum_o[...] = jnp.concatenate([sums, jnp.zeros_like(sums[0:6])], axis=0)
    low = dmiddle.astype(BF16)
    both(low, [a0[...], a1[...]], 0)
    for yr in range(2):
        (d0, d1)[yr][...] = by_head(dot_nn(low, weights[yr][0]))


def backward_body(first, mixed, qt, kt, vt, dt, ot, lse, bias, dq_o, dk_o, dv_o, dq, dk, dv):
    heads, _, window = dq.shape
    made = tiles(window)

    def head(i, carry):
        h = first + i
        delta = jnp.sum(dt[h].astype(F32) * ot[mixed + i], axis=0, keepdims=True)
        for ref in (dk, dv):
            ref[i] = jnp.zeros_like(ref[i])
        for q0, qn, k0, k1 in made:
            query, grad = qt[h, :, q0 : q0 + qn], dt[h, :, q0 : q0 + qn]
            scores = dot_tn(kt[h, :, k0:k1], query)
            dprobs = dot_tn(vt[h, :, k0:k1], grad)
            probs = jnp.exp2(scores * LOG2 + (bias[k0:k1, q0 : q0 + qn] - lse[mixed + i, :, q0 : q0 + qn]))
            dscores = (probs * (dprobs - delta[:, q0 : q0 + qn])).astype(BF16)
            dq[i, :, q0 : q0 + qn] = dot_nn(kt[h, :, k0:k1], dscores)
            dk[i, :, k0:k1] += dot_nt(query, dscores)
            dv[i, :, k0:k1] += dot_nt(grad, probs.astype(BF16))
        return carry

    lax.fori_loop(0, heads, head, 0, unroll=2)
    for ref, out, factor in ((dq, dq_o, SCALE), (dk, dk_o, SCALE), (dv, dv_o, 1.0)):
        out[...] = (flat_heads(ref[...]) * factor).astype(BF16)


def weigh_body(places, high, parts, nt_r, qa, ka, va, qb, kb, vb, *refs):
    blocks = refs[: len(places)]
    refs = refs[len(places) :]
    dn, sums = refs[:2]
    outs = refs[2 : 2 + parts]
    weights = refs[2 + parts]
    assemble(blocks, places, high, weights)
    normed = nt_r[...]
    ones = jnp.ones((8, normed.shape[1]), BF16)
    total = None
    for w, (a, b) in enumerate(((qa, qb), (ka, kb), (va, vb))):
        low = jnp.concatenate([a[...], b[...]], axis=0)
        disassemble(dot_nt(normed, low), outs, (w,))
        part = dot_nn(weights[w], low)
        total = part if total is None else total + part
        if w != 1:
            sums[w // 2 : w // 2 + 1] = dot_nt(ones, low)[0:1]
    dn[...] = total


def finish_body(info, dn0, dn1, x_r, mid, small, target, qv0, qv1, out_o, sum_o):
    perm = permutation(target[...])
    grad = (dn0[...] + dn1[...]).T
    xhat, inverse = norm_parts(x_r[...].astype(F32))
    dx = mid[...] + norm_back(grad, xhat, inverse, small[0:1])
    out_o[...] = dot_nn(dx.astype(BF16), perm).astype(BF16)
    sums = [jnp.sum(part, axis=0, keepdims=True) for part in (grad * xhat, grad)]
    sums = common_order(jnp.concatenate(sums + [jnp.zeros((6, grad.shape[1]), F32)], axis=0), perm)
    sum_o[...] = rows_of(info, sums[0:2], [(qv0[w : w + 1], qv1[w : w + 1]) for w in range(2)])


def deal_body(info, wo, wu, wd, mine, theirs):
    half = mine.shape[1]
    values = [wo[...].astype(F32).T.astype(BF16), wu[...], wd[...].astype(F32).T.astype(BF16)]

    @pl.when(info[0] == 0)
    def _():
        for w, value in enumerate(values):
            mine[w], theirs[w] = value[:half], value[half:]

    @pl.when(info[0] != 0)
    def _():
        for w, value in enumerate(values):
            theirs[w], mine[w] = value[:half], value[half:]


def meet_a_body(info, mine, got, small, units, units_pair, first):
    half = got.shape[1]
    wr, wc = small.shape[1], units.shape[1]
    zeros = jnp.zeros((8, 4 * wr), F32)

    def meet(own_first):
        def pair(own, other):
            return jnp.concatenate([own, other] if own_first else [other, own], axis=1)

        for w in range(3):
            first[0, w * half : (w + 1) * half, :] = pair(mine[w], got[w])
        params = small[...].astype(F32)
        if not own_first:
            params = jnp.concatenate([params[:, half:], params[:, :half]], axis=1)
        above = jnp.concatenate([params[p : p + 1] for p in range(4)], axis=1)
        below = jnp.concatenate([params[4:5], params[5:6], zeros[0:1, : 2 * wr]], axis=1)
        both = pair(units[...], units_pair[...]).astype(F32)
        extra = jnp.concatenate([both, zeros[:5], above, below, zeros[:6]], axis=0)
        first[0, 3 * half : 3 * half + 16, :] = extra.astype(BF16)

    @pl.when(info[0] == 0)
    def _():
        meet(True)

    @pl.when(info[0] != 0)
    def _():
        meet(False)


def meet_b_body(info, mine, got, second):
    half = got.shape[1]

    def meet(low, high):
        for w in range(3):
            second[0, w * half : (w + 1) * half, :] = jnp.concatenate([low[w], high[w]], axis=1)

    @pl.when(info[0] == 0)
    def _():
        meet(mine, got)

    @pl.when(info[0] != 0)
    def _():
        meet(got, mine)


def stack_body(*refs):
    out = refs[-1]
    for at, ref in enumerate(refs[:-1]):
        out[at] = ref[0]


def pack(out, row, sums):
    count = sums.shape[0]
    high = sums.astype(BF16)
    out[row : row + count] = high
    out[row + count : row + 2 * count] = (sums - high.astype(F32)).astype(BF16)


def unpack_sums(ref, row, count):
    both = ref[row : row + 2 * count].astype(F32)
    return both[:count] + both[count:]


def block_sums(keep, got, out, row):
    deep, high, _ = keep.shape
    for z in range(deep):
        total = keep[z].astype(F32) + got[z].astype(F32)
        out[row + z * high : row + (z + 1) * high] = total.astype(BF16)


def far_b_body(keep, got, sums, sums_got, out, sum_o):
    total = sums[...] + sums_got[...]
    sum_o[...] = total
    for x in range(2):
        block_sums(keep.at[1, x], got.at[1, x], out, x * (out.shape[0] - 32) // 2)
    pack(out, out.shape[0] - 32, total)


def far_a_body(keep, got, out0, out1):
    block_sums(keep.at[0], got.at[0], out0, 0)
    block_sums(keep.at[1], got.at[1], out1, 0)


def pass_on(keep, got, far, out):
    deep, high, _ = keep.shape
    for z in range(deep):
        rows = slice(z * high, (z + 1) * high)
        total = keep[z].astype(F32) + got[z].astype(F32) + far[rows].astype(F32)
        out[rows] = total.astype(BF16)


def near_b_body(keep, got, far, sums, out, sum_o):
    count = out.shape[0] - 32
    pass_on(keep.at[0, 1], got.at[0, 1], far.at[count : 2 * count], out)
    total = sums[...] + unpack_sums(far, 2 * count, 16)
    sum_o[...] = total
    pack(out, count, total)


def near_a_body(keep, got, far, sums, sums_got, out, sum_o):
    pass_on(keep.at[1], got.at[1], far, out)
    total = sums[...] + sums_got[...]
    sum_o[...] = total
    pack(out, out.shape[0] - 16, total)


def block_total(keep, got, far, passed, z):
    rows = slice(z * keep.shape[1], (z + 1) * keep.shape[1])
    return keep[z].astype(F32) + got[z].astype(F32) + far[rows].astype(F32) + passed[rows].astype(F32)


def high_b_body(keep, got, far, passed, sums, own, out, sum_o):
    kept, given = keep.at[0, 0], got.at[0, 0]
    deep, high, _ = kept.shape
    total = sums[...] + unpack_sums(passed, deep * high, sums.shape[0])
    sum_o[...] = total
    for z in range(deep):
        value = block_total(kept, given, far, passed, z)
        if z < deep // 2:
            own[z] = value
        else:
            out[(z - deep // 2) * high : (z - deep // 2 + 1) * high] = value.astype(BF16)
    pack(out, deep // 2 * high, total)


def middle_b_body(own, got, sums, own_o, out, sum_o):
    _, high, _ = own.shape
    total = sums[...] + unpack_sums(got, 2 * high, sums.shape[0])
    sum_o[...] = total
    own_o[...] = own[0] + got[0:high].astype(F32)
    out[0:high] = (own[1] + got[high : 2 * high].astype(F32)).astype(BF16)
    pack(out, high, total)


def high_a_body(keep, got, far, passed, sums, *outs):
    kept, given = keep.at[0], got.at[0]
    deep, high, _ = kept.shape
    total = sums[...] + unpack_sums(passed, deep * high, sums.shape[0])
    outs[-1][...] = total
    for z in range(deep):
        value = block_total(kept, given, far, passed, z)
        if z == 0:
            outs[0][...] = value
        else:
            outs[z][0:high] = value.astype(BF16)
            pack(outs[z], high, total)


def last_body(info, own, sums, *refs):
    parts, (mine, theirs, sum_o) = refs[:-3], refs[-3:]
    high = own.shape[0]
    half = high // 3
    total, wide = own[...], sums[...]
    for part in parts:
        total = total + part[0:high].astype(F32)
        wide = wide + unpack_sums(part, high, sums.shape[0])
    sum_o[...] = wide
    wc = mine.shape[2]

    def give(low, upper):
        for w in range(3):
            low[w] = total[w * half : (w + 1) * half, :wc]
            upper[w] = total[w * half : (w + 1) * half, wc:]

    @pl.when(info[0] == 0)
    def _():
        give(mine, theirs)

    @pl.when(info[0] != 0)
    def _():
        give(theirs, mine)


def deliver_body(turned, info, mine, got, *outs):
    half = mine.shape[1]

    def deliver(low, high):
        for w, out in enumerate(outs):
            if turned[w]:
                out[...] = jnp.concatenate([low[w], high[w]], axis=0).T
            else:
                out[0:half] = low[w]
                out[half:] = high[w]

    @pl.when(info[0] == 0)
    def _():
        deliver(mine, got)

    @pl.when(info[0] != 0)
    def _():
        deliver(got, mine)


def join_body(info, segment_ids, own, beside, across, corner, out):
    core, y = info[0], info[1]
    length, window = out.shape[1], own.shape[0]
    gap = length - window
    cuts = cuts_of(segment_ids[...])
    own_cut = jnp.where(y == 0, cuts[0:1], cuts[1:2])
    other_cut = jnp.where(y == 0, cuts[1:2], cuts[0:1])

    def row(low, high, place, cut):
        out[place, 0:gap] = low[0:gap]
        at = (gap + lax.broadcasted_iota(jnp.int32, (window - gap, 1), 0)).astype(F32)
        seam = jnp.where(at < cut, low[gap:window].astype(F32), high[0 : window - gap].astype(F32))
        out[place, gap:window] = seam.astype(BF16)
        out[place, window:length] = high[window - gap : window]

    @pl.when(core == 0)
    def _():
        row(own, beside, y, own_cut)
        row(across, corner, 1 - y, other_cut)

    @pl.when(core != 0)
    def _():
        row(beside, own, y, own_cut)
        row(corner, across, 1 - y, other_cut)


def per_device(
    hidden_in,
    segment_ids,
    pad_flags,
    gain1,
    shift1,
    w_query,
    b_query,
    w_key,
    w_value,
    b_value,
    w_out,
    b_out,
    gain2,
    shift2,
    w_up,
    b_up,
    w_down,
    b_down,
    cotangent,
):
    fs, mp = lax.axis_size("fsdp"), lax.axis_size("mp")
    rows, length, width = hidden_in.shape
    wr, wc = w_query.shape
    half, cols = wr // 2, 2 * wc
    heads = cols // HD
    f, m = lax.axis_index("fsdp"), lax.axis_index("mp")
    core, y = m % 2, m // 2
    side = jnp.stack([core, y])
    window = length // 2 + MOST // 2
    deep = fs // 2
    flips = [2 * z for z in range(1, deep)]
    staged = half % 16 == 0 and deep == 4
    if staged:
        places = [[((z * 2 + x) * 2 + c) * half for z in range(deep)] for x in range(2) for c in range(2)]
        high, parts = half, 2
    else:
        places, high, parts = [[0]], width, 1
    wide, tall = (window, width), (width, window)
    by_heads, by_few = (heads, PAD, window), (heads // 2, PAD, window)
    weights = pltpu.VMEM((3, width, cols), BF16)

    def to(value, flip_f, flip_m):
        return send(value, fs, mp, flip_f, flip_m)

    def begin(target):
        return call(
            start_body,
            [(wide, BF16), (wide, BF16), (wide, F32), ((window, -(-window // 256) * 256), F32)],
            [side, hidden_in, cotangent, segment_ids, pad_flags, target],
            (),
            1,
            us=3,
            mib=4,
        )

    def project(given, blocks, first, extra=()):
        outs = [(by_heads, BF16)] * 3 + [((8, cols), F32)]
        if first:
            outs += [((8, width), F32), (wide, BF16), (tall, BF16)]
        return call(
            functools.partial(project_body, places, high, not extra, first),
            outs,
            [given] + blocks + list(extra),
            [weights],
            us=2,
            mib=4,
        )

    def attend(part, qkv_heads, bias):
        first, count = (0, heads) if part is None else (part * (heads // 2), heads // 2)
        return call(
            functools.partial(forward_body, first),
            [((count, PAD, window), F32), ((count, 1, window), F32)],
            list(qkv_heads) + [bias],
            us=5,
        )

    def feed(x, mixed, small, shifts, target, blocks):
        units_shape = (window, cols)
        return call(
            functools.partial(feed_body, places, high),
            [(wide, BF16), (wide, F32), ((window, 1), F32), (wide, BF16)]
            + [(units_shape, BF16)] * 4
            + [(units_shape, F32)] * 2,
            [x] + mixed + [small] + shifts + [target] + blocks,
            [weights, weights],
            us=5,
            mib=7,
        )

    def feed_back(side, ct, made, small, target, blocks):
        if staged:
            grads = [((2, 2, deep, 3 * half, cols), BF16)] * 2
        else:
            grads = [((2, 3, width, cols), BF16)]
        return call(
            functools.partial(feed_back_body, places, high, parts),
            [(wide, F32), (by_heads, BF16), (by_heads, BF16), ((16, cols), F32)] + grads,
            [side, ct] + list(made) + [small, target] + blocks,
            [weights, weights],
            1,
            us=7,
            mib=10,
        )

    def backward(part, qkv_heads, da, o, lse, bias):
        return call(
            functools.partial(backward_body, part * (heads // 2), part * (heads // 2) if o.shape[0] == heads else 0),
            [((heads // 2 * HD, window), BF16)] * 3,
            list(qkv_heads) + [da, o, lse, bias],
            [pltpu.VMEM(by_few, F32)] * 3,
            us=15,
        )

    def weigh(normed_t, blocks, low_a, low_b):
        if staged:
            grads = [((2, deep, 3 * half, cols), BF16)] * 2
        else:
            grads = [((3, width, cols), BF16)]
        return call(
            functools.partial(weigh_body, places, high, parts),
            [(tall, F32), ((2, cols), F32)] + grads,
            [normed_t] + list(low_a) + list(low_b) + blocks,
            [weights],
            us=0.1,
        )

    def finish(side, dn0, dn1, x, dmiddle, small, target, qv0, qv1):
        return call(
            finish_body,
            [(wide, BF16), ((8, cols), F32)],
            [side, dn0, dn1, x, dmiddle, small, target, qv0, qv1],
            (),
            1,
            us=20,
            mib=5,
        )

    def join(own, beside, across, corner):
        operands = [side, segment_ids, own, beside, across, corner]
        return call(join_body, [((rows, length, width), BF16)], operands, (), 1, us=20)[0]

    if not staged:

        def gathered(blocks):
            full = []
            for block in blocks:
                block = lax.all_gather(block, "fsdp", axis=0, tiled=True)
                full.append(lax.all_gather(block, "mp", axis=1, tiled=True))
            full = jnp.stack(full)
            return [full[:, :, yr * cols : (yr + 1) * cols].reshape(1, 3 * width, cols) for yr in range(2)]

        target = lax.iota(jnp.int32, width)[None]
        wa = gathered([w_query, w_key, w_value])
        wb = gathered([w_out.T, w_up, w_down.T])
        small = jnp.stack([gain1, shift1, b_out, gain2, shift2, b_down] + [jnp.zeros_like(gain1)] * 2)
        small = lax.all_gather(small, "fsdp", axis=1, tiled=True).astype(F32)
        units = jnp.stack([b_query, b_value, b_up] + [jnp.zeros_like(b_up)] * 5)
        units = lax.all_gather(units, "mp", axis=1, tiled=True).astype(F32)
        units = [units[:, :cols], units[:, cols:]]
        x, ct, xhat, bias = begin(target)
        *heads0, _, _, normed, normed_t = project(xhat, [wa[0]], True, (small, units[0]))
        *heads1, _ = project(normed, [wa[1]], False, (small, units[1]))
        both = (heads0, heads1)
        mixed = [attend(0, heads0, bias), attend(1, heads0, bias)] + [attend(None, heads1, bias)] * 2
        made = feed(x, [o for o, _ in mixed[:3]], small, units, target, wb)
        result = made[0]
        none = jnp.zeros_like(side)
        dmiddle, da0, da1, sums_b, grads_b = feed_back(none, ct, made[1:], small, target, wb)
        dn, qv, grads_a = [], [], []
        for yr, da in enumerate((da0, da1)):
            lows = [backward(part, both[yr], da, *mixed[2 * yr + part], bias) for part in range(2)]
            got = weigh(normed_t, [wa[yr]], *lows)
            dn.append(got[0])
            qv.append(got[1])
            grads_a.append(got[2])
        grad_window, sums_a = finish(none, dn[0], dn[1], x, dmiddle, small, target, *qv)

        def scattered(pair):
            full = jnp.concatenate(pair, axis=2).astype(F32)
            full = lax.psum_scatter(full, "mp", scatter_dimension=2, tiled=True)
            return lax.psum_scatter(full, "fsdp", scatter_dimension=1, tiled=True)

        grad_q, grad_k, grad_v = scattered(grads_a)
        grad_out, grad_up, grad_down = scattered([grads_b[0], grads_b[1]])
        grad_out, grad_down = grad_out.T, grad_down.T
        sums_a, sums_b = sums_a.reshape(4, width), sums_b.reshape(8, width)
        sums = jnp.concatenate([sums_a[0:2], sums_b[0:4], sums_a[2:4], sums_b[4:5]])
        sums = lax.psum(sums, BOTH)
        mine_f = lax.dynamic_slice(sums, (0, f * wr), (6, wr))
        mine_u = lax.dynamic_slice(sums, (6, m * wc), (3, wc))

        def shared(value):
            across = to(value, 0, 2)
            return join(value, to(value, 0, 1), across, to(across, 0, 1))

        out_hidden, grad_hidden = shared(result), shared(grad_window)
    else:
        piece_a, piece_b = (1, 3 * half + 16, cols), (1, 3 * half, cols)

        def stacked(pieces):
            return call(stack_body, [((deep,) + pieces[0].shape[1:], BF16)], pieces)[0]

        def part(block, of):
            return lax.dynamic_slice(block, (of * half, 0), (half, wc))

        theirs = jnp.stack([part(w, 1 - core) for w in (w_query, w_key, w_value)])
        got = to(theirs, 0, 1)
        theirs, gain1, b_query, w_query, w_key, w_value = fence(theirs, gain1, b_query, w_query, w_key, w_value)
        mine = jnp.stack([part(w, core) for w in (w_query, w_key, w_value)])
        small = jnp.stack([gain1, shift1, b_out, gain2, shift2, b_down])
        units = jnp.stack([b_query, b_value, b_up])
        units_pair = to(units, 0, 1)
        feature = lax.iota(jnp.int32, width)
        target = (((feature // half) ^ (f * 2 + core)) * half + feature % half)[None]
        got, units_pair, small, mine = fence(got, units_pair, small, mine)

        first = call(
            meet_a_body, [(piece_a, BF16)], [side, mine, got, small, units, units_pair], (), 1
        )[0]
        first_parts = [to(first, flip, 0) for flip in flips]
        first, w_out, w_up, w_down = fence(first, w_out, w_up, w_down)
        mine, theirs = call(deal_body, [((3, half, wc), BF16)] * 2, [side, w_out, w_up, w_down], (), 1)
        got = to(theirs, 0, 1)
        second = call(meet_b_body, [(piece_b, BF16)], [side, mine, got], (), 1)[0]
        first, first_parts, second, hidden_in, target = fence(first, first_parts, second, hidden_in, target)

        qkv = stacked([first] + first_parts)
        qkv_x, qkv_y = to(qkv, 1, 0), to(qkv, 0, 2)
        second_parts = [to(second, flip, 0) for flip in flips]
        x, ct, xhat, bias = begin(target)
        second_parts, second, qkv, qkv_x, qkv_y, xhat = fence(second_parts, second, qkv, qkv_x, qkv_y, xhat)
        qkv_xy = to(qkv, 1, 2)

        qkv_c, qkv_xc = to(qkv, 0, 1), to(qkv_x, 0, 1)
        odu = stacked([second] + second_parts)
        near = [qkv, qkv_c, qkv_x, qkv_xc]
        *heads0, shift0, small, normed, normed_t = project(xhat, near, True)
        heads0, qkv_y, odu = fence(heads0, qkv_y, odu)
        qkv_yc, odu_x, odu_y, odu_xy = to(qkv_y, 0, 1), to(odu, 1, 0), to(odu, 0, 2), to(odu, 1, 2)
        o00, l00 = attend(0, heads0, bias)
        o00, heads0, qkv_yc, qkv_xy, odu = fence(o00, heads0, qkv_yc, qkv_xy, odu)
        qkv_xyc, odu_c = to(qkv_xy, 0, 1), to(odu, 0, 1)
        o01, l01 = attend(1, heads0, bias)
        o01, qkv_xyc, odu_c, normed = fence(o01, qkv_xyc, odu_c, normed)
        far = [qkv_y, qkv_yc, qkv_xy, qkv_xyc]
        *heads1, shift1u = project(normed, far, False)
        o1, l1 = attend(None, heads1, bias)
        o1, odu_x, odu_y = fence(o1, odu_x, odu_y)
        odu_xc, odu_yc = to(odu_x, 0, 1), to(odu_y, 0, 1)
        o1, odu_xc, odu_yc, odu_xy = fence(o1, odu_xc, odu_yc, odu_xy)
        odu_xyc = to(odu_xy, 0, 1)

        odu_blocks = [odu, odu_c, odu_x, odu_xc, odu_y, odu_yc, odu_xy, odu_xyc]
        made = fence(*feed(x, [o00, o01, o1], small, [shift0, shift1u], target, odu_blocks))
        result = made[0]
        res_c, res_y = to(result, 0, 1), to(result, 0, 2)
        made = feed_back(side, ct, made[1:], small, target, odu_blocks)
        dmiddle, da0, da1, b_sums, b_keep, b_send, res_c = fence(*made, res_c)

        n_far, n_near = 2 * deep * 3 * half, deep * 3 * half
        f32_16, f32_8 = ((16, cols), F32), ((8, cols), F32)
        b_got, b_sums_got = to(b_send, 0, 1), to(b_sums, 0, 1)
        low10 = backward(0, heads1, da1, o1, l1, bias)
        low10, heads1, b_got, b_sums_got = fence(low10, heads1, b_got, b_sums_got)
        b_far, b_sums = call(
            far_b_body,
            [((n_far + 32, cols), BF16), f32_16],
            [b_keep, b_got, b_sums, b_sums_got],
        )
        b_far = to(b_far, 0, 2)
        low11 = backward(1, heads1, da1, o1, l1, bias)
        low11, normed_t = fence(low11, normed_t)
        dn1, qv1, keep1, send1 = weigh(normed_t, far, low10, low11)
        dn1, keep1, send1, da0, res_y = fence(dn1, keep1, send1, da0, res_y)
        got1, res_yc = to(send1, 0, 1), to(res_y, 0, 1)
        low00 = backward(0, heads0, da0, o00, l00, bias)
        low00, heads0, got1, res_yc = fence(low00, heads0, got1, res_yc)
        a_far0, a_far1 = call(far_a_body, [((n_near, cols), BF16)] * 2, [keep1, got1])
        a_far0, a_far1, heads0 = fence(a_far0, a_far1, heads0)
        a_far1, a_far0 = to(a_far1, 0, 2), to(a_far0, 0, 2)
        low01 = backward(1, heads0, da0, o01, l01, bias)
        low01, normed_t, b_far = fence(low01, normed_t, b_far)
        b_x, b_sums = call(
            near_b_body, [((n_near + 32, cols), BF16), f32_16], [b_keep, b_got, b_far, b_sums]
        )
        b_x = to(b_x, 1, 0)
        dn0, qv0, keep0, send0 = weigh(normed_t, near, low00, low01)
        dn0, keep0, send0, dmiddle = fence(dn0, keep0, send0, dmiddle)
        got0 = to(send0, 0, 1)
        n_two = 2 * 3 * half
        grad_window, a_sums = finish(side, dn0, dn1, x, dmiddle, small, target, qv0, qv1)
        grad_window, a_sums, got0, a_far1, b_x = fence(grad_window, a_sums, got0, a_far1, b_x)

        gw_y, gw_c, a_sums_got = to(grad_window, 0, 2), to(grad_window, 0, 1), to(a_sums, 0, 1)
        a_sums_got, gw_c, keep0 = fence(a_sums_got, gw_c, keep0)
        a_x, a_sums = call(
            near_a_body, [((n_near + 16, cols), BF16), f32_8], [keep0, got0, a_far1, a_sums, a_sums_got]
        )
        a_x, b_keep = fence(a_x, b_keep)
        a_x = to(a_x, 1, 0)
        b_own, b_z2, b_sums = call(
            high_b_body,
            [((2, 3 * half, cols), F32), ((n_two + 32, cols), BF16), f32_16],
            [b_keep, b_got, b_far, b_x, b_sums],
        )
        b_z2, result = fence(b_z2, result)
        b_z2 = to(b_z2, 4, 0)
        out_hidden = join(result, res_c, res_y, res_yc)
        b_z2, out_hidden = fence(b_z2, out_hidden)

        def last(own, sums, got, kind):
            return call(last_body, [((3, half, wc), F32)] * 2 + [kind], [side, own, sums] + got, (), 1, us=20)

        def deliver(mine, got, turned):
            shapes = [((wc, wr) if t else (wr, wc), F32) for t in turned]
            return call(functools.partial(deliver_body, turned), shapes, [side, mine, got], (), 1)

        b_own, b_z1, b_sums = call(
            middle_b_body,
            [((3 * half, cols), F32), ((3 * half + 32, cols), BF16), f32_16],
            [b_own, b_z2, b_sums],
            us=20,
        )
        b_z1, a_x, a_far0, keep0 = fence(b_z1, a_x, a_far0, keep0)
        a_split = call(
            high_a_body,
            [((3 * half, cols), F32)] + [((3 * half + 16, cols), BF16)] * (deep - 1) + [f32_8],
            [keep0, got0, a_far0, a_x, a_sums],
        )
        a_split, b_z1, b_own = fence(a_split, b_z1, b_own)
        a_high = [to(part, flip, 0) for part, flip in zip(a_split[1:-1], flips)]
        b_z1 = to(b_z1, 2, 0)
        b_z1, gw_y = fence(b_z1, gw_y)
        b_mine, b_theirs, b_sums = last(b_own, b_sums, [b_z1], f32_16)
        b_last, gw_yc = to(b_theirs, 0, 1), to(gw_y, 0, 1)
        grad_hidden = join(grad_window, gw_c, gw_y, gw_yc)
        b_last, grad_hidden = fence(b_last, grad_hidden)
        grad_out, grad_up, grad_down = deliver(b_mine, b_last, (True, False, True))
        a_own, a_high, grad_out, grad_hidden = fence(a_split[0], a_high, grad_out, grad_hidden)
        a_mine, a_theirs, a_sums = last(a_own, a_split[-1], a_high, f32_8)
        a_last = to(a_theirs, 0, 1)
        a_sums = a_sums + to(a_sums, 0, 2)
        grad_q, grad_k, grad_v = deliver(a_mine, a_last, (False, False, False))
        sums = jnp.concatenate(
            [
                a_sums.reshape(4, width)[0:2],
                b_sums.reshape(8, width)[0:4],
                a_sums.reshape(4, width)[2:4],
                b_sums.reshape(8, width)[4:5],
            ]
        )
        mine_f = lax.dynamic_slice(sums, (0, f * wr), (6, wr))
        mine_u = lax.dynamic_slice(sums, (6, m * wc), (3, wc))
    return (
        out_hidden,
        grad_hidden,
        mine_f[0],
        mine_f[1],
        grad_q,
        mine_u[0],
        grad_k,
        grad_v,
        mine_u[1],
        grad_out,
        mine_f[2],
        mine_f[3],
        mine_f[4],
        grad_up,
        mine_u[2],
        grad_down,
        mine_f[5],
    )


def solution(mesh):
    return jax.shard_map(
        per_device,
        mesh=mesh,
        in_specs=(
            P("fsdp", None, None),
            P("fsdp", None),
            P("fsdp", None),
            P("fsdp"),
            P("fsdp"),
            P("fsdp", "mp"),
            P("mp"),
            P("fsdp", "mp"),
            P("fsdp", "mp"),
            P("mp"),
            P("mp", "fsdp"),
            P("fsdp"),
            P("fsdp"),
            P("fsdp"),
            P("fsdp", "mp"),
            P("mp"),
            P("mp", "fsdp"),
            P("fsdp"),
            P("fsdp", None, None),
        ),
        out_specs=(
            P("fsdp", None, None),
            P("fsdp", None, None),
            P("fsdp"),
            P("fsdp"),
            P("fsdp", "mp"),
            P("mp"),
            P("fsdp", "mp"),
            P("fsdp", "mp"),
            P("mp"),
            P("mp", "fsdp"),
            P("fsdp"),
            P("fsdp"),
            P("fsdp"),
            P("fsdp", "mp"),
            P("mp"),
            P("mp", "fsdp"),
            P("fsdp"),
        ),
        check_vma=False,
    )
```

```python
import functools
import math

import jax
import jax.numpy as jnp
from jax import lax
from jax.experimental import pallas as pl
from jax.experimental.pallas import tpu as pltpu
from jax.sharding import PartitionSpec as P

HD = 24
PAD = 32
MOST = 128
BOTH = ("fsdp", "mp")
EPS = 1e-05
F32 = jnp.float32
BF16 = jnp.bfloat16
LOG2 = math.log2(math.e) / math.sqrt(HD)
SCALE = 1.0 / math.sqrt(HD)
GELU = math.sqrt(2.0 / math.pi)


def send(value, fs, mp, flip_f, flip_m):
    pairs = [(f * mp + m, (f ^ flip_f) * mp + (m ^ flip_m)) for f in range(fs) for m in range(mp)]
    return lax.ppermute(value, BOTH, pairs)


def dot_nn(left, right):
    return lax.dot_general(left, right, (((1,), (0,)), ((), ())), preferred_element_type=F32)


def dot_nt(left, right):
    return lax.dot_general(left, right, (((1,), (1,)), ((), ())), preferred_element_type=F32)


def dot_tn(left, right):
    return lax.dot_general(left, right, (((0,), (0,)), ((), ())), preferred_element_type=F32)


def norm_parts(values):
    centre = jnp.mean(values, axis=-1, keepdims=True)
    centered = values - centre
    inverse = lax.rsqrt(jnp.mean(centered * centered, axis=-1, keepdims=True) + EPS)
    return centered * inverse, inverse


def norm_back(grad, normed, inverse, gain):
    scaled = grad * gain
    return inverse * (
        scaled
        - jnp.mean(scaled, axis=-1, keepdims=True)
        - normed * jnp.mean(scaled * normed, axis=-1, keepdims=True)
    )


def call(body, outs, operands, scratch=(), scalars=0, us=0.1, mib=6):
    whole = pl.BlockSpec(memory_space=pltpu.VMEM)
    few = pl.BlockSpec(memory_space=pltpu.SMEM)
    return pl.pallas_call(
        body,
        out_shape=tuple(jax.ShapeDtypeStruct(s, d) for s, d in outs),
        in_specs=[few] * scalars + [whole] * (len(operands) - scalars),
        out_specs=tuple(whole for _ in outs),
        scratch_shapes=list(scratch),
        name=getattr(body, "func", body).__name__,
        compiler_params=pltpu.CompilerParams(vmem_limit_bytes=mib << 20),
        cost_estimate=pl.CostEstimate(
            flops=int(us * 2e9), transcendentals=0, bytes_accessed=int(us * 3e6)
        ),
    )(*operands)


def fence(*values):
    return lax.optimization_barrier(values)


def tiles(window):
    made = []
    for q0 in range(0, window, 256):
        qn = min(256, window - q0)
        k0 = max(0, q0 - MOST)
        made.append((q0, qn, k0, min(window, q0 + qn + MOST)))
    return made


def permutation(target):
    width = target.shape[1]
    return (lax.broadcasted_iota(jnp.int32, (width, width), 0) == target).astype(BF16)


def cuts_of(segments):
    middle = segments.shape[1] // 2
    held = segments[:, middle : middle + 1]
    first = jnp.sum((segments < held).astype(F32), axis=1, keepdims=True)
    last = jnp.sum((segments <= held).astype(F32), axis=1, keepdims=True)
    return jnp.where(middle - first <= last - middle, first, last)


def start_body(info, hidden, cotangent, segment_ids, pad_flags, target, x_o, c_o, xhat_o, bias_o):
    core, y = info[0], info[1]
    window = x_o.shape[0]
    gap = hidden.shape[1] - window
    start = pl.multiple_of(core * gap, 16)
    segments = segment_ids[...]
    cuts = cuts_of(segments)
    cut = jnp.where(y == 0, cuts[0:1], cuts[1:2])
    here = (start + lax.broadcasted_iota(jnp.int32, (window, 1), 0)).astype(F32)
    before = (here < cut).astype(F32)
    owned = jnp.where(core == 0, before, 1.0 - before)
    perm = permutation(target[...])
    x = dot_nn(hidden[y, pl.ds(start, window), :], perm)
    x_o[...] = x.astype(BF16)
    c_o[...] = (dot_nn(cotangent[y, pl.ds(start, window), :], perm) * owned).astype(BF16)
    xhat_o[...] = norm_parts(x)[0]
    segs = jnp.where(y == 0, segments[0:1], segments[1:2]).astype(F32)
    pads = pad_flags[...]
    pads = jnp.where(y == 0, pads[0:1], pads[1:2])
    code = jnp.where(pads == 0, segs, -1.0)
    segs = jnp.where(core == 0, segs[:, :window], segs[:, gap:])
    wide = bias_o.shape[1]
    if wide > window:
        segs = jnp.concatenate([segs, jnp.full((1, wide - window), -2.0, F32)], axis=1)
    code = jnp.where(core == 0, code[:, :window], code[:, gap:])
    column = jnp.broadcast_to(code, (8, window)).T[:, 0:1]
    key = lax.broadcasted_iota(jnp.int32, (window, wide), 0)
    query = lax.broadcasted_iota(jnp.int32, (window, wide), 1)
    bias_o[...] = jnp.where((column == segs) | (key == query), 0.0, -1e30)


def assemble(blocks, places, high, weights):
    for block, rows in zip(blocks, places):
        for z, row in enumerate(rows):
            for w in range(3):
                weights[w, row : row + high] = block[z, w * high : (w + 1) * high]


def disassemble(value, outs, pick):
    value = value.astype(BF16)
    if len(outs) == 1:
        outs[0][pick] = value
        return
    _, deep, high, _ = outs[0].shape[-4:]
    half = high // 3
    yr, w = pick[:-1], pick[-1]
    for x in range(2):
        for z in range(deep):
            for c in range(2):
                at = ((z * 2 + x) * 2 + c) * half
                outs[c][yr + (x, z, pl.ds(w * half, half))] = value[at : at + half]


def common_order(rows, perm):
    high = rows.astype(BF16)
    rest = rows - high.astype(F32)
    mid = rest.astype(BF16)
    last = (rest - mid.astype(F32)).astype(BF16)
    return dot_nn(high, perm) + dot_nn(mid, perm) + dot_nn(last, perm)


def by_head(value, fill=0.0):
    tokens, columns = value.shape
    parts = value.T.reshape(columns // HD, HD, tokens)
    row = lax.broadcasted_iota(jnp.int32, (columns // HD, PAD - HD, tokens), 1)
    extra = jnp.where(row == 0, fill, 0.0)
    return jnp.concatenate([parts, extra], axis=1).astype(BF16)


def flat_heads(value):
    heads, _, tokens = value.shape
    return value[:, :HD, :].reshape(heads * HD, tokens)


def project_body(places, high, unpack, first, given, *refs):
    blocks = refs[: len(places)]
    refs = refs[len(places) :]
    if not unpack:
        small_i, shift_i = refs[:2]
        refs = refs[2:]
    qt, kt, vt, shift_o = refs[:4]
    weights = refs[-1]
    assemble(blocks, places, high, weights)
    if unpack:
        shifts = blocks[0][0, 3 * high : 3 * high + 16].astype(F32)[0:8]
    else:
        shifts = shift_i[...]
    shift_o[...] = shifts
    if first:
        small_o, n_o, nt_o = refs[4:7]
        if unpack:
            deep = blocks[0].shape[0]
            wide = blocks[0].shape[2] // 4
            rows = [
                [blocks[2 * x][z, 3 * high : 3 * high + 16].astype(F32) for x in range(2)]
                for z in range(deep)
            ]
            made = []
            for p in range(6):
                r, at = 8 + p // 4, p % 4 * wide
                made.append(
                    jnp.concatenate(
                        [rows[z][x][r : r + 1, at : at + wide] for z in range(deep) for x in range(2)],
                        axis=1,
                    )
                )
            made += [jnp.zeros_like(made[0])] * 2
            small = jnp.concatenate(made, axis=0)
        else:
            small = small_i[...]
        small_o[...] = small
        exact = given[...] * small[0:1] + small[1:2]
        normed = exact.astype(BF16)
        n_o[...] = normed
        nt_o[...] = exact.T.astype(BF16)
    else:
        normed = given[...]
    qt[...] = by_head(dot_nn(normed, weights[0]) + shifts[0:1])
    kt[...] = by_head(dot_nn(normed, weights[1]))
    vt[...] = by_head(dot_nn(normed, weights[2]) + shifts[1:2], 1.0)


def forward_body(first, qt, kt, vt, bias, ot, lse):
    heads, _, window = ot.shape
    rows = 4 * PAD

    def four(i, carry):
        h = first + 4 * i
        for q0, qn, k0, k1 in tiles(window):
            query = qt[pl.ds(h, 4), :, q0 : q0 + qn].reshape(rows, qn).astype(F32)
            if qn < 256:
                query = jnp.concatenate([query, jnp.zeros((rows, 256 - qn), F32)], axis=1)
            own = lax.broadcasted_iota(jnp.int32, (rows, 256), 0) // PAD
            block = [jnp.where(own == n, query, 0.0).astype(BF16) for n in range(4)]
            keys = kt[pl.ds(h, 4), :, k0:k1].reshape(rows, k1 - k0)
            values = vt[pl.ds(h, 4), :, k0:k1].reshape(rows, k1 - k0)
            scores = dot_tn(keys, jnp.concatenate(block, axis=1))
            tops, weights = [], []
            for n in range(4):
                part = scores[:, n * 256 : (n + 1) * 256] * LOG2 + bias[k0:k1, q0 : q0 + 256]
                top = jnp.max(part, axis=0, keepdims=True)
                tops.append(top)
                weights.append(jnp.exp2(part - top).astype(BF16))
            mixed = dot_nn(values, jnp.concatenate(weights, axis=1))
            for n in range(4):
                own_mixed = mixed[n * PAD : (n + 1) * PAD, n * 256 : n * 256 + qn]
                total = own_mixed[HD : HD + 1]
                ot[4 * i + n, :, q0 : q0 + qn] = own_mixed / total
                lse[4 * i + n, :, q0 : q0 + qn] = tops[n][:, :qn] + jnp.log2(total)
        return carry

    lax.fori_loop(0, heads // 4, four, 0)


def feed_body(places, high, x_r, o00, o01, o1, small, cols0, cols1, target, *refs):
    count = len(places)
    blocks = refs[: 2 * count]
    refs = refs[2 * count :]
    out_o, xhat_o, inv_o, n_o = refs[:4]
    atts, acts, slopes, weights = refs[4:6], refs[6:8], refs[8:10], refs[10:]
    for yr in range(2):
        assemble(blocks[yr * count : (yr + 1) * count], places, high, weights[yr])
    atts[0][...] = jnp.concatenate([flat_heads(o00[...]), flat_heads(o01[...])], axis=0).T.astype(BF16)
    atts[1][...] = flat_heads(o1[...]).T.astype(BF16)
    x = x_r[...].astype(F32)
    middle = x + dot_nt(atts[0][...], weights[0][0]) + dot_nt(atts[1][...], weights[1][0]) + small[2:3]
    xhat, inverse = norm_parts(middle)
    xhat_o[...] = xhat
    inv_o[...] = inverse
    normed = (xhat * small[3:4] + small[4:5]).astype(BF16)
    n_o[...] = normed
    result = middle + small[5:6]
    for yr, cols in enumerate((cols0, cols1)):
        pre = dot_nn(normed, weights[yr][1]) + cols[2:3]
        square = pre * pre
        bent = jnp.tanh(GELU * (pre + 0.044715 * (pre * square)))
        act = (0.5 * pre * (1.0 + bent)).astype(BF16)
        acts[yr][...] = act
        slopes[yr][...] = 0.5 * (1.0 + bent) + 0.5 * pre * (1.0 - bent * bent) * (
            GELU * (1.0 + 3.0 * 0.044715 * square)
        )
        result = result + dot_nt(act, weights[yr][2])
    out_o[...] = dot_nn(result.astype(BF16), permutation(target[...])).astype(BF16)


def rows_of(info, feats, units):
    width = feats.shape[1]
    cols = width // 2
    made = []
    for i in range(feats.shape[0]):
        made += [feats[i : i + 1, :cols], feats[i : i + 1, cols:]]
    for own, other in units:
        made += [jnp.where(info[1] == 0, own, other), jnp.where(info[1] == 0, other, own)]
    return jnp.concatenate(made, axis=0)


def feed_back_body(places, high, parts, info, c_r, xhat_r, inv_r, n_r, a0, a1, act0, act1, slope0, slope1, small, target, *refs):
    count = len(places)
    blocks = refs[: 2 * count]
    refs = refs[2 * count :]
    mid_o, d0, d1, sum_o = refs[:4]
    outs = refs[4 : 4 + parts]
    weights = refs[4 + parts :]
    for yr in range(2):
        assemble(blocks[yr * count : (yr + 1) * count], places, high, weights[yr])
    ct_low, normed = c_r[...], n_r[...]
    cols = act0.shape[1]

    def both(left, right, w):
        grads = dot_tn(left, jnp.concatenate(right, axis=1))
        for yr in range(2):
            disassemble(grads[:, yr * cols : (yr + 1) * cols], outs, (yr, w))

    both(ct_low, [act0[...], act1[...]], 2)
    dpres = [
        (dot_nn(ct_low, weights[yr][2]) * slope[...]).astype(BF16) for yr, slope in enumerate((slope0, slope1))
    ]
    both(normed, dpres, 1)
    ups = [jnp.sum(dpre.astype(F32), axis=0, keepdims=True) for dpre in dpres]
    dnorm = dot_nt(dpres[0], weights[0][1]) + dot_nt(dpres[1], weights[1][1])
    ct, xhat = ct_low.astype(F32), xhat_r[...]
    dmiddle = ct + norm_back(dnorm, xhat, inv_r[...], small[3:4])
    mid_o[...] = dmiddle
    sums = [jnp.sum(part, axis=0, keepdims=True) for part in (dmiddle, dnorm * xhat, dnorm, ct)]
    sums = common_order(
        jnp.concatenate(sums + [jnp.zeros((4, dnorm.shape[1]), F32)], axis=0), permutation(target[...])
    )
    sums = rows_of(info, sums[0:4], [ups])
    sum_o[...] = jnp.concatenate([sums, jnp.zeros_like(sums[0:6])], axis=0)
    low = dmiddle.astype(BF16)
    both(low, [a0[...], a1[...]], 0)
    for yr in range(2):
        (d0, d1)[yr][...] = by_head(dot_nn(low, weights[yr][0]))


def backward_body(first, mixed, qt, kt, vt, dt, ot, lse, bias, dq_o, dk_o, dv_o, dq, dk, dv):
    heads, _, window = dq.shape
    made = tiles(window)

    def head(i, carry):
        h = first + i
        delta = jnp.sum(dt[h].astype(F32) * ot[mixed + i], axis=0, keepdims=True)
        for ref in (dk, dv):
            ref[i] = jnp.zeros_like(ref[i])
        for q0, qn, k0, k1 in made:
            query, grad = qt[h, :, q0 : q0 + qn], dt[h, :, q0 : q0 + qn]
            scores = dot_tn(kt[h, :, k0:k1], query)
            dprobs = dot_tn(vt[h, :, k0:k1], grad)
            probs = jnp.exp2(scores * LOG2 + (bias[k0:k1, q0 : q0 + qn] - lse[mixed + i, :, q0 : q0 + qn]))
            dscores = (probs * (dprobs - delta[:, q0 : q0 + qn])).astype(BF16)
            dq[i, :, q0 : q0 + qn] = dot_nn(kt[h, :, k0:k1], dscores)
            dk[i, :, k0:k1] += dot_nt(query, dscores)
            dv[i, :, k0:k1] += dot_nt(grad, probs.astype(BF16))
        return carry

    lax.fori_loop(0, heads, head, 0, unroll=2)
    for ref, out, factor in ((dq, dq_o, SCALE), (dk, dk_o, SCALE), (dv, dv_o, 1.0)):
        out[...] = (flat_heads(ref[...]) * factor).astype(BF16)


def weigh_body(places, high, parts, nt_r, qa, ka, va, qb, kb, vb, *refs):
    blocks = refs[: len(places)]
    refs = refs[len(places) :]
    dn, sums = refs[:2]
    outs = refs[2 : 2 + parts]
    weights = refs[2 + parts]
    assemble(blocks, places, high, weights)
    normed = nt_r[...]
    ones = jnp.ones((8, normed.shape[1]), BF16)
    total = None
    for w, (a, b) in enumerate(((qa, qb), (ka, kb), (va, vb))):
        low = jnp.concatenate([a[...], b[...]], axis=0)
        disassemble(dot_nt(normed, low), outs, (w,))
        part = dot_nn(weights[w], low)
        total = part if total is None else total + part
        if w != 1:
            sums[w // 2 : w // 2 + 1] = dot_nt(ones, low)[0:1]
    dn[...] = total


def finish_body(info, dn0, dn1, x_r, mid, small, target, qv0, qv1, out_o, sum_o):
    perm = permutation(target[...])
    grad = (dn0[...] + dn1[...]).T
    xhat, inverse = norm_parts(x_r[...].astype(F32))
    dx = mid[...] + norm_back(grad, xhat, inverse, small[0:1])
    out_o[...] = dot_nn(dx.astype(BF16), perm).astype(BF16)
    sums = [jnp.sum(part, axis=0, keepdims=True) for part in (grad * xhat, grad)]
    sums = common_order(jnp.concatenate(sums + [jnp.zeros((6, grad.shape[1]), F32)], axis=0), perm)
    sum_o[...] = rows_of(info, sums[0:2], [(qv0[w : w + 1], qv1[w : w + 1]) for w in range(2)])


def deal_body(info, wo, wu, wd, mine, theirs):
    half = mine.shape[1]
    values = [wo[...].astype(F32).T.astype(BF16), wu[...], wd[...].astype(F32).T.astype(BF16)]

    @pl.when(info[0] == 0)
    def _():
        for w, value in enumerate(values):
            mine[w], theirs[w] = value[:half], value[half:]

    @pl.when(info[0] != 0)
    def _():
        for w, value in enumerate(values):
            theirs[w], mine[w] = value[:half], value[half:]


def meet_a_body(info, mine, got, small, units, units_pair, first):
    half = got.shape[1]
    wr, wc = small.shape[1], units.shape[1]
    zeros = jnp.zeros((8, 4 * wr), F32)

    def meet(own_first):
        def pair(own, other):
            return jnp.concatenate([own, other] if own_first else [other, own], axis=1)

        for w in range(3):
            first[0, w * half : (w + 1) * half, :] = pair(mine[w], got[w])
        params = small[...].astype(F32)
        if not own_first:
            params = jnp.concatenate([params[:, half:], params[:, :half]], axis=1)
        above = jnp.concatenate([params[p : p + 1] for p in range(4)], axis=1)
        below = jnp.concatenate([params[4:5], params[5:6], zeros[0:1, : 2 * wr]], axis=1)
        both = pair(units[...], units_pair[...]).astype(F32)
        extra = jnp.concatenate([both, zeros[:5], above, below, zeros[:6]], axis=0)
        first[0, 3 * half : 3 * half + 16, :] = extra.astype(BF16)

    @pl.when(info[0] == 0)
    def _():
        meet(True)

    @pl.when(info[0] != 0)
    def _():
        meet(False)


def meet_b_body(info, mine, got, second):
    half = got.shape[1]

    def meet(low, high):
        for w in range(3):
            second[0, w * half : (w + 1) * half, :] = jnp.concatenate([low[w], high[w]], axis=1)

    @pl.when(info[0] == 0)
    def _():
        meet(mine, got)

    @pl.when(info[0] != 0)
    def _():
        meet(got, mine)


def stack_body(*refs):
    out = refs[-1]
    for at, ref in enumerate(refs[:-1]):
        out[at] = ref[0]


def pack(out, row, sums):
    count = sums.shape[0]
    high = sums.astype(BF16)
    out[row : row + count] = high
    out[row + count : row + 2 * count] = (sums - high.astype(F32)).astype(BF16)


def unpack_sums(ref, row, count):
    both = ref[row : row + 2 * count].astype(F32)
    return both[:count] + both[count:]


def block_sums(keep, got, out, row):
    deep, high, _ = keep.shape
    for z in range(deep):
        total = keep[z].astype(F32) + got[z].astype(F32)
        out[row + z * high : row + (z + 1) * high] = total.astype(BF16)


def far_b_body(keep, got, sums, sums_got, out, sum_o):
    total = sums[...] + sums_got[...]
    sum_o[...] = total
    for x in range(2):
        block_sums(keep.at[1, x], got.at[1, x], out, x * (out.shape[0] - 32) // 2)
    pack(out, out.shape[0] - 32, total)


def far_a_body(keep, got, out0, out1):
    block_sums(keep.at[0], got.at[0], out0, 0)
    block_sums(keep.at[1], got.at[1], out1, 0)


def pass_on(keep, got, far, out):
    deep, high, _ = keep.shape
    for z in range(deep):
        rows = slice(z * high, (z + 1) * high)
        total = keep[z].astype(F32) + got[z].astype(F32) + far[rows].astype(F32)
        out[rows] = total.astype(BF16)


def near_b_body(keep, got, far, sums, out, sum_o):
    count = out.shape[0] - 32
    pass_on(keep.at[0, 1], got.at[0, 1], far.at[count : 2 * count], out)
    total = sums[...] + unpack_sums(far, 2 * count, 16)
    sum_o[...] = total
    pack(out, count, total)


def near_a_body(keep, got, far, sums, sums_got, out, sum_o):
    pass_on(keep.at[1], got.at[1], far, out)
    total = sums[...] + sums_got[...]
    sum_o[...] = total
    pack(out, out.shape[0] - 16, total)


def block_total(keep, got, far, passed, z):
    rows = slice(z * keep.shape[1], (z + 1) * keep.shape[1])
    return keep[z].astype(F32) + got[z].astype(F32) + far[rows].astype(F32) + passed[rows].astype(F32)


def high_b_body(keep, got, far, passed, sums, own, out, sum_o):
    kept, given = keep.at[0, 0], got.at[0, 0]
    deep, high, _ = kept.shape
    total = sums[...] + unpack_sums(passed, deep * high, sums.shape[0])
    sum_o[...] = total
    for z in range(deep):
        value = block_total(kept, given, far, passed, z)
        if z < deep // 2:
            own[z] = value
        else:
            out[(z - deep // 2) * high : (z - deep // 2 + 1) * high] = value.astype(BF16)
    pack(out, deep // 2 * high, total)


def middle_b_body(own, got, sums, own_o, out, sum_o):
    _, high, _ = own.shape
    total = sums[...] + unpack_sums(got, 2 * high, sums.shape[0])
    sum_o[...] = total
    own_o[...] = own[0] + got[0:high].astype(F32)
    out[0:high] = (own[1] + got[high : 2 * high].astype(F32)).astype(BF16)
    pack(out, high, total)


def high_a_body(keep, got, far, passed, sums, *outs):
    kept, given = keep.at[0], got.at[0]
    deep, high, _ = kept.shape
    total = sums[...] + unpack_sums(passed, deep * high, sums.shape[0])
    outs[-1][...] = total
    for z in range(deep):
        value = block_total(kept, given, far, passed, z)
        if z == 0:
            outs[0][...] = value
        else:
            outs[z][0:high] = value.astype(BF16)
            pack(outs[z], high, total)


def last_body(info, own, sums, *refs):
    parts, (mine, theirs, sum_o) = refs[:-3], refs[-3:]
    high = own.shape[0]
    half = high // 3
    total, wide = own[...], sums[...]
    for part in parts:
        total = total + part[0:high].astype(F32)
        wide = wide + unpack_sums(part, high, sums.shape[0])
    sum_o[...] = wide
    wc = mine.shape[2]

    def give(low, upper):
        for w in range(3):
            low[w] = total[w * half : (w + 1) * half, :wc]
            upper[w] = total[w * half : (w + 1) * half, wc:]

    @pl.when(info[0] == 0)
    def _():
        give(mine, theirs)

    @pl.when(info[0] != 0)
    def _():
        give(theirs, mine)


def deliver_body(turned, info, mine, got, *outs):
    half = mine.shape[1]

    def deliver(low, high):
        for w, out in enumerate(outs):
            if turned[w]:
                out[...] = jnp.concatenate([low[w], high[w]], axis=0).T
            else:
                out[0:half] = low[w]
                out[half:] = high[w]

    @pl.when(info[0] == 0)
    def _():
        deliver(mine, got)

    @pl.when(info[0] != 0)
    def _():
        deliver(got, mine)


def join_body(info, segment_ids, own, beside, across, corner, out):
    core, y = info[0], info[1]
    length, window = out.shape[1], own.shape[0]
    gap = length - window
    cuts = cuts_of(segment_ids[...])
    own_cut = jnp.where(y == 0, cuts[0:1], cuts[1:2])
    other_cut = jnp.where(y == 0, cuts[1:2], cuts[0:1])

    def row(low, high, place, cut):
        out[place, 0:gap] = low[0:gap]
        at = (gap + lax.broadcasted_iota(jnp.int32, (window - gap, 1), 0)).astype(F32)
        seam = jnp.where(at < cut, low[gap:window].astype(F32), high[0 : window - gap].astype(F32))
        out[place, gap:window] = seam.astype(BF16)
        out[place, window:length] = high[window - gap : window]

    @pl.when(core == 0)
    def _():
        row(own, beside, y, own_cut)
        row(across, corner, 1 - y, other_cut)

    @pl.when(core != 0)
    def _():
        row(beside, own, y, own_cut)
        row(corner, across, 1 - y, other_cut)


def per_device(
    hidden_in,
    segment_ids,
    pad_flags,
    gain1,
    shift1,
    w_query,
    b_query,
    w_key,
    w_value,
    b_value,
    w_out,
    b_out,
    gain2,
    shift2,
    w_up,
    b_up,
    w_down,
    b_down,
    cotangent,
):
    fs, mp = lax.axis_size("fsdp"), lax.axis_size("mp")
    rows, length, width = hidden_in.shape
    wr, wc = w_query.shape
    half, cols = wr // 2, 2 * wc
    heads = cols // HD
    f, m = lax.axis_index("fsdp"), lax.axis_index("mp")
    core, y = m % 2, m // 2
    side = jnp.stack([core, y])
    window = length // 2 + MOST // 2
    deep = fs // 2
    flips = [2 * z for z in range(1, deep)]
    staged = half % 16 == 0 and deep == 4
    if staged:
        places = [[((z * 2 + x) * 2 + c) * half for z in range(deep)] for x in range(2) for c in range(2)]
        high, parts = half, 2
    else:
        places, high, parts = [[0]], width, 1
    wide, tall = (window, width), (width, window)
    by_heads, by_few = (heads, PAD, window), (heads // 2, PAD, window)
    weights = pltpu.VMEM((3, width, cols), BF16)

    def to(value, flip_f, flip_m):
        return send(value, fs, mp, flip_f, flip_m)

    def begin(target):
        return call(
            start_body,
            [(wide, BF16), (wide, BF16), (wide, F32), ((window, -(-window // 256) * 256), F32)],
            [side, hidden_in, cotangent, segment_ids, pad_flags, target],
            (),
            1,
            us=3,
            mib=4,
        )

    def project(given, blocks, first, extra=()):
        outs = [(by_heads, BF16)] * 3 + [((8, cols), F32)]
        if first:
            outs += [((8, width), F32), (wide, BF16), (tall, BF16)]
        return call(
            functools.partial(project_body, places, high, not extra, first),
            outs,
            [given] + blocks + list(extra),
            [weights],
            us=2,
            mib=4,
        )

    def attend(part, qkv_heads, bias):
        first, count = (0, heads) if part is None else (part * (heads // 2), heads // 2)
        return call(
            functools.partial(forward_body, first),
            [((count, PAD, window), F32), ((count, 1, window), F32)],
            list(qkv_heads) + [bias],
            us=5,
        )

    def feed(x, mixed, small, shifts, target, blocks):
        units_shape = (window, cols)
        return call(
            functools.partial(feed_body, places, high),
            [(wide, BF16), (wide, F32), ((window, 1), F32), (wide, BF16)]
            + [(units_shape, BF16)] * 4
            + [(units_shape, F32)] * 2,
            [x] + mixed + [small] + shifts + [target] + blocks,
            [weights, weights],
            us=5,
            mib=7,
        )

    def feed_back(side, ct, made, small, target, blocks):
        if staged:
            grads = [((2, 2, deep, 3 * half, cols), BF16)] * 2
        else:
            grads = [((2, 3, width, cols), BF16)]
        return call(
            functools.partial(feed_back_body, places, high, parts),
            [(wide, F32), (by_heads, BF16), (by_heads, BF16), ((16, cols), F32)] + grads,
            [side, ct] + list(made) + [small, target] + blocks,
            [weights, weights],
            1,
            us=7,
            mib=10,
        )

    def backward(part, qkv_heads, da, o, lse, bias):
        return call(
            functools.partial(backward_body, part * (heads // 2), part * (heads // 2) if o.shape[0] == heads else 0),
            [((heads // 2 * HD, window), BF16)] * 3,
            list(qkv_heads) + [da, o, lse, bias],
            [pltpu.VMEM(by_few, F32)] * 3,
            us=15,
        )

    def weigh(normed_t, blocks, low_a, low_b):
        if staged:
            grads = [((2, deep, 3 * half, cols), BF16)] * 2
        else:
            grads = [((3, width, cols), BF16)]
        return call(
            functools.partial(weigh_body, places, high, parts),
            [(tall, F32), ((2, cols), F32)] + grads,
            [normed_t] + list(low_a) + list(low_b) + blocks,
            [weights],
            us=0.1,
        )

    def finish(side, dn0, dn1, x, dmiddle, small, target, qv0, qv1):
        return call(
            finish_body,
            [(wide, BF16), ((8, cols), F32)],
            [side, dn0, dn1, x, dmiddle, small, target, qv0, qv1],
            (),
            1,
            us=20,
            mib=5,
        )

    def join(own, beside, across, corner):
        operands = [side, segment_ids, own, beside, across, corner]
        return call(join_body, [((rows, length, width), BF16)], operands, (), 1, us=20)[0]

    if not staged:

        def gathered(blocks):
            full = []
            for block in blocks:
                block = lax.all_gather(block, "fsdp", axis=0, tiled=True)
                full.append(lax.all_gather(block, "mp", axis=1, tiled=True))
            full = jnp.stack(full)
            return [full[:, :, yr * cols : (yr + 1) * cols].reshape(1, 3 * width, cols) for yr in range(2)]

        target = lax.iota(jnp.int32, width)[None]
        wa = gathered([w_query, w_key, w_value])
        wb = gathered([w_out.T, w_up, w_down.T])
        small = jnp.stack([gain1, shift1, b_out, gain2, shift2, b_down] + [jnp.zeros_like(gain1)] * 2)
        small = lax.all_gather(small, "fsdp", axis=1, tiled=True).astype(F32)
        units = jnp.stack([b_query, b_value, b_up] + [jnp.zeros_like(b_up)] * 5)
        units = lax.all_gather(units, "mp", axis=1, tiled=True).astype(F32)
        units = [units[:, :cols], units[:, cols:]]
        x, ct, xhat, bias = begin(target)
        *heads0, _, _, normed, normed_t = project(xhat, [wa[0]], True, (small, units[0]))
        *heads1, _ = project(normed, [wa[1]], False, (small, units[1]))
        both = (heads0, heads1)
        mixed = [attend(0, heads0, bias), attend(1, heads0, bias)] + [attend(None, heads1, bias)] * 2
        made = feed(x, [o for o, _ in mixed[:3]], small, units, target, wb)
        result = made[0]
        none = jnp.zeros_like(side)
        dmiddle, da0, da1, sums_b, grads_b = feed_back(none, ct, made[1:], small, target, wb)
        dn, qv, grads_a = [], [], []
        for yr, da in enumerate((da0, da1)):
            lows = [backward(part, both[yr], da, *mixed[2 * yr + part], bias) for part in range(2)]
            got = weigh(normed_t, [wa[yr]], *lows)
            dn.append(got[0])
            qv.append(got[1])
            grads_a.append(got[2])
        grad_window, sums_a = finish(none, dn[0], dn[1], x, dmiddle, small, target, *qv)

        def scattered(pair):
            full = jnp.concatenate(pair, axis=2).astype(F32)
            full = lax.psum_scatter(full, "mp", scatter_dimension=2, tiled=True)
            return lax.psum_scatter(full, "fsdp", scatter_dimension=1, tiled=True)

        grad_q, grad_k, grad_v = scattered(grads_a)
        grad_out, grad_up, grad_down = scattered([grads_b[0], grads_b[1]])
        grad_out, grad_down = grad_out.T, grad_down.T
        sums_a, sums_b = sums_a.reshape(4, width), sums_b.reshape(8, width)
        sums = jnp.concatenate([sums_a[0:2], sums_b[0:4], sums_a[2:4], sums_b[4:5]])
        sums = lax.psum(sums, BOTH)
        mine_f = lax.dynamic_slice(sums, (0, f * wr), (6, wr))
        mine_u = lax.dynamic_slice(sums, (6, m * wc), (3, wc))

        def shared(value):
            across = to(value, 0, 2)
            return join(value, to(value, 0, 1), across, to(across, 0, 1))

        out_hidden, grad_hidden = shared(result), shared(grad_window)
    else:
        piece_a, piece_b = (1, 3 * half + 16, cols), (1, 3 * half, cols)

        def stacked(pieces):
            return call(stack_body, [((deep,) + pieces[0].shape[1:], BF16)], pieces)[0]

        def part(block, of):
            return lax.dynamic_slice(block, (of * half, 0), (half, wc))

        theirs = jnp.stack([part(w, 1 - core) for w in (w_query, w_key, w_value)])
        got = to(theirs, 0, 1)
        theirs, gain1, b_query, w_query, w_key, w_value = fence(theirs, gain1, b_query, w_query, w_key, w_value)
        mine = jnp.stack([part(w, core) for w in (w_query, w_key, w_value)])
        small = jnp.stack([gain1, shift1, b_out, gain2, shift2, b_down])
        units = jnp.concatenate([b_query, b_value, b_up]).reshape(3, wc)
        units_pair = to(units, 0, 1)
        feature = lax.iota(jnp.int32, width)
        target = (((feature // half) ^ (f * 2 + core)) * half + feature % half)[None]
        got, units_pair, small, mine = fence(got, units_pair, small, mine)

        first = call(
            meet_a_body, [(piece_a, BF16)], [side, mine, got, small, units, units_pair], (), 1
        )[0]
        first_parts = [to(first, flip, 0) for flip in flips]
        first, w_out, w_up, w_down = fence(first, w_out, w_up, w_down)
        mine, theirs = call(deal_body, [((3, half, wc), BF16)] * 2, [side, w_out, w_up, w_down], (), 1)
        got = to(theirs, 0, 1)
        second = call(meet_b_body, [(piece_b, BF16)], [side, mine, got], (), 1)[0]
        first, first_parts, second, hidden_in, target = fence(first, first_parts, second, hidden_in, target)

        qkv = stacked([first] + first_parts)
        qkv_x, qkv_y = to(qkv, 1, 0), to(qkv, 0, 2)
        second_parts = [to(second, flip, 0) for flip in flips]
        x, ct, xhat, bias = begin(target)
        second_parts, second, qkv, qkv_x, qkv_y, xhat = fence(second_parts, second, qkv, qkv_x, qkv_y, xhat)
        qkv_xy = to(qkv, 1, 2)

        qkv_c, qkv_xc = to(qkv, 0, 1), to(qkv_x, 0, 1)
        odu = stacked([second] + second_parts)
        near = [qkv, qkv_c, qkv_x, qkv_xc]
        *heads0, shift0, small, normed, normed_t = project(xhat, near, True)
        heads0, qkv_y, odu = fence(heads0, qkv_y, odu)
        qkv_yc, odu_x, odu_y, odu_xy = to(qkv_y, 0, 1), to(odu, 1, 0), to(odu, 0, 2), to(odu, 1, 2)
        o00, l00 = attend(0, heads0, bias)
        o00, heads0, qkv_yc, qkv_xy, odu = fence(o00, heads0, qkv_yc, qkv_xy, odu)
        qkv_xyc, odu_c = to(qkv_xy, 0, 1), to(odu, 0, 1)
        o01, l01 = attend(1, heads0, bias)
        o01, qkv_xyc, odu_c, normed = fence(o01, qkv_xyc, odu_c, normed)
        far = [qkv_y, qkv_yc, qkv_xy, qkv_xyc]
        *heads1, shift1u = project(normed, far, False)
        o1, l1 = attend(None, heads1, bias)
        o1, odu_x, odu_y = fence(o1, odu_x, odu_y)
        odu_xc, odu_yc = to(odu_x, 0, 1), to(odu_y, 0, 1)
        o1, odu_xc, odu_yc, odu_xy = fence(o1, odu_xc, odu_yc, odu_xy)
        odu_xyc = to(odu_xy, 0, 1)

        odu_blocks = [odu, odu_c, odu_x, odu_xc, odu_y, odu_yc, odu_xy, odu_xyc]
        made = fence(*feed(x, [o00, o01, o1], small, [shift0, shift1u], target, odu_blocks))
        result = made[0]
        res_c, res_y = to(result, 0, 1), to(result, 0, 2)
        made = feed_back(side, ct, made[1:], small, target, odu_blocks)
        dmiddle, da0, da1, b_sums, b_keep, b_send, res_c = fence(*made, res_c)

        n_far, n_near = 2 * deep * 3 * half, deep * 3 * half
        f32_16, f32_8 = ((16, cols), F32), ((8, cols), F32)
        b_got, b_sums_got = to(b_send, 0, 1), to(b_sums, 0, 1)
        low10 = backward(0, heads1, da1, o1, l1, bias)
        low10, heads1, b_got, b_sums_got = fence(low10, heads1, b_got, b_sums_got)
        b_far, b_sums = call(
            far_b_body,
            [((n_far + 32, cols), BF16), f32_16],
            [b_keep, b_got, b_sums, b_sums_got],
        )
        b_far = to(b_far, 0, 2)
        low11 = backward(1, heads1, da1, o1, l1, bias)
        low11, normed_t = fence(low11, normed_t)
        dn1, qv1, keep1, send1 = weigh(normed_t, far, low10, low11)
        dn1, keep1, send1, da0, res_y = fence(dn1, keep1, send1, da0, res_y)
        got1, res_yc = to(send1, 0, 1), to(res_y, 0, 1)
        low00 = backward(0, heads0, da0, o00, l00, bias)
        low00, heads0, got1, res_yc = fence(low00, heads0, got1, res_yc)
        a_far0, a_far1 = call(far_a_body, [((n_near, cols), BF16)] * 2, [keep1, got1])
        a_far0, a_far1, heads0 = fence(a_far0, a_far1, heads0)
        a_far1, a_far0 = to(a_far1, 0, 2), to(a_far0, 0, 2)
        low01 = backward(1, heads0, da0, o01, l01, bias)
        low01, normed_t, b_far = fence(low01, normed_t, b_far)
        b_x, b_sums = call(
            near_b_body, [((n_near + 32, cols), BF16), f32_16], [b_keep, b_got, b_far, b_sums]
        )
        b_x = to(b_x, 1, 0)
        dn0, qv0, keep0, send0 = weigh(normed_t, near, low00, low01)
        dn0, keep0, send0, dmiddle = fence(dn0, keep0, send0, dmiddle)
        got0 = to(send0, 0, 1)
        n_two = 2 * 3 * half
        grad_window, a_sums = finish(side, dn0, dn1, x, dmiddle, small, target, qv0, qv1)
        grad_window, a_sums, got0, a_far1, b_x = fence(grad_window, a_sums, got0, a_far1, b_x)

        gw_y, gw_c, a_sums_got = to(grad_window, 0, 2), to(grad_window, 0, 1), to(a_sums, 0, 1)
        a_sums_got, gw_c, keep0 = fence(a_sums_got, gw_c, keep0)
        a_x, a_sums = call(
            near_a_body, [((n_near + 16, cols), BF16), f32_8], [keep0, got0, a_far1, a_sums, a_sums_got]
        )
        a_x, b_keep = fence(a_x, b_keep)
        a_x = to(a_x, 1, 0)
        b_own, b_z2, b_sums = call(
            high_b_body,
            [((2, 3 * half, cols), F32), ((n_two + 32, cols), BF16), f32_16],
            [b_keep, b_got, b_far, b_x, b_sums],
        )
        b_z2, result = fence(b_z2, result)
        b_z2 = to(b_z2, 4, 0)
        out_hidden = join(result, res_c, res_y, res_yc)
        b_z2, out_hidden = fence(b_z2, out_hidden)

        def last(own, sums, got, kind):
            return call(last_body, [((3, half, wc), F32)] * 2 + [kind], [side, own, sums] + got, (), 1, us=20)

        def deliver(mine, got, turned):
            shapes = [((wc, wr) if t else (wr, wc), F32) for t in turned]
            return call(functools.partial(deliver_body, turned), shapes, [side, mine, got], (), 1)

        b_own, b_z1, b_sums = call(
            middle_b_body,
            [((3 * half, cols), F32), ((3 * half + 32, cols), BF16), f32_16],
            [b_own, b_z2, b_sums],
            us=20,
        )
        b_z1, a_x, a_far0, keep0 = fence(b_z1, a_x, a_far0, keep0)
        a_split = call(
            high_a_body,
            [((3 * half, cols), F32)] + [((3 * half + 16, cols), BF16)] * (deep - 1) + [f32_8],
            [keep0, got0, a_far0, a_x, a_sums],
        )
        a_split, b_z1, b_own = fence(a_split, b_z1, b_own)
        a_high = [to(part, flip, 0) for part, flip in zip(a_split[1:-1], flips)]
        b_z1 = to(b_z1, 2, 0)
        b_z1, gw_y = fence(b_z1, gw_y)
        b_mine, b_theirs, b_sums = last(b_own, b_sums, [b_z1], f32_16)
        b_last, gw_yc = to(b_theirs, 0, 1), to(gw_y, 0, 1)
        grad_hidden = join(grad_window, gw_c, gw_y, gw_yc)
        b_last, grad_hidden = fence(b_last, grad_hidden)
        grad_out, grad_up, grad_down = deliver(b_mine, b_last, (True, False, True))
        a_own, a_high, grad_out, grad_hidden = fence(a_split[0], a_high, grad_out, grad_hidden)
        a_mine, a_theirs, a_sums = last(a_own, a_split[-1], a_high, f32_8)
        a_last = to(a_theirs, 0, 1)
        a_sums = a_sums + to(a_sums, 0, 2)
        grad_q, grad_k, grad_v = deliver(a_mine, a_last, (False, False, False))
        sums = jnp.concatenate(
            [
                a_sums.reshape(4, width)[0:2],
                b_sums.reshape(8, width)[0:4],
                a_sums.reshape(4, width)[2:4],
                b_sums.reshape(8, width)[4:5],
            ]
        )
        mine_f = lax.dynamic_slice(sums, (0, f * wr), (6, wr))
        mine_u = lax.dynamic_slice(sums, (6, m * wc), (3, wc))
    return (
        out_hidden,
        grad_hidden,
        mine_f[0],
        mine_f[1],
        grad_q,
        mine_u[0],
        grad_k,
        grad_v,
        mine_u[1],
        grad_out,
        mine_f[2],
        mine_f[3],
        mine_f[4],
        grad_up,
        mine_u[2],
        grad_down,
        mine_f[5],
    )


def solution(mesh):
    return jax.shard_map(
        per_device,
        mesh=mesh,
        in_specs=(
            P("fsdp", None, None),
            P("fsdp", None),
            P("fsdp", None),
            P("fsdp"),
            P("fsdp"),
            P("fsdp", "mp"),
            P("mp"),
            P("fsdp", "mp"),
            P("fsdp", "mp"),
            P("mp"),
            P("mp", "fsdp"),
            P("fsdp"),
            P("fsdp"),
            P("fsdp"),
            P("fsdp", "mp"),
            P("mp"),
            P("mp", "fsdp"),
            P("fsdp"),
            P("fsdp", None, None),
        ),
        out_specs=(
            P("fsdp", None, None),
            P("fsdp", None, None),
            P("fsdp"),
            P("fsdp"),
            P("fsdp", "mp"),
            P("mp"),
            P("fsdp", "mp"),
            P("fsdp", "mp"),
            P("mp"),
            P("mp", "fsdp"),
            P("fsdp"),
            P("fsdp"),
            P("fsdp"),
            P("fsdp", "mp"),
            P("mp"),
            P("mp", "fsdp"),
            P("fsdp"),
        ),
        check_vma=False,
    )
```

```python
import functools
import math

import jax
import jax.numpy as jnp
from jax import lax
from jax.experimental import pallas as pl
from jax.experimental.pallas import tpu as pltpu
from jax.sharding import PartitionSpec as P

HD = 24
PAD = 32
MOST = 128
BOTH = ("fsdp", "mp")
EPS = 1e-05
F32 = jnp.float32
BF16 = jnp.bfloat16
LOG2 = math.log2(math.e) / math.sqrt(HD)
SCALE = 1.0 / math.sqrt(HD)
GELU = math.sqrt(2.0 / math.pi)


def send(value, fs, mp, flip_f, flip_m):
    pairs = [(f * mp + m, (f ^ flip_f) * mp + (m ^ flip_m)) for f in range(fs) for m in range(mp)]
    return lax.ppermute(value, BOTH, pairs)


def dot_nn(left, right):
    return lax.dot_general(left, right, (((1,), (0,)), ((), ())), preferred_element_type=F32)


def dot_nt(left, right):
    return lax.dot_general(left, right, (((1,), (1,)), ((), ())), preferred_element_type=F32)


def dot_tn(left, right):
    return lax.dot_general(left, right, (((0,), (0,)), ((), ())), preferred_element_type=F32)


def norm_parts(values):
    centre = jnp.mean(values, axis=-1, keepdims=True)
    centered = values - centre
    inverse = lax.rsqrt(jnp.mean(centered * centered, axis=-1, keepdims=True) + EPS)
    return centered * inverse, inverse


def norm_back(grad, normed, inverse, gain):
    scaled = grad * gain
    return inverse * (
        scaled
        - jnp.mean(scaled, axis=-1, keepdims=True)
        - normed * jnp.mean(scaled * normed, axis=-1, keepdims=True)
    )


def call(body, outs, operands, scratch=(), scalars=0, us=0.1, mib=6):
    whole = pl.BlockSpec(memory_space=pltpu.VMEM)
    few = pl.BlockSpec(memory_space=pltpu.SMEM)
    return pl.pallas_call(
        body,
        out_shape=tuple(jax.ShapeDtypeStruct(s, d) for s, d in outs),
        in_specs=[few] * scalars + [whole] * (len(operands) - scalars),
        out_specs=tuple(whole for _ in outs),
        scratch_shapes=list(scratch),
        name=getattr(body, "func", body).__name__,
        compiler_params=pltpu.CompilerParams(vmem_limit_bytes=mib << 20),
        cost_estimate=pl.CostEstimate(
            flops=int(us * 2e9), transcendentals=0, bytes_accessed=int(us * 3e6)
        ),
    )(*operands)


def fence(*values):
    return lax.optimization_barrier(values)


def tiles(window):
    made = []
    for q0 in range(0, window, 256):
        qn = min(256, window - q0)
        k0 = max(0, q0 - MOST)
        made.append((q0, qn, k0, min(window, q0 + qn + MOST)))
    return made


def permutation(target):
    width = target.shape[1]
    return (lax.broadcasted_iota(jnp.int32, (width, width), 0) == target).astype(BF16)


def cuts_of(segments):
    middle = segments.shape[1] // 2
    held = segments[:, middle : middle + 1]
    first = jnp.sum((segments < held).astype(F32), axis=1, keepdims=True)
    last = jnp.sum((segments <= held).astype(F32), axis=1, keepdims=True)
    return jnp.where(middle - first <= last - middle, first, last)


def start_body(info, hidden, cotangent, segment_ids, pad_flags, target, x_o, c_o, xhat_o, bias_o):
    core, y = info[0], info[1]
    window = x_o.shape[0]
    gap = hidden.shape[1] - window
    start = pl.multiple_of(core * gap, 16)
    segments = segment_ids[...]
    cuts = cuts_of(segments)
    cut = jnp.where(y == 0, cuts[0:1], cuts[1:2])
    here = (start + lax.broadcasted_iota(jnp.int32, (window, 1), 0)).astype(F32)
    before = (here < cut).astype(F32)
    owned = jnp.where(core == 0, before, 1.0 - before)
    perm = permutation(target[...])
    x = dot_nn(hidden[y, pl.ds(start, window), :], perm)
    x_o[...] = x.astype(BF16)
    c_o[...] = (dot_nn(cotangent[y, pl.ds(start, window), :], perm) * owned).astype(BF16)
    xhat_o[...] = norm_parts(x)[0]
    segs = jnp.where(y == 0, segments[0:1], segments[1:2]).astype(F32)
    pads = pad_flags[...]
    pads = jnp.where(y == 0, pads[0:1], pads[1:2])
    code = jnp.where(pads == 0, segs, -1.0)
    segs = jnp.where(core == 0, segs[:, :window], segs[:, gap:])
    wide = bias_o.shape[1]
    if wide > window:
        segs = jnp.concatenate([segs, jnp.full((1, wide - window), -2.0, F32)], axis=1)
    code = jnp.where(core == 0, code[:, :window], code[:, gap:])
    column = jnp.broadcast_to(code, (8, window)).T[:, 0:1]
    key = lax.broadcasted_iota(jnp.int32, (window, wide), 0)
    query = lax.broadcasted_iota(jnp.int32, (window, wide), 1)
    bias_o[...] = jnp.where((column == segs) | (key == query), 0.0, -1e30)


def assemble(blocks, places, high, weights):
    for block, rows in zip(blocks, places):
        for z, row in enumerate(rows):
            for w in range(3):
                weights[w, row : row + high] = block[z, w * high : (w + 1) * high]


def disassemble(value, outs, pick):
    value = value.astype(BF16)
    if len(outs) == 1:
        outs[0][pick] = value
        return
    _, deep, high, _ = outs[0].shape[-4:]
    half = high // 3
    yr, w = pick[:-1], pick[-1]
    for x in range(2):
        for z in range(deep):
            for c in range(2):
                at = ((z * 2 + x) * 2 + c) * half
                outs[c][yr + (x, z, pl.ds(w * half, half))] = value[at : at + half]


def common_order(rows, perm):
    high = rows.astype(BF16)
    rest = rows - high.astype(F32)
    mid = rest.astype(BF16)
    last = (rest - mid.astype(F32)).astype(BF16)
    return dot_nn(high, perm) + dot_nn(mid, perm) + dot_nn(last, perm)


def by_head(value, fill=0.0):
    tokens, columns = value.shape
    parts = value.T.reshape(columns // HD, HD, tokens)
    row = lax.broadcasted_iota(jnp.int32, (columns // HD, PAD - HD, tokens), 1)
    extra = jnp.where(row == 0, fill, 0.0)
    return jnp.concatenate([parts, extra], axis=1).astype(BF16)


def flat_heads(value):
    heads, _, tokens = value.shape
    return value[:, :HD, :].reshape(heads * HD, tokens)


def project_body(places, high, unpack, first, given, *refs):
    blocks = refs[: len(places)]
    refs = refs[len(places) :]
    if not unpack:
        small_i, shift_i = refs[:2]
        refs = refs[2:]
    qt, kt, vt, shift_o = refs[:4]
    weights = refs[-1]
    assemble(blocks, places, high, weights)
    if unpack:
        shifts = blocks[0][0, 3 * high : 3 * high + 16].astype(F32)[0:8]
    else:
        shifts = shift_i[...]
    shift_o[...] = shifts
    if first:
        small_o, n_o, nt_o = refs[4:7]
        if unpack:
            deep = blocks[0].shape[0]
            wide = blocks[0].shape[2] // 4
            rows = [
                [blocks[2 * x][z, 3 * high : 3 * high + 16].astype(F32) for x in range(2)]
                for z in range(deep)
            ]
            made = []
            for p in range(6):
                r, at = 8 + p // 4, p % 4 * wide
                made.append(
                    jnp.concatenate(
                        [rows[z][x][r : r + 1, at : at + wide] for z in range(deep) for x in range(2)],
                        axis=1,
                    )
                )
            made += [jnp.zeros_like(made[0])] * 2
            small = jnp.concatenate(made, axis=0)
        else:
            small = small_i[...]
        small_o[...] = small
        exact = given[...] * small[0:1] + small[1:2]
        normed = exact.astype(BF16)
        n_o[...] = normed
        nt_o[...] = exact.T.astype(BF16)
    else:
        normed = given[...]
    qt[...] = by_head(dot_nn(normed, weights[0]) + shifts[0:1])
    kt[...] = by_head(dot_nn(normed, weights[1]))
    vt[...] = by_head(dot_nn(normed, weights[2]) + shifts[1:2], 1.0)


def forward_body(first, qt, kt, vt, bias, ot, lse):
    heads, _, window = ot.shape
    rows = 4 * PAD

    def four(i, carry):
        h = first + 4 * i
        for q0, qn, k0, k1 in tiles(window):
            query = qt[pl.ds(h, 4), :, q0 : q0 + qn].reshape(rows, qn).astype(F32)
            if qn < 256:
                query = jnp.concatenate([query, jnp.zeros((rows, 256 - qn), F32)], axis=1)
            own = lax.broadcasted_iota(jnp.int32, (rows, 256), 0) // PAD
            block = [jnp.where(own == n, query, 0.0).astype(BF16) for n in range(4)]
            keys = kt[pl.ds(h, 4), :, k0:k1].reshape(rows, k1 - k0)
            values = vt[pl.ds(h, 4), :, k0:k1].reshape(rows, k1 - k0)
            scores = dot_tn(keys, jnp.concatenate(block, axis=1))
            tops, weights = [], []
            for n in range(4):
                part = scores[:, n * 256 : (n + 1) * 256] * LOG2 + bias[k0:k1, q0 : q0 + 256]
                top = jnp.max(part, axis=0, keepdims=True)
                tops.append(top)
                weights.append(jnp.exp2(part - top).astype(BF16))
            mixed = dot_nn(values, jnp.concatenate(weights, axis=1))
            for n in range(4):
                own_mixed = mixed[n * PAD : (n + 1) * PAD, n * 256 : n * 256 + qn]
                total = own_mixed[HD : HD + 1]
                ot[4 * i + n, :, q0 : q0 + qn] = own_mixed / total
                lse[4 * i + n, :, q0 : q0 + qn] = tops[n][:, :qn] + jnp.log2(total)
        return carry

    lax.fori_loop(0, heads // 4, four, 0)


def feed_body(places, high, x_r, o00, o01, o1, small, cols0, cols1, target, *refs):
    count = len(places)
    blocks = refs[: 2 * count]
    refs = refs[2 * count :]
    out_o, xhat_o, inv_o, n_o = refs[:4]
    atts, acts, slopes, weights = refs[4:6], refs[6:8], refs[8:10], refs[10:]
    for yr in range(2):
        assemble(blocks[yr * count : (yr + 1) * count], places, high, weights[yr])
    atts[0][...] = jnp.concatenate([flat_heads(o00[...]), flat_heads(o01[...])], axis=0).T.astype(BF16)
    atts[1][...] = flat_heads(o1[...]).T.astype(BF16)
    x = x_r[...].astype(F32)
    middle = x + dot_nt(atts[0][...], weights[0][0]) + dot_nt(atts[1][...], weights[1][0]) + small[2:3]
    xhat, inverse = norm_parts(middle)
    xhat_o[...] = xhat
    inv_o[...] = inverse
    normed = (xhat * small[3:4] + small[4:5]).astype(BF16)
    n_o[...] = normed
    result = middle + small[5:6]
    for yr, cols in enumerate((cols0, cols1)):
        pre = dot_nn(normed, weights[yr][1]) + cols[2:3]
        square = pre * pre
        bent = jnp.tanh(GELU * (pre + 0.044715 * (pre * square)))
        act = (0.5 * pre * (1.0 + bent)).astype(BF16)
        acts[yr][...] = act
        slopes[yr][...] = 0.5 * (1.0 + bent) + 0.5 * pre * (1.0 - bent * bent) * (
            GELU * (1.0 + 3.0 * 0.044715 * square)
        )
        result = result + dot_nt(act, weights[yr][2])
    out_o[...] = dot_nn(result.astype(BF16), permutation(target[...])).astype(BF16)


def rows_of(info, feats, units):
    width = feats.shape[1]
    cols = width // 2
    made = []
    for i in range(feats.shape[0]):
        made += [feats[i : i + 1, :cols], feats[i : i + 1, cols:]]
    for own, other in units:
        made += [jnp.where(info[1] == 0, own, other), jnp.where(info[1] == 0, other, own)]
    return jnp.concatenate(made, axis=0)


def feed_back_body(places, high, parts, info, c_r, xhat_r, inv_r, n_r, a0, a1, act0, act1, slope0, slope1, small, target, *refs):
    count = len(places)
    blocks = refs[: 2 * count]
    refs = refs[2 * count :]
    mid_o, d0, d1, sum_o = refs[:4]
    outs = refs[4 : 4 + parts]
    weights = refs[4 + parts :]
    for yr in range(2):
        assemble(blocks[yr * count : (yr + 1) * count], places, high, weights[yr])
    ct_low, normed = c_r[...], n_r[...]
    cols = act0.shape[1]

    def both(left, right, w):
        grads = dot_tn(left, jnp.concatenate(right, axis=1))
        for yr in range(2):
            disassemble(grads[:, yr * cols : (yr + 1) * cols], outs, (yr, w))

    both(ct_low, [act0[...], act1[...]], 2)
    dpres = [
        (dot_nn(ct_low, weights[yr][2]) * slope[...]).astype(BF16) for yr, slope in enumerate((slope0, slope1))
    ]
    both(normed, dpres, 1)
    ups = [jnp.sum(dpre.astype(F32), axis=0, keepdims=True) for dpre in dpres]
    dnorm = dot_nt(dpres[0], weights[0][1]) + dot_nt(dpres[1], weights[1][1])
    ct, xhat = ct_low.astype(F32), xhat_r[...]
    dmiddle = ct + norm_back(dnorm, xhat, inv_r[...], small[3:4])
    mid_o[...] = dmiddle
    sums = [jnp.sum(part, axis=0, keepdims=True) for part in (dmiddle, dnorm * xhat, dnorm, ct)]
    sums = common_order(
        jnp.concatenate(sums + [jnp.zeros((4, dnorm.shape[1]), F32)], axis=0), permutation(target[...])
    )
    sums = rows_of(info, sums[0:4], [ups])
    sum_o[...] = jnp.concatenate([sums, jnp.zeros_like(sums[0:6])], axis=0)
    low = dmiddle.astype(BF16)
    both(low, [a0[...], a1[...]], 0)
    for yr in range(2):
        (d0, d1)[yr][...] = by_head(dot_nn(low, weights[yr][0]))


def backward_body(first, mixed, qt, kt, vt, dt, ot, lse, bias, dq_o, dk_o, dv_o, dq, dk, dv):
    heads, _, window = dq.shape
    made = tiles(window)

    def head(i, carry):
        h = first + i
        delta = jnp.sum(dt[h].astype(F32) * ot[mixed + i], axis=0, keepdims=True)
        for ref in (dk, dv):
            ref[i] = jnp.zeros_like(ref[i])
        for q0, qn, k0, k1 in made:
            query, grad = qt[h, :, q0 : q0 + qn], dt[h, :, q0 : q0 + qn]
            scores = dot_tn(kt[h, :, k0:k1], query)
            dprobs = dot_tn(vt[h, :, k0:k1], grad)
            probs = jnp.exp2(scores * LOG2 + (bias[k0:k1, q0 : q0 + qn] - lse[mixed + i, :, q0 : q0 + qn]))
            dscores = (probs * (dprobs - delta[:, q0 : q0 + qn])).astype(BF16)
            dq[i, :, q0 : q0 + qn] = dot_nn(kt[h, :, k0:k1], dscores)
            dk[i, :, k0:k1] += dot_nt(query, dscores)
            dv[i, :, k0:k1] += dot_nt(grad, probs.astype(BF16))
        return carry

    lax.fori_loop(0, heads, head, 0, unroll=2)
    for ref, out, factor in ((dq, dq_o, SCALE), (dk, dk_o, SCALE), (dv, dv_o, 1.0)):
        out[...] = (flat_heads(ref[...]) * factor).astype(BF16)


def weigh_body(places, high, parts, nt_r, qa, ka, va, qb, kb, vb, *refs):
    blocks = refs[: len(places)]
    refs = refs[len(places) :]
    dn, sums = refs[:2]
    outs = refs[2 : 2 + parts]
    weights = refs[2 + parts]
    assemble(blocks, places, high, weights)
    normed = nt_r[...]
    ones = jnp.ones((8, normed.shape[1]), BF16)
    total = None
    for w, (a, b) in enumerate(((qa, qb), (ka, kb), (va, vb))):
        low = jnp.concatenate([a[...], b[...]], axis=0)
        disassemble(dot_nt(normed, low), outs, (w,))
        part = dot_nn(weights[w], low)
        total = part if total is None else total + part
        if w != 1:
            sums[w // 2 : w // 2 + 1] = dot_nt(ones, low)[0:1]
    dn[...] = total


def finish_body(info, dn0, dn1, x_r, mid, small, target, qv0, qv1, out_o, sum_o):
    perm = permutation(target[...])
    grad = (dn0[...] + dn1[...]).T
    xhat, inverse = norm_parts(x_r[...].astype(F32))
    dx = mid[...] + norm_back(grad, xhat, inverse, small[0:1])
    out_o[...] = dot_nn(dx.astype(BF16), perm).astype(BF16)
    sums = [jnp.sum(part, axis=0, keepdims=True) for part in (grad * xhat, grad)]
    sums = common_order(jnp.concatenate(sums + [jnp.zeros((6, grad.shape[1]), F32)], axis=0), perm)
    sum_o[...] = rows_of(info, sums[0:2], [(qv0[w : w + 1], qv1[w : w + 1]) for w in range(2)])


def deal_body(info, wo, wu, wd, mine, theirs):
    half = mine.shape[1]
    values = [wo[...].astype(F32).T.astype(BF16), wu[...], wd[...].astype(F32).T.astype(BF16)]

    @pl.when(info[0] == 0)
    def _():
        for w, value in enumerate(values):
            mine[w], theirs[w] = value[:half], value[half:]

    @pl.when(info[0] != 0)
    def _():
        for w, value in enumerate(values):
            theirs[w], mine[w] = value[:half], value[half:]


def meet_a_body(info, mine, got, small, units, units_pair, first):
    half = got.shape[1]
    wr, wc = small.shape[1], units.shape[1]
    zeros = jnp.zeros((8, 4 * wr), F32)

    def meet(own_first):
        def pair(own, other):
            return jnp.concatenate([own, other] if own_first else [other, own], axis=1)

        for w in range(3):
            first[0, w * half : (w + 1) * half, :] = pair(mine[w], got[w])
        params = small[...].astype(F32)
        if not own_first:
            params = jnp.concatenate([params[:, half:], params[:, :half]], axis=1)
        above = jnp.concatenate([params[p : p + 1] for p in range(4)], axis=1)
        below = jnp.concatenate([params[4:5], params[5:6], zeros[0:1, : 2 * wr]], axis=1)
        both = pair(units[...], units_pair[...]).astype(F32)
        extra = jnp.concatenate([both, zeros[:5], above, below, zeros[:6]], axis=0)
        first[0, 3 * half : 3 * half + 16, :] = extra.astype(BF16)

    @pl.when(info[0] == 0)
    def _():
        meet(True)

    @pl.when(info[0] != 0)
    def _():
        meet(False)


def meet_b_body(info, mine, got, second):
    half = got.shape[1]

    def meet(low, high):
        for w in range(3):
            second[0, w * half : (w + 1) * half, :] = jnp.concatenate([low[w], high[w]], axis=1)

    @pl.when(info[0] == 0)
    def _():
        meet(mine, got)

    @pl.when(info[0] != 0)
    def _():
        meet(got, mine)


def stack_body(*refs):
    out = refs[-1]
    for at, ref in enumerate(refs[:-1]):
        out[at] = ref[0]


def pack(out, row, sums):
    count = sums.shape[0]
    high = sums.astype(BF16)
    out[row : row + count] = high
    out[row + count : row + 2 * count] = (sums - high.astype(F32)).astype(BF16)


def unpack_sums(ref, row, count):
    both = ref[row : row + 2 * count].astype(F32)
    return both[:count] + both[count:]


def block_sums(keep, got, out, row):
    deep, high, _ = keep.shape
    for z in range(deep):
        total = keep[z].astype(F32) + got[z].astype(F32)
        out[row + z * high : row + (z + 1) * high] = total.astype(BF16)


def far_b_body(keep, got, sums, sums_got, out, sum_o):
    total = sums[...] + sums_got[...]
    sum_o[...] = total
    for x in range(2):
        block_sums(keep.at[1, x], got.at[1, x], out, x * (out.shape[0] - 32) // 2)
    pack(out, out.shape[0] - 32, total)


def far_a_body(keep, got, out0, out1):
    block_sums(keep.at[0], got.at[0], out0, 0)
    block_sums(keep.at[1], got.at[1], out1, 0)


def pass_on(keep, got, far, out):
    deep, high, _ = keep.shape
    for z in range(deep):
        rows = slice(z * high, (z + 1) * high)
        total = keep[z].astype(F32) + got[z].astype(F32) + far[rows].astype(F32)
        out[rows] = total.astype(BF16)


def near_b_body(keep, got, far, sums, out, sum_o):
    count = out.shape[0] - 32
    pass_on(keep.at[0, 1], got.at[0, 1], far.at[count : 2 * count], out)
    total = sums[...] + unpack_sums(far, 2 * count, 16)
    sum_o[...] = total
    pack(out, count, total)


def near_a_body(keep, got, far, sums, sums_got, out, sum_o):
    pass_on(keep.at[1], got.at[1], far, out)
    total = sums[...] + sums_got[...]
    sum_o[...] = total
    pack(out, out.shape[0] - 16, total)


def block_total(keep, got, far, passed, z):
    rows = slice(z * keep.shape[1], (z + 1) * keep.shape[1])
    return keep[z].astype(F32) + got[z].astype(F32) + far[rows].astype(F32) + passed[rows].astype(F32)


def high_b_body(keep, got, far, passed, sums, own, out, sum_o):
    kept, given = keep.at[0, 0], got.at[0, 0]
    deep, high, _ = kept.shape
    total = sums[...] + unpack_sums(passed, deep * high, sums.shape[0])
    sum_o[...] = total
    for z in range(deep):
        value = block_total(kept, given, far, passed, z)
        if z < deep // 2:
            own[z] = value
        else:
            out[(z - deep // 2) * high : (z - deep // 2 + 1) * high] = value.astype(BF16)
    pack(out, deep // 2 * high, total)


def middle_b_body(own, got, sums, own_o, out, sum_o):
    _, high, _ = own.shape
    total = sums[...] + unpack_sums(got, 2 * high, sums.shape[0])
    sum_o[...] = total
    own_o[...] = own[0] + got[0:high].astype(F32)
    out[0:high] = (own[1] + got[high : 2 * high].astype(F32)).astype(BF16)
    pack(out, high, total)


def high_a_body(keep, got, far, passed, sums, *outs):
    kept, given = keep.at[0], got.at[0]
    deep, high, _ = kept.shape
    total = sums[...] + unpack_sums(passed, deep * high, sums.shape[0])
    outs[-1][...] = total
    for z in range(deep):
        value = block_total(kept, given, far, passed, z)
        if z == 0:
            outs[0][...] = value
        else:
            outs[z][0:high] = value.astype(BF16)
            pack(outs[z], high, total)


def last_body(info, own, sums, *refs):
    parts, (mine, theirs, sum_o) = refs[:-3], refs[-3:]
    high = own.shape[0]
    half = high // 3
    total, wide = own[...], sums[...]
    for part in parts:
        total = total + part[0:high].astype(F32)
        wide = wide + unpack_sums(part, high, sums.shape[0])
    sum_o[...] = wide
    wc = mine.shape[2]

    def give(low, upper):
        for w in range(3):
            low[w] = total[w * half : (w + 1) * half, :wc]
            upper[w] = total[w * half : (w + 1) * half, wc:]

    @pl.when(info[0] == 0)
    def _():
        give(mine, theirs)

    @pl.when(info[0] != 0)
    def _():
        give(theirs, mine)


def deliver_body(turned, info, mine, got, *outs):
    half = mine.shape[1]

    def deliver(low, high):
        for w, out in enumerate(outs):
            if turned[w]:
                out[...] = jnp.concatenate([low[w], high[w]], axis=0).T
            else:
                out[0:half] = low[w]
                out[half:] = high[w]

    @pl.when(info[0] == 0)
    def _():
        deliver(mine, got)

    @pl.when(info[0] != 0)
    def _():
        deliver(got, mine)


def join_body(info, segment_ids, own, beside, across, corner, out):
    core, y = info[0], info[1]
    length, window = out.shape[1], own.shape[0]
    gap = length - window
    cuts = cuts_of(segment_ids[...])
    own_cut = jnp.where(y == 0, cuts[0:1], cuts[1:2])
    other_cut = jnp.where(y == 0, cuts[1:2], cuts[0:1])

    def row(low, high, place, cut):
        out[place, 0:gap] = low[0:gap]
        at = (gap + lax.broadcasted_iota(jnp.int32, (window - gap, 1), 0)).astype(F32)
        seam = jnp.where(at < cut, low[gap:window].astype(F32), high[0 : window - gap].astype(F32))
        out[place, gap:window] = seam.astype(BF16)
        out[place, window:length] = high[window - gap : window]

    @pl.when(core == 0)
    def _():
        row(own, beside, y, own_cut)
        row(across, corner, 1 - y, other_cut)

    @pl.when(core != 0)
    def _():
        row(beside, own, y, own_cut)
        row(corner, across, 1 - y, other_cut)


def per_device(
    hidden_in,
    segment_ids,
    pad_flags,
    gain1,
    shift1,
    w_query,
    b_query,
    w_key,
    w_value,
    b_value,
    w_out,
    b_out,
    gain2,
    shift2,
    w_up,
    b_up,
    w_down,
    b_down,
    cotangent,
):
    fs, mp = lax.axis_size("fsdp"), lax.axis_size("mp")
    rows, length, width = hidden_in.shape
    wr, wc = w_query.shape
    half, cols = wr // 2, 2 * wc
    heads = cols // HD
    f, m = lax.axis_index("fsdp"), lax.axis_index("mp")
    core, y = m % 2, m // 2
    side = jnp.stack([core, y])
    window = length // 2 + MOST // 2
    deep = fs // 2
    flips = [2 * z for z in range(1, deep)]
    staged = half % 16 == 0 and deep == 4
    if staged:
        places = [[((z * 2 + x) * 2 + c) * half for z in range(deep)] for x in range(2) for c in range(2)]
        high, parts = half, 2
    else:
        places, high, parts = [[0]], width, 1
    wide, tall = (window, width), (width, window)
    by_heads, by_few = (heads, PAD, window), (heads // 2, PAD, window)
    weights = pltpu.VMEM((3, width, cols), BF16)

    def to(value, flip_f, flip_m):
        return send(value, fs, mp, flip_f, flip_m)

    def begin(target):
        return call(
            start_body,
            [(wide, BF16), (wide, BF16), (wide, F32), ((window, -(-window // 256) * 256), F32)],
            [side, hidden_in, cotangent, segment_ids, pad_flags, target],
            (),
            1,
            us=3,
            mib=4,
        )

    def project(given, blocks, first, extra=()):
        outs = [(by_heads, BF16)] * 3 + [((8, cols), F32)]
        if first:
            outs += [((8, width), F32), (wide, BF16), (tall, BF16)]
        return call(
            functools.partial(project_body, places, high, not extra, first),
            outs,
            [given] + blocks + list(extra),
            [weights],
            us=2,
            mib=4,
        )

    def attend(part, qkv_heads, bias):
        first, count = (0, heads) if part is None else (part * (heads // 2), heads // 2)
        return call(
            functools.partial(forward_body, first),
            [((count, PAD, window), F32), ((count, 1, window), F32)],
            list(qkv_heads) + [bias],
            us=5,
        )

    def feed(x, mixed, small, shifts, target, blocks):
        units_shape = (window, cols)
        return call(
            functools.partial(feed_body, places, high),
            [(wide, BF16), (wide, F32), ((window, 1), F32), (wide, BF16)]
            + [(units_shape, BF16)] * 4
            + [(units_shape, F32)] * 2,
            [x] + mixed + [small] + shifts + [target] + blocks,
            [weights, weights],
            us=5,
            mib=7,
        )

    def feed_back(side, ct, made, small, target, blocks):
        if staged:
            grads = [((2, 2, deep, 3 * half, cols), BF16)] * 2
        else:
            grads = [((2, 3, width, cols), BF16)]
        return call(
            functools.partial(feed_back_body, places, high, parts),
            [(wide, F32), (by_heads, BF16), (by_heads, BF16), ((16, cols), F32)] + grads,
            [side, ct] + list(made) + [small, target] + blocks,
            [weights, weights],
            1,
            us=7,
            mib=10,
        )

    def backward(part, qkv_heads, da, o, lse, bias):
        return call(
            functools.partial(backward_body, part * (heads // 2), part * (heads // 2) if o.shape[0] == heads else 0),
            [((heads // 2 * HD, window), BF16)] * 3,
            list(qkv_heads) + [da, o, lse, bias],
            [pltpu.VMEM(by_few, F32)] * 3,
            us=15,
        )

    def weigh(normed_t, blocks, low_a, low_b):
        if staged:
            grads = [((2, deep, 3 * half, cols), BF16)] * 2
        else:
            grads = [((3, width, cols), BF16)]
        return call(
            functools.partial(weigh_body, places, high, parts),
            [(tall, F32), ((2, cols), F32)] + grads,
            [normed_t] + list(low_a) + list(low_b) + blocks,
            [weights],
            us=0.1,
        )

    def finish(side, dn0, dn1, x, dmiddle, small, target, qv0, qv1):
        return call(
            finish_body,
            [(wide, BF16), ((8, cols), F32)],
            [side, dn0, dn1, x, dmiddle, small, target, qv0, qv1],
            (),
            1,
            us=20,
            mib=5,
        )

    def join(own, beside, across, corner):
        operands = [side, segment_ids, own, beside, across, corner]
        return call(join_body, [((rows, length, width), BF16)], operands, (), 1, us=20)[0]

    if not staged:

        def gathered(blocks):
            full = []
            for block in blocks:
                block = lax.all_gather(block, "fsdp", axis=0, tiled=True)
                full.append(lax.all_gather(block, "mp", axis=1, tiled=True))
            full = jnp.stack(full)
            return [full[:, :, yr * cols : (yr + 1) * cols].reshape(1, 3 * width, cols) for yr in range(2)]

        target = lax.iota(jnp.int32, width)[None]
        wa = gathered([w_query, w_key, w_value])
        wb = gathered([w_out.T, w_up, w_down.T])
        small = jnp.stack([gain1, shift1, b_out, gain2, shift2, b_down] + [jnp.zeros_like(gain1)] * 2)
        small = lax.all_gather(small, "fsdp", axis=1, tiled=True).astype(F32)
        units = jnp.stack([b_query, b_value, b_up] + [jnp.zeros_like(b_up)] * 5)
        units = lax.all_gather(units, "mp", axis=1, tiled=True).astype(F32)
        units = [units[:, :cols], units[:, cols:]]
        x, ct, xhat, bias = begin(target)
        *heads0, _, _, normed, normed_t = project(xhat, [wa[0]], True, (small, units[0]))
        *heads1, _ = project(normed, [wa[1]], False, (small, units[1]))
        both = (heads0, heads1)
        mixed = [attend(0, heads0, bias), attend(1, heads0, bias)] + [attend(None, heads1, bias)] * 2
        made = feed(x, [o for o, _ in mixed[:3]], small, units, target, wb)
        result = made[0]
        none = jnp.zeros_like(side)
        dmiddle, da0, da1, sums_b, grads_b = feed_back(none, ct, made[1:], small, target, wb)
        dn, qv, grads_a = [], [], []
        for yr, da in enumerate((da0, da1)):
            lows = [backward(part, both[yr], da, *mixed[2 * yr + part], bias) for part in range(2)]
            got = weigh(normed_t, [wa[yr]], *lows)
            dn.append(got[0])
            qv.append(got[1])
            grads_a.append(got[2])
        grad_window, sums_a = finish(none, dn[0], dn[1], x, dmiddle, small, target, *qv)

        def scattered(pair):
            full = jnp.concatenate(pair, axis=2).astype(F32)
            full = lax.psum_scatter(full, "mp", scatter_dimension=2, tiled=True)
            return lax.psum_scatter(full, "fsdp", scatter_dimension=1, tiled=True)

        grad_q, grad_k, grad_v = scattered(grads_a)
        grad_out, grad_up, grad_down = scattered([grads_b[0], grads_b[1]])
        grad_out, grad_down = grad_out.T, grad_down.T
        sums_a, sums_b = sums_a.reshape(4, width), sums_b.reshape(8, width)
        sums = jnp.concatenate([sums_a[0:2], sums_b[0:4], sums_a[2:4], sums_b[4:5]])
        sums = lax.psum(sums, BOTH)
        mine_f = lax.dynamic_slice(sums, (0, f * wr), (6, wr))
        mine_u = lax.dynamic_slice(sums, (6, m * wc), (3, wc))

        def shared(value):
            across = to(value, 0, 2)
            return join(value, to(value, 0, 1), across, to(across, 0, 1))

        out_hidden, grad_hidden = shared(result), shared(grad_window)
    else:
        piece_a, piece_b = (1, 3 * half + 16, cols), (1, 3 * half, cols)

        def stacked(pieces):
            return call(stack_body, [((deep,) + pieces[0].shape[1:], BF16)], pieces)[0]

        def part(block, of):
            return lax.dynamic_slice(block, (of * half, 0), (half, wc))

        theirs = jnp.stack([part(w, 1 - core) for w in (w_query, w_key, w_value)])
        got = to(theirs, 0, 1)
        theirs, gain1, b_query, w_query, w_key, w_value = fence(theirs, gain1, b_query, w_query, w_key, w_value)
        mine = jnp.stack([part(w, core) for w in (w_query, w_key, w_value)])
        small = jnp.stack([gain1, shift1, b_out, gain2, shift2, b_down])
        units = jnp.concatenate([b_query, b_value, b_up]).reshape(3, wc)
        units_pair = to(units, 0, 1)
        feature = lax.iota(jnp.int32, width)
        target = (((feature // half) ^ (f * 2 + core)) * half + feature % half)[None]
        got, units_pair, small, mine = fence(got, units_pair, small, mine)

        first = call(
            meet_a_body, [(piece_a, BF16)], [side, mine, got, small, units, units_pair], (), 1
        )[0]
        first_parts = [to(first, flip, 0) for flip in flips]
        first, w_out, w_up, w_down = fence(first, w_out, w_up, w_down)
        mine, theirs = call(deal_body, [((3, half, wc), BF16)] * 2, [side, w_out, w_up, w_down], (), 1)
        got = to(theirs, 0, 1)
        second = call(meet_b_body, [(piece_b, BF16)], [side, mine, got], (), 1)[0]
        first, first_parts, second, hidden_in, target = fence(first, first_parts, second, hidden_in, target)

        qkv = stacked([first] + first_parts)
        qkv_x, qkv_y = to(qkv, 1, 0), to(qkv, 0, 2)
        second_parts = [to(second, flip, 0) for flip in flips]
        x, ct, xhat, bias = begin(target)
        second_parts, second, qkv, qkv_x, qkv_y, xhat = fence(second_parts, second, qkv, qkv_x, qkv_y, xhat)
        qkv_xy = to(qkv, 1, 2)

        qkv_c, qkv_xc = to(qkv, 0, 1), to(qkv_x, 0, 1)
        odu = stacked([second] + second_parts)
        near = [qkv, qkv_c, qkv_x, qkv_xc]
        *heads0, shift0, small, normed, normed_t = project(xhat, near, True)
        heads0, qkv_y, odu = fence(heads0, qkv_y, odu)
        qkv_yc, odu_x, odu_y, odu_xy = to(qkv_y, 0, 1), to(odu, 1, 0), to(odu, 0, 2), to(odu, 1, 2)
        o00, l00 = attend(0, heads0, bias)
        o00, heads0, qkv_yc, qkv_xy, odu = fence(o00, heads0, qkv_yc, qkv_xy, odu)
        qkv_xyc, odu_c = to(qkv_xy, 0, 1), to(odu, 0, 1)
        o01, l01 = attend(1, heads0, bias)
        o01, qkv_xyc, odu_c, normed = fence(o01, qkv_xyc, odu_c, normed)
        far = [qkv_y, qkv_yc, qkv_xy, qkv_xyc]
        *heads1, shift1u = project(normed, far, False)
        o1, l1 = attend(None, heads1, bias)
        o1, odu_x, odu_y = fence(o1, odu_x, odu_y)
        odu_xc, odu_yc = to(odu_x, 0, 1), to(odu_y, 0, 1)
        o1, odu_xc, odu_yc, odu_xy = fence(o1, odu_xc, odu_yc, odu_xy)
        odu_xyc = to(odu_xy, 0, 1)

        odu_blocks = [odu, odu_c, odu_x, odu_xc, odu_y, odu_yc, odu_xy, odu_xyc]
        made = fence(*feed(x, [o00, o01, o1], small, [shift0, shift1u], target, odu_blocks))
        result = made[0]
        res_c, res_y = to(result, 0, 1), to(result, 0, 2)
        made = feed_back(side, ct, made[1:], small, target, odu_blocks)
        dmiddle, da0, da1, b_sums, b_keep, b_send, res_c = fence(*made, res_c)

        n_far, n_near = 2 * deep * 3 * half, deep * 3 * half
        f32_16, f32_8 = ((16, cols), F32), ((8, cols), F32)
        b_got, b_sums_got = to(b_send, 0, 1), to(b_sums, 0, 1)
        low10 = backward(0, heads1, da1, o1, l1, bias)
        low10, heads1, b_got, b_sums_got = fence(low10, heads1, b_got, b_sums_got)
        b_far, b_sums = call(
            far_b_body,
            [((n_far + 32, cols), BF16), f32_16],
            [b_keep, b_got, b_sums, b_sums_got],
        )
        b_far = to(b_far, 0, 2)
        low11 = backward(1, heads1, da1, o1, l1, bias)
        low11, normed_t = fence(low11, normed_t)
        dn1, qv1, keep1, send1 = weigh(normed_t, far, low10, low11)
        dn1, keep1, send1, da0, res_y = fence(dn1, keep1, send1, da0, res_y)
        got1, res_yc = to(send1, 0, 1), to(res_y, 0, 1)
        low00 = backward(0, heads0, da0, o00, l00, bias)
        low00, heads0, got1, res_yc = fence(low00, heads0, got1, res_yc)
        a_far0, a_far1 = call(far_a_body, [((n_near, cols), BF16)] * 2, [keep1, got1])
        a_far0, a_far1, heads0 = fence(a_far0, a_far1, heads0)
        a_far1, a_far0 = to(a_far1, 0, 2), to(a_far0, 0, 2)
        low01 = backward(1, heads0, da0, o01, l01, bias)
        low01, normed_t, b_far = fence(low01, normed_t, b_far)
        b_x, b_sums = call(
            near_b_body, [((n_near + 32, cols), BF16), f32_16], [b_keep, b_got, b_far, b_sums]
        )
        b_x = to(b_x, 1, 0)
        dn0, qv0, keep0, send0 = weigh(normed_t, near, low00, low01)
        dn0, keep0, send0, dmiddle = fence(dn0, keep0, send0, dmiddle)
        got0 = to(send0, 0, 1)
        n_two = 2 * 3 * half
        grad_window, a_sums = finish(side, dn0, dn1, x, dmiddle, small, target, qv0, qv1)
        grad_window, a_sums, got0, a_far1, b_x = fence(grad_window, a_sums, got0, a_far1, b_x)

        gw_y, gw_c, a_sums_got = to(grad_window, 0, 2), to(grad_window, 0, 1), to(a_sums, 0, 1)
        b_own, b_z2, b_sums = call(
            high_b_body,
            [((2, 3 * half, cols), F32), ((n_two + 32, cols), BF16), f32_16],
            [b_keep, b_got, b_far, b_x, b_sums],
        )
        b_z2, result = fence(b_z2, result)
        b_z2 = to(b_z2, 4, 0)
        out_hidden = join(result, res_c, res_y, res_yc)
        a_sums_got, gw_c, keep0, out_hidden = fence(a_sums_got, gw_c, keep0, out_hidden)
        a_x, a_sums = call(
            near_a_body, [((n_near + 16, cols), BF16), f32_8], [keep0, got0, a_far1, a_sums, a_sums_got]
        )
        a_x = to(a_x, 1, 0)

        def last(own, sums, got, kind):
            return call(last_body, [((3, half, wc), F32)] * 2 + [kind], [side, own, sums] + got, (), 1, us=20)

        def deliver(mine, got, turned):
            shapes = [((wc, wr) if t else (wr, wc), F32) for t in turned]
            return call(functools.partial(deliver_body, turned), shapes, [side, mine, got], (), 1)

        b_own, b_z1, b_sums = call(
            middle_b_body,
            [((3 * half, cols), F32), ((3 * half + 32, cols), BF16), f32_16],
            [b_own, b_z2, b_sums],
            us=20,
        )
        b_z1, a_x, a_far0, keep0 = fence(b_z1, a_x, a_far0, keep0)
        a_split = call(
            high_a_body,
            [((3 * half, cols), F32)] + [((3 * half + 16, cols), BF16)] * (deep - 1) + [f32_8],
            [keep0, got0, a_far0, a_x, a_sums],
        )
        a_split, b_z1, b_own = fence(a_split, b_z1, b_own)
        a_high = [to(part, flip, 0) for part, flip in zip(a_split[1:-1], flips)]
        b_z1 = to(b_z1, 2, 0)
        b_z1, gw_y = fence(b_z1, gw_y)
        b_mine, b_theirs, b_sums = last(b_own, b_sums, [b_z1], f32_16)
        b_last, gw_yc = to(b_theirs, 0, 1), to(gw_y, 0, 1)
        grad_hidden = join(grad_window, gw_c, gw_y, gw_yc)
        b_last, grad_hidden = fence(b_last, grad_hidden)
        grad_out, grad_up, grad_down = deliver(b_mine, b_last, (True, False, True))
        a_own, a_high, grad_out, grad_hidden = fence(a_split[0], a_high, grad_out, grad_hidden)
        a_mine, a_theirs, a_sums = last(a_own, a_split[-1], a_high, f32_8)
        a_last = to(a_theirs, 0, 1)
        a_sums = a_sums + to(a_sums, 0, 2)
        grad_q, grad_k, grad_v = deliver(a_mine, a_last, (False, False, False))
        sums = jnp.concatenate(
            [
                a_sums.reshape(4, width)[0:2],
                b_sums.reshape(8, width)[0:4],
                a_sums.reshape(4, width)[2:4],
                b_sums.reshape(8, width)[4:5],
            ]
        )
        mine_f = lax.dynamic_slice(sums, (0, f * wr), (6, wr))
        mine_u = lax.dynamic_slice(sums, (6, m * wc), (3, wc))
    return (
        out_hidden,
        grad_hidden,
        mine_f[0],
        mine_f[1],
        grad_q,
        mine_u[0],
        grad_k,
        grad_v,
        mine_u[1],
        grad_out,
        mine_f[2],
        mine_f[3],
        mine_f[4],
        grad_up,
        mine_u[2],
        grad_down,
        mine_f[5],
    )


def solution(mesh):
    return jax.shard_map(
        per_device,
        mesh=mesh,
        in_specs=(
            P("fsdp", None, None),
            P("fsdp", None),
            P("fsdp", None),
            P("fsdp"),
            P("fsdp"),
            P("fsdp", "mp"),
            P("mp"),
            P("fsdp", "mp"),
            P("fsdp", "mp"),
            P("mp"),
            P("mp", "fsdp"),
            P("fsdp"),
            P("fsdp"),
            P("fsdp"),
            P("fsdp", "mp"),
            P("mp"),
            P("mp", "fsdp"),
            P("fsdp"),
            P("fsdp", None, None),
        ),
        out_specs=(
            P("fsdp", None, None),
            P("fsdp", None, None),
            P("fsdp"),
            P("fsdp"),
            P("fsdp", "mp"),
            P("mp"),
            P("fsdp", "mp"),
            P("fsdp", "mp"),
            P("mp"),
            P("mp", "fsdp"),
            P("fsdp"),
            P("fsdp"),
            P("fsdp"),
            P("fsdp", "mp"),
            P("mp"),
            P("mp", "fsdp"),
            P("fsdp"),
        ),
        check_vma=False,
    )
```
